32 devices in a mesh: fsdp: 16 (over z, y, x), rep: 2 (over core).
Axes of the slice: x: 2, y: 2, z: 4, core: 2. Of those that a mesh axis runs over, the one named last changes fastest.
Arguments:
- tokens: bfloat16 [32, 1024, 768], P(('fsdp', 'rep')), may hold values from -6 to 6
- context: bfloat16 [32, 1024, 768], P(('fsdp', 'rep')), may hold values from -6 to 6
- clip_lengths: int32 [32], P(('fsdp', 'rep')), may hold values from 512 to 1024, as said below
- context_frames: int32 [32], P(('fsdp', 'rep')), may hold values from 1 to 4, as said below
- norm1_gain: bfloat16 [768], P('fsdp'), may hold values from 0.099609375 to 1.8984375
- norm1_bias: bfloat16 [768], P('fsdp'), may hold values from -1.5 to 1.5
- cross_q: bfloat16 [768, 768], P('fsdp'), may hold values from -0.21875 to 0.21875
- cross_k: bfloat16 [768, 768], P('fsdp'), may hold values from -0.21875 to 0.21875
- cross_v: bfloat16 [768, 768], P('fsdp'), may hold values from -0.21875 to 0.21875
- cross_out: bfloat16 [768, 768], P('fsdp'), may hold values from -4 to 4
- norm2_gain: bfloat16 [768], P('fsdp'), may hold values from 0.099609375 to 1.8984375
- norm2_bias: bfloat16 [768], P('fsdp'), may hold values from -1.5 to 1.5
- attn_qkv: bfloat16 [768, 2304], P('fsdp'), may hold values from -0.21875 to 0.21875
- attn_out: bfloat16 [768, 768], P('fsdp'), may hold values from -1.5 to 1.5
- norm3_gain: bfloat16 [768], P('fsdp'), may hold values from 0.099609375 to 1.8984375
- norm3_bias: bfloat16 [768], P('fsdp'), may hold values from -1.5 to 1.5
- mlp_up: bfloat16 [768, 3072], P('fsdp'), may hold values from -0.21875 to 0.21875
- mlp_down: bfloat16 [3072, 768], P('fsdp'), may hold values from -0.109375 to 0.109375
- cotangent: bfloat16 [32, 1024, 768], P(('fsdp', 'rep')), may hold values from -6 to 6
Outputs:
- block_out: bfloat16 [32, 1024, 768], P(('fsdp', 'rep'))
- input_grad: float32 [32, 1024, 768], P(('fsdp', 'rep'))
- grad_norm1_gain: float32 [768], P('fsdp')
- grad_norm1_bias: float32 [768], P('fsdp')
- grad_cross_q: float32 [768, 768], P('fsdp')
- grad_cross_k: float32 [768, 768], P('fsdp')
- grad_cross_v: float32 [768, 768], P('fsdp')
- grad_cross_out: float32 [768, 768], P('fsdp')
- grad_norm2_gain: float32 [768], P('fsdp')
- grad_norm2_bias: float32 [768], P('fsdp')
- grad_attn_qkv: float32 [768, 2304], P('fsdp')
- grad_attn_out: float32 [768, 768], P('fsdp')
- grad_norm3_gain: float32 [768], P('fsdp')
- grad_norm3_bias: float32 [768], P('fsdp')
- grad_mlp_up: float32 [768, 3072], P('fsdp')
- grad_mlp_down: float32 [3072, 768], P('fsdp')
The draws below stay inside these ranges and needn't reach their ends.
Inputs may be any that keep to these rules, and one draw needn't show every extreme that they name: A clip's valid tokens fill its first clip_lengths slots; at least one clip has all 1024 slots valid. `context_frames`: A clip's valid context frames, of 256 tokens each, fill its first context slots; some clip has 4 valid frames and some clip has one.
All inputs are finite; a program needn't handle non-finite values.
Results may differ from the reference program's by a relative error of at most 0.019.
Values may be sent and summed in bfloat16 or wider, within the bound.
A program may use at most 384 MiB of HBM per device.

```python
import jax
import jax.numpy as jnp
from jax import lax

D = 768
FF = 3072
HEAD = 64
HEADS = 12
SLOT = 1024
FRAME_TOK = 256
FRAMES = 4
CTXS = 1024
CLIPS = 32


def draw_clip_lengths(key, part):
    first_key, second_key = jax.random.split(key)
    drawn = jax.random.randint(first_key, (CLIPS,), SLOT // 2, SLOT + 1)
    chosen = jax.random.randint(second_key, (), 0, CLIPS)
    return jnp.where(jnp.arange(CLIPS) == chosen, SLOT, drawn).astype(jnp.int32)


def draw_context_frames(key, part):
    first_key, second_key, third_key = jax.random.split(key, 3)
    drawn = jax.random.randint(first_key, (CLIPS,), 1, FRAMES + 1)
    fullest = jax.random.randint(second_key, (), 0, CLIPS)
    emptiest = (fullest + 1 + jax.random.randint(third_key, (), 0, CLIPS - 1)) % CLIPS
    drawn = jnp.where(jnp.arange(CLIPS) == fullest, FRAMES, drawn)
    drawn = jnp.where(jnp.arange(CLIPS) == emptiest, 1, drawn)
    return drawn.astype(jnp.int32)


def block_scale(stream_key, shape, pieces, least, high):
    def one(dim, shards_of):
        steps = jax.random.uniform(jax.random.fold_in(jax.random.fold_in(stream_key, 6), dim), (shards_of,), jnp.float32, least / len(pieces), high / len(pieces))
        return jnp.repeat(jnp.exp(steps), shape[dim] // shards_of).reshape((-1,) + (1,) * (len(shape) - dim - 1))

    level = one(*pieces[0])
    for cut in pieces[1:]:
        level = level * one(*cut)
    return level


def noise(stream_key, shape, scale, reach, cuts=(), kind=jnp.bfloat16):
    entries = scale * jax.random.normal(stream_key, shape, jnp.float32)
    if cuts:
        entries = entries * block_scale(stream_key, shape, cuts, -0.22, 0.18)
    return jnp.clip(entries, -reach, reach).astype(kind)


def setup_inputs(seed: int = 0) -> dict:
    key_of = jax.random.split(jax.random.key(seed), 20)
    tokens = noise(key_of[0], (CLIPS, SLOT, D), 1.0, 6.0, ((0, 32),))
    context = noise(key_of[1], (CLIPS, CTXS, D), 1.0, 6.0, ((0, 32),))
    clip_lengths = draw_clip_lengths(jax.random.fold_in(key_of[19], 71), 0)
    context_frames = draw_context_frames(jax.random.fold_in(key_of[19], 71), 0)
    norm1_gain = jnp.clip(1.0 + 0.18 * jax.random.normal(key_of[4], (D,), jnp.float32), 0.099609375, 1.8984375).astype(jnp.bfloat16)
    norm1_bias = noise(key_of[5], (D,), 0.3, 1.5, ((0, 16),))
    cross_q = noise(key_of[6], (D, D), D ** -0.5, 0.21875, ((0, 16),))
    cross_k = noise(key_of[7], (D, D), D ** -0.5, 0.21875, ((0, 16),))
    cross_v = noise(key_of[8], (D, D), D ** -0.5, 0.21875, ((0, 16),))
    cross_out = noise(key_of[9], (D, D), 2 ** -0.5, 4.0, ((0, 16),))
    norm2_gain = jnp.clip(1.0 + 0.18 * jax.random.normal(key_of[10], (D,), jnp.float32), 0.099609375, 1.8984375).astype(jnp.bfloat16)
    norm2_bias = noise(key_of[11], (D,), 0.3, 1.5, ((0, 16),))
    attn_qkv = noise(key_of[12], (D, 3 * D), D ** -0.5, 0.21875, ((0, 16),))
    attn_out = noise(key_of[13], (D, D), 16 ** -0.5, 1.5, ((0, 16),))
    norm3_gain = jnp.clip(1.0 + 0.18 * jax.random.normal(key_of[14], (D,), jnp.float32), 0.099609375, 1.8984375).astype(jnp.bfloat16)
    norm3_bias = noise(key_of[15], (D,), 0.3, 1.5, ((0, 16),))
    mlp_up = noise(key_of[16], (D, FF), D ** -0.5, 0.21875, ((0, 16),))
    mlp_down = noise(key_of[17], (FF, D), FF ** -0.5, 0.109375, ((0, 16),))
    cotangent = noise(key_of[18], (CLIPS, SLOT, D), 1.0, 6.0, ((0, 32),))
    return dict(tokens=tokens, context=context, clip_lengths=clip_lengths, context_frames=context_frames, norm1_gain=norm1_gain, norm1_bias=norm1_bias, cross_q=cross_q, cross_k=cross_k, cross_v=cross_v, cross_out=cross_out, norm2_gain=norm2_gain, norm2_bias=norm2_bias, attn_qkv=attn_qkv, attn_out=attn_out, norm3_gain=norm3_gain, norm3_bias=norm3_bias, mlp_up=mlp_up, mlp_down=mlp_down, cotangent=cotangent)


@jax.custom_vjp
def low(v):
    return lax.optimization_barrier(v.astype(jnp.bfloat16)).astype(jnp.float32)

@jax.custom_vjp
def low_back(v):
    return v

def low_keep(v):
    return (low(v), None)

def low_pass(kept, grad):
    return (grad,)

def back_keep(v):
    return (v, None)

def back_low(kept, grad):
    return (low(grad),)
low.defvjp(low_keep, low_pass)
low_back.defvjp(back_keep, back_low)
epsilon = 1e-05
precise = lax.Precision.HIGHEST

def normalize(values, gain_row, bias_row):
    average = lax.optimization_barrier(jnp.mean(values, -1, keepdims=True))
    centred = values - average
    variance = lax.optimization_barrier(jnp.mean(centred * centred, -1, keepdims=True))
    return centred * lax.rsqrt(variance + epsilon) * gain_row + bias_row

def project(operand, matrix):
    return jnp.dot(operand, matrix, precision=precise, preferred_element_type=jnp.float32)

def attention(queries, key_rows, value_rows, allowed):
    row_count = queries.shape[0]
    block_rows = min(512, row_count)
    query_blocks = queries.reshape(row_count // block_rows, block_rows, HEADS, HEAD)
    starts = jnp.arange(row_count // block_rows, dtype=jnp.int32) * block_rows
    key_heads = key_rows.reshape(key_rows.shape[0], HEADS, HEAD)
    value_heads = value_rows.reshape(value_rows.shape[0], HEADS, HEAD)

    def one_block(block_pair):
        query_block, row_start = block_pair
        scores = low_back(jnp.einsum('qhd,khd->hqk', query_block, key_heads, precision=precise) * HEAD ** (-0.5))
        scores = jnp.where(allowed(row_start, block_rows)[None], scores, -1e+30)
        weights = low(jax.nn.softmax(scores, axis=-1))
        blended = jnp.einsum('hqk,khd->qhd', weights, value_heads, precision=precise)
        return blended.reshape(block_rows, HEADS * HEAD)
    blocks = lax.map(jax.checkpoint(one_block), (query_blocks, starts))
    return blocks.reshape(row_count, HEADS * HEAD)

def clip_forward(stream_in, context_rows, valid_len, frame_count, weight_set):
    gain_one, bias_one, cross_query, cross_key, cross_value, cross_proj, gain_two, bias_two, joint_qkv, self_proj, gain_three, bias_three, expand, shrink = weight_set
    key_index = jnp.arange(CTXS, dtype=jnp.int32)

    def cross_allowed(row_start, block_rows):
        return jnp.broadcast_to((key_index < frame_count * FRAME_TOK)[None, :], (block_rows, CTXS))

    def causal_allowed(row_start, block_rows):
        rows_here = row_start + jnp.arange(block_rows, dtype=jnp.int32)[:, None]
        columns = jnp.arange(SLOT, dtype=jnp.int32)[None, :]
        return (columns <= rows_here) & (columns < valid_len)
    normed_one = low(normalize(stream_in, gain_one, bias_one))
    queries_one = low(low_back(project(normed_one, cross_query)))
    keys_one = low(low_back(project(context_rows, cross_key)))
    values_one = low(low_back(project(context_rows, cross_value)))
    attended_one = low(low_back(attention(queries_one, keys_one, values_one, cross_allowed)))
    stream_mid = stream_in + low_back(project(attended_one, cross_proj))
    normed_two = low(normalize(stream_mid, gain_two, bias_two))
    joint_rows = low(low_back(project(normed_two, joint_qkv)))
    attended_two = low(low_back(attention(joint_rows[:, :D], joint_rows[:, D:2 * D], joint_rows[:, 2 * D:], causal_allowed)))
    stream_late = stream_mid + low_back(project(attended_two, self_proj))
    normed_three = low(normalize(stream_late, gain_three, bias_three))
    hidden = low(jax.nn.gelu(low_back(project(normed_three, expand)), approximate=True))
    stream_out = stream_late + low_back(project(hidden, shrink))
    padding = (jnp.arange(SLOT, dtype=jnp.int32) < valid_len).astype(jnp.float32)[:, None]
    return stream_out * padding

def reference(tokens, context, clip_lengths, context_frames, norm1_gain, norm1_bias, cross_q, cross_k, cross_v, cross_out, norm2_gain, norm2_bias, attn_qkv, attn_out, norm3_gain, norm3_bias, mlp_up, mlp_down, cotangent):
    weight_set = tuple((matrix.astype(jnp.float32) for matrix in (norm1_gain, norm1_bias, cross_q, cross_k, cross_v, cross_out, norm2_gain, norm2_bias, attn_qkv, attn_out, norm3_gain, norm3_bias, mlp_up, mlp_down)))
    zero_grads = jax.tree.map(jnp.zeros_like, weight_set)

    def scan_step(running, clip_item):
        stream_in, context_rows, valid_len, frame_count, upstream = clip_item
        context_f32 = context_rows.astype(jnp.float32)
        result, pullback = jax.vjp(lambda stream, weight_list: clip_forward(stream, context_f32, valid_len, frame_count, weight_list), stream_in.astype(jnp.float32), weight_set)
        grad_in, grad_params = pullback(upstream.astype(jnp.float32))
        running = jax.tree.map(lambda first_val, second_val: first_val + second_val, running, grad_params)
        return (running, (result.astype(jnp.bfloat16), grad_in))
    running, (outputs, grads_in) = lax.scan(scan_step, zero_grads, (tokens, context, clip_lengths, context_frames, cotangent))
    grad_scale = (CLIPS * SLOT) ** (-0.5)
    finals = [grad * grad_scale for grad in running]
    return (outputs, grads_in, finals[0], finals[1], finals[2], finals[3], finals[4], finals[5], finals[6], finals[7], finals[8], finals[9], finals[10], finals[11], finals[12], finals[13])
```

```python
import functools

import jax
import jax.numpy as jnp
from jax import lax
from jax.experimental import pallas as pl
from jax.experimental.pallas import tpu as pltpu
from jax.sharding import PartitionSpec as P

D = 768
FRAME_TOK = 256
EPS = 1e-05
MESH = pl.DeviceIdType.MESH

F32, BF16 = jnp.float32, jnp.bfloat16
NN = (((1,), (0,)), ((), ()))
NT = (((1,), (1,)), ((), ()))
TN = (((0,), (0,)), ((), ()))
def dg(a, b, dims): return lax.dot_general(a, b, dims, preferred_element_type=F32)

def head_sides(side, q2, k2, bias):
    lane = lax.broadcasted_iota(jnp.int32, (1, 128), 1)
    mine = (lane >= 64) if side else (lane < 64)
    extra = lane == (0 if side else 64)
    qa = jnp.where(mine, q2, jnp.where(extra, 1.0, 0.0).astype(BF16))
    ka = jnp.where(mine, k2, jnp.where(extra, bias, 0.0).astype(BF16))
    return qa, ka

def fwd_kernel(n_ref, q_ref, k_ref, v_ref, o_ref, l_ref, vt, *, causal, bq, unit):
    T = q_ref.shape[0]; K = k_ref.shape[0]
    live = n_ref[0] * unit
    bias = jnp.where(lax.broadcasted_iota(jnp.int32, (K, 1), 0) < live, 0.0, -1e30).astype(F32)
    q2 = q_ref[...] * BF16(0.125)
    k2 = k_ref[...]
    vt[...] = v_ref[...].T
    for side in range(2):
        qa, ka = head_sides(side, q2, k2, bias)
        for j in range(T // bq):
            span = (j + 1) * bq if causal else K
            s = dg(ka[:span], qa[j * bq:(j + 1) * bq], NT)
            if causal:
                top = j * bq
                diag = s[top:]
                ok = lax.broadcasted_iota(jnp.int32, (bq, bq), 0) <= lax.broadcasted_iota(jnp.int32, (bq, bq), 1)
                diag = jnp.where(ok, diag, -1e30)
                s = diag if top == 0 else jnp.concatenate([s[:top], diag], 0)
            m = jnp.max(s, 0, keepdims=True)
            p = jnp.exp(s - m)
            l = jnp.sum(p, 0, keepdims=True)
            ot = dg(vt[side * 64:(side + 1) * 64, :span], p.astype(BF16), NN) * (1.0 / l)
            o_ref[j * bq:(j + 1) * bq, side * 64:(side + 1) * 64] = ot.T.astype(BF16)
            l_ref[0, side:side + 1, j * bq:(j + 1) * bq] = m + jnp.log(l)

def attn_fwd(live, q, k, v, qo, ko, vo, causal, unit, bq=256):
    T, K = q.shape[0], k.shape[0]
    G = 6
    return pl.pallas_call(functools.partial(fwd_kernel, causal=causal, bq=bq, unit=unit),
        grid=(G,),
        in_specs=[pl.BlockSpec(memory_space=pltpu.SMEM), pl.BlockSpec((T, 128), lambda i: (0, i + qo)), pl.BlockSpec((K, 128), lambda i: (0, i + ko)), pl.BlockSpec((K, 128), lambda i: (0, i + vo))],
        out_specs=[pl.BlockSpec((T, 128), lambda i: (0, i)), pl.BlockSpec((1, 2, T), lambda i: (i, 0, 0))],
        out_shape=[jax.ShapeDtypeStruct((T, 768), BF16), jax.ShapeDtypeStruct((G, 2, T), F32)],
        scratch_shapes=[pltpu.VMEM((128, K), BF16)],
        compiler_params=pltpu.CompilerParams(vmem_limit_bytes=48 << 20), name="attn_fwd")(live, q, k, v)

def bwd_kernel(n_ref, q_ref, k_ref, v_ref, o_ref, do_ref, l_ref, g_ref, kt, dqt, dka, dva, *, causal, bq, bk, unit):
    T = q_ref.shape[0]; K = k_ref.shape[0]
    live = n_ref[0] * unit
    bias = jnp.where(lax.broadcasted_iota(jnp.int32, (K, 1), 0) < live, 0.0, -1e30).astype(F32)
    q2 = q_ref[...] * BF16(0.125)
    k2 = k_ref[...]; v2 = v_ref[...]
    do2 = do_ref[...]
    kt[...] = k2.T
    prod = (do2.astype(F32) * o_ref[...].astype(F32)).T
    lane = lax.broadcasted_iota(jnp.int32, (1, 128), 1)
    for side in range(2):
        qa, ka = head_sides(side, q2, k2, bias)
        mine = (lane >= 64) if side else (lane < 64)
        va = jnp.where(mine, v2, BF16(0))
        delta = jnp.sum(prod[side * 64:(side + 1) * 64], 0, keepdims=True)
        lse = l_ref[0, side:side + 1, :]
        for i in range(K // bk):
            dk = dv = None
            kb, vb = ka[i * bk:(i + 1) * bk], va[i * bk:(i + 1) * bk]
            for j in range(T // bq):
                if causal and (j + 1) * bq <= i * bk: continue
                cols = slice(j * bq, (j + 1) * bq)
                s = dg(kb, qa[cols], NT)
                p = jnp.exp(s - lse[:, cols])
                if causal and j * bq < (i + 1) * bk:
                    ok = i * bk + lax.broadcasted_iota(jnp.int32, (bk, bq), 0) <= j * bq + lax.broadcasted_iota(jnp.int32, (bk, bq), 1)
                    p = jnp.where(ok, p, 0.0)
                dp = dg(vb, do2[cols], NT)
                ds = (p * (dp - delta[:, cols])).astype(BF16)
                a = dg(p.astype(BF16), do2[cols], NN)
                b = dg(ds, q2[cols], NN)
                dv = a if dv is None else dv + a
                dk = b if dk is None else dk + b
                c = dg(kt[side * 64:(side + 1) * 64, i * bk:(i + 1) * bk], ds, NN)
                if i == 0: dqt[side * 64:(side + 1) * 64, cols] = c
                else: dqt[side * 64:(side + 1) * 64, cols] += c
            rows = slice(i * bk, (i + 1) * bk)
            if side == 0:
                dka[rows] = dk; dva[rows] = dv
            else:
                g_ref[1, rows, :] = jnp.where(lane < 64, dka[rows], dk).astype(BF16)
                g_ref[2, rows, :] = jnp.where(lane < 64, dva[rows], dv).astype(BF16)
    g_ref[0] = (dqt[...] * 0.125).T.astype(BF16)

def attn_bwd(live, q, k, v, o, do, lse, qo, ko, vo, causal, unit, bq=256, bk=256):
    T, K = q.shape[0], k.shape[0]
    G = 6
    return pl.pallas_call(functools.partial(bwd_kernel, causal=causal, bq=bq, bk=bk, unit=unit),
        grid=(G,),
        in_specs=[pl.BlockSpec(memory_space=pltpu.SMEM), pl.BlockSpec((T, 128), lambda i: (0, i + qo)), pl.BlockSpec((K, 128), lambda i: (0, i + ko)), pl.BlockSpec((K, 128), lambda i: (0, i + vo)),
                  pl.BlockSpec((T, 128), lambda i: (0, i)), pl.BlockSpec((T, 128), lambda i: (0, i)), pl.BlockSpec((1, 2, T), lambda i: (i, 0, 0))],
        out_specs=pl.BlockSpec((3, T, 128), lambda i: (0, 0, i)),
        out_shape=jax.ShapeDtypeStruct((3, T, 768), BF16),
        scratch_shapes=[pltpu.VMEM((128, K), BF16), pltpu.VMEM((128, T), F32), pltpu.VMEM((K, 128), F32), pltpu.VMEM((K, 128), F32)],
        compiler_params=pltpu.CompilerParams(vmem_limit_bytes=48 << 20), name="attn_bwd")(live, q, k, v, o, do, lse)


def grid_of(n):
    if n == 16:
        return 4, 2, 2
    if n == 64:
        return 4, 4, 4
    return n, 1, 1


def pieces_of(shards):
    out = []
    for i, s in enumerate(shards):
        rows, cols = s
        step = 256 if rows > cols // 8 and cols == 768 else min(cols, 768)
        out += [(i, c, step) for c in range(0, cols, step)]
    return out


class Place:
    def __init__(self, dims):
        self.Z, self.Y, self.X = dims
        self.me = lax.axis_index("fsdp")
        self.core = lax.axis_index("rep")
        self.z = self.me // (self.Y * self.X)
        self.y = (self.me // self.X) % self.Y
        self.x = self.me % self.X

    def at(self, z, y, x):
        return ((z * self.Y + y) * self.X + x, self.core)

    def peers(self, axis):
        count = {"z": self.Z, "y": self.Y, "x": self.X}[axis]
        mine = {"z": self.z, "y": self.y, "x": self.x}[axis]
        out = []
        for k in range(1, count):
            there = (mine + k) % count
            at = {"z": self.z, "y": self.y, "x": self.x}
            at[axis] = there
            out.append((there, (mine + count - k) % count, self.at(at["z"], at["y"], at["x"])))
        return out

    def sibling(self):
        return (self.me, 1 - self.core)

    def greet(self):
        bar = pltpu.get_barrier_semaphore()
        devs = [d for axis in "zyx" for _, _, d in self.peers(axis)] + [self.sibling()]
        for d in devs:
            pl.semaphore_signal(bar, inc=1, device_id=d, device_id_type=MESH)
        pl.semaphore_wait(bar, len(devs))


def remote(src, dst, send, recv, dev):
    return pltpu.make_async_remote_copy(
        src_ref=src, dst_ref=dst, send_sem=send, recv_sem=recv, device_id=dev, device_id_type=MESH
    )


def gather_kernel(*refs, dims, pieces, count):
    shards, outs = refs[:count], refs[count : 2 * count]
    own_sem, s1, r1, s2, r2, s3, r3, t1, u1, t2, u2, t3, u3 = refs[2 * count :]
    pl_ = Place(dims)
    Z, Y, X = dims
    pl_.greet()
    own = [
        pltpu.make_async_copy(shards[i], outs[i].at[pl_.z, pl_.y, pl_.x], own_sem.at[i])
        for i in range(count)
    ]
    for c in own:
        c.start()

    def both_ways(core, a, b):
        mine = {"z": pl_.z, "y": pl_.y, "x": pl_.x}

        def span(m, side):
            i, c, w = pieces[m]
            return pl.ds(c + side * (w // 2), w // 2)

        def view(m, side, z=None, y=None, x=None):
            i = pieces[m][0]
            every = slice(None)
            return outs[i].at[
                every if z is None else z,
                every if y is None else y,
                every if x is None else x,
                every,
                span(m, side),
            ]

        def first(m):
            i = pieces[m][0]
            for k, (_, _, dev) in enumerate(pl_.peers("z")):
                src = shards[i].at[:, span(m, core)]
                yield remote(src, view(m, core, pl_.z, pl_.y, pl_.x), s1.at[m, k], r1.at[m, k], dev)

        def first_here(m):
            for k, (_, frm, dev) in enumerate(pl_.peers("z")):
                dst = view(m, core, frm, pl_.y, pl_.x)
                yield remote(dst, dst, s1.at[m, k], r1.at[m, k], dev), dst, (frm, pl_.y, pl_.x)

        def second(m, start):
            for k, (_, frm, dev) in enumerate(pl_.peers(a)):
                at = dict(y=pl_.y, x=pl_.x)
                if not start:
                    at[a] = frm
                v = view(m, core, None, at["y"], at["x"])
                yield remote(v, v, s2.at[m, k], r2.at[m, k], dev), (None, at["y"], at["x"])

        def third(m, start):
            for k, (_, frm, dev) in enumerate(pl_.peers(b)):
                at = {a: None, b: mine[b] if start else frm}
                v = view(m, core, None, at["y"], at["x"])
                yield remote(v, v, s3.at[m, k], r3.at[m, k], dev), (None, at["y"], at["x"])

        def give(m, k, where, sem_s, sem_r):
            v = view(m, core, *where)
            return remote(v, v, sem_s.at[m, k], sem_r.at[m, k], pl_.sibling())

        M = len(pieces)
        sent = []
        for m in range(M):
            for c in first(m):
                c.start()
                sent.append(c)
        for c in own:
            c.wait()
        for t in range(M + 2):
            if t < M:
                for k, (c, _, where) in enumerate(first_here(t)):
                    c.wait_recv()
                for c, _ in second(t, True):
                    c.start()
                    sent.append(c)
                for k, (c, _, where) in enumerate(first_here(t)):
                    g = give(t, k, where, t1, u1)
                    g.start()
                    sent.append(g)
            m = t - 1
            if 0 <= m < M:
                got = list(second(m, False))
                for c, _ in got:
                    c.wait_recv()
                for c, _ in third(m, True):
                    c.start()
                    sent.append(c)
                for k, (_, where) in enumerate(got):
                    g = give(m, k, where, t2, u2)
                    g.start()
                    sent.append(g)
            m = t - 2
            if 0 <= m < M:
                got = list(third(m, False))
                for c, _ in got:
                    c.wait_recv()
                for k, (_, where) in enumerate(got):
                    g = give(m, k, where, t3, u3)
                    g.start()
                    sent.append(g)
        for c in sent:
            c.wait_send()
        for m in range(M):
            def come(k, where, sem_s, sem_r):
                v = view(m, 1 - core, *where)
                remote(v, v, sem_s.at[m, k], sem_r.at[m, k], pl_.sibling()).wait_recv()

            for k, (_, frm, _) in enumerate(pl_.peers("z")):
                come(k, (frm, pl_.y, pl_.x), t1, u1)
            for k, (_, frm, _) in enumerate(pl_.peers(b)):
                at = dict(y=pl_.y, x=pl_.x)
                at[b] = frm
                come(k, (None, at["y"], at["x"]), t2, u2)
            for k, (_, frm, _) in enumerate(pl_.peers(a)):
                at = {b: None, a: frm}
                come(k, (None, at["y"], at["x"]), t3, u3)

    @pl.when(pl_.core == 0)
    def _():
        both_ways(0, "x", "y")

    @pl.when(pl_.core == 1)
    def _():
        both_ways(1, "y", "x")


def gather_all(shards, n):
    dims = grid_of(n)
    Z, Y, X = dims
    pieces = pieces_of([s.shape for s in shards])
    M, count = len(pieces), len(shards)
    side = max(Y, X) - 1
    sem = pltpu.SemaphoreType.DMA
    counts = [max(Z - 1, 1)] * 2 + [max(side, 1)] * 4 + [max(Z - 1, 1)] * 2 + [max(side, 1)] * 4
    any_ = pl.BlockSpec(memory_space=pl.ANY)
    outs = pl.pallas_call(
        functools.partial(gather_kernel, dims=dims, pieces=pieces, count=count),
        out_shape=[jax.ShapeDtypeStruct((Z, Y, X) + s.shape, s.dtype) for s in shards],
        in_specs=[any_] * count,
        out_specs=[any_] * count,
        scratch_shapes=[sem((count,))] + [sem((M, c)) for c in counts],
        compiler_params=pltpu.CompilerParams(collective_id=0, has_side_effects=True),
        name="gather_weights",
    )(*shards)
    return [o.reshape((n,) + s.shape) for o, s in zip(outs, shards)]


def scatter_kernel(*refs, dims, pieces, count, groups, scale):
    grads, outs = refs[:count], refs[count : count + groups]
    (acc, sib, got1, got2, got3, half, lsem, s0, r0, s1, r1, s2, r2, s3, r3, s4, r4, osem) = refs[
        count + groups :
    ]
    pl_ = Place(dims)
    Z, Y, X = dims
    pl_.greet()

    def both_ways(core, a, b):
        size = {"y": Y, "x": X}
        mine = {"y": pl_.y, "x": pl_.x}
        A, B = size[a], size[b]

        def chunk(m, side, y, x):
            i, c, w, _, _ = pieces[m]
            return grads[i].at[:, y, x, :, pl.ds(c + side * (w // 2), w // 2)]

        def order(core_, y, x):
            return (y, x) if core_ == 0 else (x, y)

        def stage0(m):
            for y in range(Y):
                for x in range(X):
                    k = y * X + x
                    p, q = order(core, y, x)
                    yield pltpu.make_async_copy(chunk(m, core, y, x), acc[m].at[p, q], lsem.at[m, k])
                    p, q = order(1 - core, y, x)
                    yield remote(
                        chunk(m, 1 - core, y, x), sib[m].at[p, q], s0.at[m, k], r0.at[m, k], pl_.sibling()
                    )

        def add(dst, *srcs):
            total = dst[...].astype(F32)
            for s in srcs:
                total = total + s[...].astype(F32)
            dst[...] = total.astype(BF16)

        def stage1(m):
            for k, (there, _, dev) in enumerate(pl_.peers(b)):
                yield remote(acc[m].at[there], got1[m].at[k], s1.at[m, k], r1.at[m, k], dev)

        def stage2(m):
            for k, (there, _, dev) in enumerate(pl_.peers(a)):
                yield remote(acc[m].at[mine[b], there], got2[m].at[k], s2.at[m, k], r2.at[m, k], dev)

        def stage3(m):
            for k, (there, _, dev) in enumerate(pl_.peers("z")):
                yield remote(
                    acc[m].at[mine[b], mine[a], there], got3[m].at[k], s3.at[m, k], r3.at[m, k], dev
                )

        def stage4(m):
            yield remote(half[m].at[core], half[m].at[core], s4.at[m], r4.at[m], pl_.sibling())

        M = len(pieces)
        for m in range(M):
            for c in stage0(m):
                c.start()
        sent = []
        for t in range(M + 4):
            if t < M:
                m = t
                for c in stage0(m):
                    c.wait()
                for j in range(B):
                    add(acc[m].at[j], sib[m].at[j])
                for c in stage1(m):
                    c.start()
                    sent.append(c)
            m = t - 1
            if 0 <= m < M:
                for c in stage1(m):
                    c.wait_recv()
                add(acc[m].at[mine[b]], *[got1[m].at[k] for k in range(B - 1)])
                for c in stage2(m):
                    c.start()
                    sent.append(c)
            m = t - 2
            if 0 <= m < M:
                for c in stage2(m):
                    c.wait_recv()
                add(acc[m].at[mine[b], mine[a]], *[got2[m].at[k] for k in range(A - 1)])
                for c in stage3(m):
                    c.start()
                    sent.append(c)
            m = t - 3
            if 0 <= m < M:
                for c in stage3(m):
                    c.wait_recv()
                total = acc[m][mine[b], mine[a], pl_.z].astype(F32)
                for k in range(Z - 1):
                    total = total + got3[m][k].astype(F32)
                half[m][core] = total * scale
                for c in stage4(m):
                    c.start()
                    sent.append(c)
        for c in sent:
            c.wait_send()
        for m in range(M):
            theirs = half[m].at[1 - core]
            remote(theirs, theirs, s4.at[m], r4.at[m], pl_.sibling()).wait_recv()
            i, c, w, o, oc = pieces[m]
            for side in range(2):
                outs[o][:, oc + side * (w // 2) : oc + (side + 1) * (w // 2)] = half[m][side]

    @pl.when(pl_.core == 0)
    def _():
        both_ways(0, "x", "y")

    @pl.when(pl_.core == 1)
    def _():
        both_ways(1, "y", "x")


def scatter_all(grads, targets, n, scale):
    dims = grid_of(n)
    Z, Y, X = dims
    grads = [g.reshape((Z, Y, X) + g.shape[1:]) for g in grads]
    pieces = [
        (i, c, w, targets[i][0], targets[i][1] + c)
        for i, c, w in pieces_of([g.shape[3:] for g in grads])
    ]
    groups = 1 + max(t[0] for t in targets)
    widths = [0] * groups
    rows = [0] * groups
    for g, (o, c) in zip(grads, targets):
        widths[o] = max(widths[o], c + g.shape[4])
        rows[o] = g.shape[3]
    M, count = len(pieces), len(grads)
    S = max(Y, X)
    sem = pltpu.SemaphoreType.DMA
    any_ = pl.BlockSpec(memory_space=pl.ANY)
    vm = pl.BlockSpec(memory_space=pltpu.VMEM)
    shape = [(grads[i].shape[3], w // 2) for i, _, w, _, _ in pieces]
    one = max(S - 1, 1)
    return pl.pallas_call(
        functools.partial(
            scatter_kernel, dims=dims, pieces=pieces, count=count, groups=groups, scale=scale
        ),
        out_shape=[jax.ShapeDtypeStruct((r, w), F32) for r, w in zip(rows, widths)],
        in_specs=[any_] * count,
        out_specs=[vm] * groups,
        scratch_shapes=[
            [pltpu.VMEM((S, S, Z) + s, BF16) for s in shape],
            [pltpu.VMEM((S, S, Z) + s, BF16) for s in shape],
            [pltpu.VMEM((one, S, Z) + s, BF16) for s in shape],
            [pltpu.VMEM((one, Z) + s, BF16) for s in shape],
            [pltpu.VMEM((max(Z - 1, 1),) + s, BF16) for s in shape],
            [pltpu.VMEM((2,) + s, F32) for s in shape],
        ]
        + [sem((M, S * S))] * 3
        + [sem((M, one))] * 4
        + [sem((M, max(Z - 1, 1)))] * 2
        + [sem((M,))] * 3,
        compiler_params=pltpu.CompilerParams(
            collective_id=1, has_side_effects=True, vmem_limit_bytes=58 << 20
        ),
        name="scatter_grads",
    )(*grads)


def moments(values):
    average = jnp.mean(values, -1, keepdims=True)
    centred = values - average
    variance = jnp.mean(centred * centred, -1, keepdims=True)
    inverse = lax.rsqrt(variance + EPS)
    return centred * inverse, inverse


def norm_back(normal, inverse, gain, grad):
    m = grad * gain
    back = inverse * (
        m - jnp.mean(m, -1, keepdims=True) - normal * jnp.mean(m * normal, -1, keepdims=True)
    )
    return back, jnp.sum(grad * normal, 0), jnp.sum(grad, 0)


GELU_A = 0.7978845608028654
GELU_B = 0.044715


def gelu(u):
    return 0.5 * u * (1.0 + jnp.tanh(GELU_A * (u + GELU_B * u * u * u)))


def gelu_slope(u):
    t = jnp.tanh(GELU_A * (u + GELU_B * u * u * u))
    return 0.5 * (1.0 + t) + 0.5 * u * (1.0 - t * t) * (GELU_A * (1.0 + 3.0 * GELU_B * u * u))


def shards(
    tokens,
    context,
    clip_lengths,
    context_frames,
    norm1_gain,
    norm1_bias,
    cross_q,
    cross_k,
    cross_v,
    cross_out,
    norm2_gain,
    norm2_bias,
    attn_qkv,
    attn_out,
    norm3_gain,
    norm3_bias,
    mlp_up,
    mlp_down,
    cotangent,
):
    n = lax.axis_size("fsdp")
    stream_in = tokens[0].astype(F32)
    context_rows = context[0]
    slot_rows = stream_in.shape[0]
    own = norm1_gain.shape[0]
    padding = (jnp.arange(slot_rows) < clip_lengths[0])[:, None]
    norms = jnp.stack([norm1_gain, norm1_bias, norm2_gain, norm2_bias, norm3_gain, norm3_bias])
    norms = jnp.pad(norms, ((0, 10), (0, 256 - own)))
    whole = gather_all(
        [norms, cross_q, cross_k, cross_v, cross_out, attn_qkv, attn_out, mlp_up, mlp_down], n
    )
    norms = whole[0][:, :6, :own].transpose(1, 0, 2).reshape(6, D).astype(F32)
    gain_one, bias_one, gain_two, bias_two, gain_three, bias_three = [norms[i] for i in range(6)]
    w_q, w_k, w_v, w_o, w_qkv, w_p, w_up, w_down = [
        w.reshape(-1, w.shape[2]) for w in whole[1:]
    ]

    normal_one, inverse_one = moments(stream_in)
    h1 = (normal_one * gain_one + bias_one).astype(BF16)
    q1 = dg(h1, w_q, NN).astype(BF16)
    k1 = dg(context_rows, w_k, NN).astype(BF16)
    v1 = dg(context_rows, w_v, NN).astype(BF16)
    o1, lse1 = attn_fwd(context_frames, q1, k1, v1, 0, 0, 0, False, FRAME_TOK, 512)
    x1 = stream_in + dg(o1, w_o, NN)
    normal_two, inverse_two = moments(x1)
    h2 = (normal_two * gain_two + bias_two).astype(BF16)
    qkv = dg(h2, w_qkv, NN).astype(BF16)
    o2, lse2 = attn_fwd(clip_lengths, qkv, qkv, qkv, 0, 6, 12, True, 1, 512)
    x2 = x1 + dg(o2, w_p, NN)
    normal_three, inverse_three = moments(x2)
    h3 = (normal_three * gain_three + bias_three).astype(BF16)
    up = dg(h3, w_up, NN)
    hidden = gelu(up).astype(BF16)
    x3 = x2 + dg(hidden, w_down, NN)
    block_out = jnp.where(padding, x3, 0.0).astype(BF16)

    dx3 = jnp.where(padding, cotangent[0].astype(F32), 0.0)
    dz = dx3.astype(BF16)
    dup = (dg(dz, w_down, NT) * gelu_slope(up)).astype(BF16)
    back, g_gain3, g_bias3 = norm_back(normal_three, inverse_three, gain_three, dg(dup, w_up, NT))
    dx2 = dx3 + back
    dy2 = dx2.astype(BF16)
    do2 = dg(dy2, w_p, NT).astype(BF16)
    dqkv = attn_bwd(clip_lengths, qkv, qkv, qkv, o2, do2, lse2, 0, 6, 12, True, 1, 256, 512)
    dh2 = sum(dg(dqkv[c], w_qkv[:, c * D : (c + 1) * D], NT) for c in range(3))
    back, g_gain2, g_bias2 = norm_back(normal_two, inverse_two, gain_two, dh2)
    dx1 = dx2 + back
    dy1 = dx1.astype(BF16)
    do1 = dg(dy1, w_o, NT).astype(BF16)
    dqkv1 = attn_bwd(context_frames, q1, k1, v1, o1, do1, lse1, 0, 0, 0, False, FRAME_TOK, 1024, 256)
    dh1 = dg(dqkv1[0], w_q, NT)
    back, g_gain1, g_bias1 = norm_back(normal_one, inverse_one, gain_one, dh1)
    input_grad = dx1 + back

    g_norms = jnp.stack([g_gain1, g_bias1, g_gain2, g_bias2, g_gain3, g_bias3]).astype(BF16)
    g_norms = jnp.pad(g_norms.reshape(6, n, own).transpose(1, 0, 2), ((0, 0), (0, 10), (0, 256 - own)))

    def weight(left, right):
        g = dg(left, right, TN).astype(BF16)
        return g.reshape(n, -1, g.shape[1])

    grads = [
        (weight(hidden, dz), (8, 0)),
        (weight(h3, dup), (7, 0)),
        (weight(o2, dy2), (6, 0)),
        (weight(h2, dqkv[0]), (5, 0)),
        (weight(h2, dqkv[1]), (5, D)),
        (weight(h2, dqkv[2]), (5, 2 * D)),
        (weight(o1, dy1), (4, 0)),
        (weight(context_rows, dqkv1[2]), (3, 0)),
        (weight(context_rows, dqkv1[1]), (2, 0)),
        (weight(h1, dqkv1[0]), (1, 0)),
        (g_norms, (0, 0)),
    ]
    scale = (slot_rows * tokens.shape[0] * n * lax.axis_size("rep")) ** (-0.5)
    done = scatter_all([g for g, _ in grads], [t for _, t in grads], n, scale)
    vec = [done[0][i, :own] for i in range(6)]
    return (
        block_out[None],
        input_grad[None],
        vec[0],
        vec[1],
        done[1],
        done[2],
        done[3],
        done[4],
        vec[2],
        vec[3],
        done[5],
        done[6],
        vec[4],
        vec[5],
        done[7],
        done[8],
    )


def solution(mesh):
    in_specs = (
        P(("fsdp", "rep"), None, None),
        P(("fsdp", "rep"), None, None),
        P(("fsdp", "rep")),
        P(("fsdp", "rep")),
        P("fsdp"),
        P("fsdp"),
        P("fsdp", None),
        P("fsdp", None),
        P("fsdp", None),
        P("fsdp", None),
        P("fsdp"),
        P("fsdp"),
        P("fsdp", None),
        P("fsdp", None),
        P("fsdp"),
        P("fsdp"),
        P("fsdp", None),
        P("fsdp", None),
        P(("fsdp", "rep"), None, None),
    )
    out_specs = (
        P(("fsdp", "rep"), None, None),
        P(("fsdp", "rep"), None, None),
        P("fsdp"),
        P("fsdp"),
        P("fsdp", None),
        P("fsdp", None),
        P("fsdp", None),
        P("fsdp", None),
        P("fsdp"),
        P("fsdp"),
        P("fsdp", None),
        P("fsdp", None),
        P("fsdp"),
        P("fsdp"),
        P("fsdp", None),
        P("fsdp", None),
    )
    return jax.shard_map(shards, mesh=mesh, in_specs=in_specs, out_specs=out_specs, check_vma=False)
```

```python
import functools

import jax
import jax.numpy as jnp
from jax import lax
from jax.experimental import pallas as pl
from jax.experimental.pallas import tpu as pltpu
from jax.sharding import PartitionSpec as P

D = 768
FRAME_TOK = 256
EPS = 1e-05
MESH = pl.DeviceIdType.MESH
VMEM_BYTES = 58 << 20

F32, BF16 = jnp.float32, jnp.bfloat16
NN = (((1,), (0,)), ((), ()))
NT = (((1,), (1,)), ((), ()))
TN = (((0,), (0,)), ((), ()))
def dg(a, b, dims): return lax.dot_general(a, b, dims, preferred_element_type=F32)

def head_sides(side, q2, k2, bias):
    lane = lax.broadcasted_iota(jnp.int32, (1, 128), 1)
    mine = (lane >= 64) if side else (lane < 64)
    extra = lane == (0 if side else 64)
    qa = jnp.where(mine, q2, jnp.where(extra, 1.0, 0.0).astype(BF16))
    ka = jnp.where(mine, k2, jnp.where(extra, bias, 0.0).astype(BF16))
    return qa, ka

def fwd_kernel(n_ref, q_ref, k_ref, v_ref, o_ref, l_ref, vt, *, causal, bq, unit, at):
    T = q_ref.shape[0]; K = k_ref.shape[0]
    live = n_ref[0] * unit
    bias = jnp.where(lax.broadcasted_iota(jnp.int32, (K, 1), 0) < live, 0.0, -1e30).astype(F32)
    q2 = q_ref[...] * BF16(0.125)
    k2 = k_ref[...]
    vt[...] = v_ref[...].T
    for side in range(2):
        at(side)
        qa, ka = head_sides(side, q2, k2, bias)
        for j in range(T // bq):
            span = (j + 1) * bq if causal else K
            s = dg(ka[:span], qa[j * bq:(j + 1) * bq], NT)
            if causal:
                top = j * bq
                diag = s[top:]
                ok = lax.broadcasted_iota(jnp.int32, (bq, bq), 0) <= lax.broadcasted_iota(jnp.int32, (bq, bq), 1)
                diag = jnp.where(ok, diag, -1e30)
                s = diag if top == 0 else jnp.concatenate([s[:top], diag], 0)
            m = jnp.max(s, 0, keepdims=True)
            p = jnp.exp(s - m)
            l = jnp.sum(p, 0, keepdims=True)
            ot = dg(vt[side * 64:(side + 1) * 64, :span], p.astype(BF16), NN) * (1.0 / l)
            o_ref[j * bq:(j + 1) * bq, side * 64:(side + 1) * 64] = ot.T.astype(BF16)
            l_ref[0, side:side + 1, j * bq:(j + 1) * bq] = m + jnp.log(l)


def bwd_kernel(n_ref, q_ref, k_ref, v_ref, o_ref, do_ref, l_ref, g_ref, kt, dqt, dka, dva, *, causal, bq, bk, unit, at):
    T = q_ref.shape[0]; K = k_ref.shape[0]
    live = n_ref[0] * unit
    bias = jnp.where(lax.broadcasted_iota(jnp.int32, (K, 1), 0) < live, 0.0, -1e30).astype(F32)
    q2 = q_ref[...] * BF16(0.125)
    k2 = k_ref[...]; v2 = v_ref[...]
    do2 = do_ref[...]
    kt[...] = k2.T
    prod = (do2.astype(F32) * o_ref[...].astype(F32)).T
    lane = lax.broadcasted_iota(jnp.int32, (1, 128), 1)
    for side in range(2):
        at(side)
        qa, ka = head_sides(side, q2, k2, bias)
        mine = (lane >= 64) if side else (lane < 64)
        va = jnp.where(mine, v2, BF16(0))
        delta = jnp.sum(prod[side * 64:(side + 1) * 64], 0, keepdims=True)
        lse = l_ref[0, side:side + 1, :]
        for i in range(K // bk):
            dk = dv = None
            kb, vb = ka[i * bk:(i + 1) * bk], va[i * bk:(i + 1) * bk]
            for j in range(T // bq):
                if causal and (j + 1) * bq <= i * bk: continue
                cols = slice(j * bq, (j + 1) * bq)
                s = dg(kb, qa[cols], NT)
                p = jnp.exp(s - lse[:, cols])
                if causal and j * bq < (i + 1) * bk:
                    ok = i * bk + lax.broadcasted_iota(jnp.int32, (bk, bq), 0) <= j * bq + lax.broadcasted_iota(jnp.int32, (bk, bq), 1)
                    p = jnp.where(ok, p, 0.0)
                dp = dg(vb, do2[cols], NT)
                ds = (p * (dp - delta[:, cols])).astype(BF16)
                a = dg(p.astype(BF16), do2[cols], NN)
                b = dg(ds, q2[cols], NN)
                dv = a if dv is None else dv + a
                dk = b if dk is None else dk + b
                c = dg(kt[side * 64:(side + 1) * 64, i * bk:(i + 1) * bk], ds, NN)
                if i == 0: dqt[side * 64:(side + 1) * 64, cols] = c
                else: dqt[side * 64:(side + 1) * 64, cols] += c
            rows = slice(i * bk, (i + 1) * bk)
            if side == 0:
                dka[rows] = dk; dva[rows] = dv
            else:
                g_ref[1, rows, :] = jnp.where(lane < 64, dka[rows], dk).astype(BF16)
                g_ref[2, rows, :] = jnp.where(lane < 64, dva[rows], dv).astype(BF16)
    g_ref[0] = (dqt[...] * 0.125).T.astype(BF16)


def grid_of(n):
    if n == 16:
        return 4, 2, 2
    if n == 64:
        return 4, 4, 4
    return n, 1, 1


def cut(shapes):
    out = []
    for i, (rows, cols) in enumerate(shapes):
        step = 256 if rows > cols // 8 and cols == 768 else min(cols, 768)
        out += [(i, c, step) for c in range(0, cols, step)]
    return out


def remote(src, dst, send, recv, dev):
    return pltpu.make_async_remote_copy(
        src_ref=src, dst_ref=dst, send_sem=send, recv_sem=recv, device_id=dev, device_id_type=MESH
    )


class Place:
    def __init__(self, dims):
        self.dims = dims
        self.size = dict(zip("zyx", dims))
        Z, Y, X = dims
        self.me = lax.axis_index("fsdp")
        self.core = lax.axis_index("rep")
        self.mine = {"z": self.me // (Y * X), "y": (self.me // X) % Y, "x": self.me % X}

    def peers(self, axis):
        mine, count = self.mine[axis], self.size[axis]
        out = []
        for k in range(1, count):
            at = dict(self.mine)
            at[axis] = (mine + k) % count
            dev = ((at["z"] * self.size["y"] + at["y"]) * self.size["x"] + at["x"], self.core)
            out.append((at[axis], (mine + count - k) % count, dev))
        return out

    def sibling(self):
        return (self.me, 1 - self.core)

    def greet(self):
        bar = pltpu.get_barrier_semaphore()
        devs = [d for axis in "zyx" for _, _, d in self.peers(axis)] + [self.sibling()]
        for d in devs:
            pl.semaphore_signal(bar, inc=1, device_id=d, device_id_type=MESH)
        pl.semaphore_wait(bar, len(devs))

    def by_core(self, action):
        @pl.when(self.core == 0)
        def _():
            action(0, "x", "y")

        @pl.when(self.core == 1)
        def _():
            action(1, "y", "x")


class Gather:
    def __init__(self, shapes, n):
        self.dims = grid_of(n)
        self.pieces = cut(shapes)
        self.count = len(shapes)
        self.shapes = shapes
        self.steps = len(self.pieces) + 2

    def outs(self):
        return [jax.ShapeDtypeStruct(self.dims + tuple(s), BF16) for s in self.shapes]

    def scratch(self):
        Z, Y, X = self.dims
        M, z, s = len(self.pieces), max(self.dims[0] - 1, 1), max(Y - 1, X - 1, 1)
        sem = pltpu.SemaphoreType.DMA
        return [sem((self.count,))] + [sem((M, c)) for c in (z, z, s, s, s, s, z, z, s, s, s, s)]

    def bind(self, shards, outs, scratch):
        self.shards, self.out = shards, outs
        self.own, *self.sem = scratch
        self.place = Place(self.dims)

    def half(self, m, side):
        _, c, w = self.pieces[m]
        return pl.ds(c + side * (w // 2), w // 2)

    def view(self, m, side, at):
        z, y, x = [slice(None) if at.get(k) is None else at[k] for k in "zyx"]
        return self.out[self.pieces[m][0]].at[z, y, x, :, self.half(m, side)]

    def hop(self, stage, m, side, axes, coming):
        a, b = axes
        mine = self.place.mine
        axis = ("z", a, b)[stage]
        out = []
        for k, (_, frm, dev) in enumerate(self.place.peers(axis)):
            at = dict(mine)
            for done in ("z", a)[:stage]:
                at[done] = None
            if coming:
                at[axis] = frm
            v = self.view(m, side, at)
            src = v
            if stage == 0 and not coming:
                src = self.shards[self.pieces[m][0]].at[:, self.half(m, side)]
            s, r = self.sem[2 * stage : 2 * stage + 2]
            out.append((at, lambda v=v, src=src, s=s, r=r, k=k, dev=dev: remote(src, v, s.at[m, k], r.at[m, k], dev)))
        return out

    def give(self, stage, m, side, at, k):
        v = self.view(m, side, at)
        s, r = self.sem[6 + 2 * stage : 8 + 2 * stage]
        return remote(v, v, s.at[m, k], r.at[m, k], self.place.sibling())

    def own_copies(self):
        p = self.place.mine
        return [
            pltpu.make_async_copy(s, o.at[p["z"], p["y"], p["x"]], self.own.at[i])
            for i, (s, o) in enumerate(zip(self.shards, self.out))
        ]

    def begin(self):
        for c in self.own_copies():
            c.start()

        def go(core, a, b):
            for m in range(len(self.pieces)):
                for _, c in self.hop(0, m, core, (a, b), False):
                    c().start()

        self.place.by_core(go)

    def step(self, t):
        if t == 0:
            for c in self.own_copies():
                c.wait()

        def go(core, a, b):
            for stage in range(3):
                m = t - stage
                if not 0 <= m < len(self.pieces):
                    continue
                came = self.hop(stage, m, core, (a, b), True)
                for _, c in came:
                    c().wait_recv()
                if stage < 2:
                    for _, c in self.hop(stage + 1, m, core, (a, b), False):
                        c().start()
                for k, (at, _) in enumerate(came):
                    self.give(stage, m, core, at, k).start()

        self.place.by_core(go)

    def end(self):
        def go(core, a, b):
            for m in range(len(self.pieces)):
                for stage in range(3):
                    for k, (at, c) in enumerate(self.hop(stage, m, core, (a, b), False)):
                        c().wait_send()
                    for k, (at, _) in enumerate(self.hop(stage, m, core, (a, b), True)):
                        self.give(stage, m, core, at, k).wait_send()
                    for k, (at, _) in enumerate(self.hop(stage, m, core, (b, a), True)):
                        self.give(stage, m, 1 - core, at, k).wait_recv()

        self.place.by_core(go)


class Scatter:
    def __init__(self, shapes, targets, n):
        self.dims = grid_of(n)
        self.pieces = [(i, c, w, targets[i][0], targets[i][1] + c) for i, c, w in cut(shapes)]
        self.shapes, self.targets = shapes, targets
        self.steps = len(self.pieces) + 3

    def outs(self):
        width, rows = {}, {}
        for (r, w), (o, c) in zip(self.shapes, self.targets):
            width[o], rows[o] = max(width.get(o, 0), c + w), r
        return [jax.ShapeDtypeStruct((rows[o], width[o]), F32) for o in range(len(width))]

    def scratch(self):
        Z, Y, X = self.dims
        M, S = len(self.pieces), max(Y, X)
        one, z = max(S - 1, 1), max(Z - 1, 1)
        shape = [(self.shapes[i][0], w // 2) for i, _, w, _, _ in self.pieces]
        sem = pltpu.SemaphoreType.DMA
        lead = [(S, S, Z), (S, S, Z), (one, S, Z), (one, Z), (z,)]
        return (
            [[pltpu.VMEM(l + s, BF16) for s in shape] for l in lead]
            + [[pltpu.VMEM((2,) + s, F32) for s in shape]]
            + [sem((M, S * S))] * 3
            + [sem((M, one))] * 4
            + [sem((M, z))] * 2
            + [sem((M,))] * 2
        )

    def bind(self, grads, outs, scratch):
        self.grads, self.out = grads, outs
        self.acc, self.sib, self.got1, self.got2, self.got3, self.fin, self.lsem, *self.sem = scratch
        self.place = Place(self.dims)

    def meet(self, m, core):
        Z, Y, X = self.dims
        i, c, w, _, _ = self.pieces[m]
        for y in range(Y):
            for x in range(X):
                k = y * X + x
                take = [self.grads[i].at[:, y, x, :, pl.ds(c + s * (w // 2), w // 2)] for s in range(2)]
                at = [(y, x), (x, y)]
                yield pltpu.make_async_copy(take[core], self.acc[m].at[at[core]], self.lsem.at[m, k])
                yield remote(
                    take[1 - core],
                    self.sib[m].at[at[1 - core]],
                    self.sem[0].at[m, k],
                    self.sem[1].at[m, k],
                    self.place.sibling(),
                )

    def hop(self, stage, m, axes):
        a, b = axes
        mine = self.place.mine
        s, r = self.sem[2 * stage : 2 * stage + 2]
        got = (None, self.got1, self.got2, self.got3)[stage]
        for k, (there, _, dev) in enumerate(self.place.peers((None, b, a, "z")[stage])):
            at = (mine[b], mine[a])[: stage - 1] + (there,)
            yield remote(self.acc[m].at[at], got[m].at[k], s.at[m, k], r.at[m, k], dev)

    def swap(self, m, side):
        v = self.fin[m].at[side]
        return remote(v, v, self.sem[8].at[m], self.sem[9].at[m], self.place.sibling())

    def add(self, dst, srcs):
        total = dst[...].astype(F32)
        for s in srcs:
            total = total + s[...].astype(F32)
        dst[...] = total.astype(BF16)

    def begin(self):
        def go(core, a, b):
            for m in range(len(self.pieces)):
                for c in self.meet(m, core):
                    c.start()

        self.place.by_core(go)

    def step(self, t):
        def go(core, a, b):
            mine, size = self.place.mine, self.place.size
            for stage in range(4):
                m = t - stage
                if not 0 <= m < len(self.pieces):
                    continue
                acc = self.acc[m]
                if stage == 0:
                    for c in self.meet(m, core):
                        c.wait()
                    for j in range(size[b]):
                        self.add(acc.at[j, : size[a]], [self.sib[m].at[j, : size[a]]])
                else:
                    for c in self.hop(stage, m, (a, b)):
                        c.wait_recv()
                if stage == 1:
                    self.add(
                        acc.at[mine[b], : size[a]],
                        [self.got1[m].at[k, : size[a]] for k in range(size[b] - 1)],
                    )
                if stage == 2:
                    self.add(
                        acc.at[mine[b], mine[a]], [self.got2[m].at[k] for k in range(size[a] - 1)]
                    )
                if stage == 3:
                    total = acc[mine[b], mine[a], mine["z"]].astype(F32)
                    for k in range(size["z"] - 1):
                        total = total + self.got3[m][k].astype(F32)
                    self.fin[m][core] = total
                    self.swap(m, core).start()
                else:
                    for c in self.hop(stage + 1, m, (a, b)):
                        c.start()

        self.place.by_core(go)

    def end(self):
        def go(core, a, b):
            for m in range(len(self.pieces)):
                for stage in range(1, 4):
                    for c in self.hop(stage, m, (a, b)):
                        c.wait_send()
                self.swap(m, core).wait_send()
                self.swap(m, 1 - core).wait_recv()

        self.place.by_core(go)
        for m, (i, c, w, o, at) in enumerate(self.pieces):
            for side in range(2):
                self.out[o][:, at + side * (w // 2) : at + (side + 1) * (w // 2)] = self.fin[m][side]


def alone(engine, operands, cid, name):
    def kernel(*refs):
        count, outs = len(operands), len(engine.outs())
        engine.bind(refs[:count], refs[count : count + outs], refs[count + outs :])
        engine.place.greet()
        engine.begin()
        for t in range(engine.steps):
            engine.step(t)
        engine.end()

    space = pl.ANY if isinstance(engine, Gather) else pltpu.VMEM
    return pl.pallas_call(
        kernel,
        out_shape=engine.outs(),
        in_specs=[pl.BlockSpec(memory_space=pl.ANY)] * len(operands),
        out_specs=[pl.BlockSpec(memory_space=space)] * len(engine.outs()),
        scratch_shapes=engine.scratch(),
        compiler_params=pltpu.CompilerParams(
            collective_id=cid, has_side_effects=True, vmem_limit_bytes=VMEM_BYTES
        ),
        name=name,
    )(*operands)


class Beside:
    def __init__(self, engine, points):
        self.engine = engine
        self.points = points

    def reach(self, i, side):
        e = self.engine
        if side == 0:

            @pl.when(i == 0)
            def _():
                e.place.greet()
                e.begin()

        for t, p in enumerate(self.points):
            if p is not None and p % 2 == side:

                @pl.when(i == p // 2)
                def _(t=t):
                    e.step(t)

    def close(self, i):
        e = self.engine

        @pl.when(i == pl.num_programs(0) - 1)
        def _():
            for t, p in enumerate(self.points):
                if p is None:
                    e.step(t)
            e.end()


def paced(engine, first, each, unit, units=12):
    points = []
    for t in range(engine.steps):
        p = int(-(-(first + t * each) // unit))
        points.append(p if p < units else None)
    return points


def attend_beside(body, attn_in, in_specs, attn_out, out_specs, attn_scratch, engine, operands, points, cid, name):
    nin, nout, nscr = len(attn_in), len(attn_out), len(attn_scratch)
    moved, landed = len(operands), len(engine.outs())

    def kernel(*refs):
        at = 0
        groups = []
        for count in (nin, moved, nout, landed, nscr):
            groups.append(refs[at : at + count])
            at += count
        engine.bind(groups[1], groups[3], refs[at:])
        beside = Beside(engine, points)
        i = pl.program_id(0)
        body(*groups[0], *groups[2], *groups[4], at=lambda side: beside.reach(i, side))
        beside.close(i)

    any_ = pl.BlockSpec(memory_space=pl.ANY)
    space = pl.ANY if isinstance(engine, Gather) else pltpu.VMEM
    outs = pl.pallas_call(
        kernel,
        grid=(6,),
        in_specs=in_specs + [any_] * moved,
        out_specs=out_specs + [pl.BlockSpec(memory_space=space)] * landed,
        out_shape=attn_out + engine.outs(),
        scratch_shapes=attn_scratch + engine.scratch(),
        compiler_params=pltpu.CompilerParams(
            collective_id=cid, has_side_effects=True, vmem_limit_bytes=VMEM_BYTES
        ),
        name=name,
    )(*attn_in, *operands)
    return outs[:nout], outs[nout:]


def attn_fwd(live, q, k, v, cols, causal, unit, bq, engine, operands, points, cid, name):
    T, K = q.shape[0], k.shape[0]
    qo, ko, vo = cols
    return attend_beside(
        functools.partial(fwd_kernel, causal=causal, bq=bq, unit=unit),
        [live, q, k, v],
        [
            pl.BlockSpec(memory_space=pltpu.SMEM),
            pl.BlockSpec((T, 128), lambda i: (0, i + qo)),
            pl.BlockSpec((K, 128), lambda i: (0, i + ko)),
            pl.BlockSpec((K, 128), lambda i: (0, i + vo)),
        ],
        [jax.ShapeDtypeStruct((T, D), BF16), jax.ShapeDtypeStruct((6, 2, T), F32)],
        [pl.BlockSpec((T, 128), lambda i: (0, i)), pl.BlockSpec((1, 2, T), lambda i: (i, 0, 0))],
        [pltpu.VMEM((128, K), BF16)],
        engine,
        operands,
        points,
        cid,
        name,
    )


def attn_bwd(live, q, k, v, o, do, lse, cols, causal, unit, bq, bk, engine, operands, points, cid, name):
    T, K = q.shape[0], k.shape[0]
    qo, ko, vo = cols
    return attend_beside(
        functools.partial(bwd_kernel, causal=causal, bq=bq, bk=bk, unit=unit),
        [live, q, k, v, o, do, lse],
        [
            pl.BlockSpec(memory_space=pltpu.SMEM),
            pl.BlockSpec((T, 128), lambda i: (0, i + qo)),
            pl.BlockSpec((K, 128), lambda i: (0, i + ko)),
            pl.BlockSpec((K, 128), lambda i: (0, i + vo)),
            pl.BlockSpec((T, 128), lambda i: (0, i)),
            pl.BlockSpec((T, 128), lambda i: (0, i)),
            pl.BlockSpec((1, 2, T), lambda i: (i, 0, 0)),
        ],
        [jax.ShapeDtypeStruct((3, T, D), BF16)],
        [pl.BlockSpec((3, T, 128), lambda i: (0, 0, i))],
        [
            pltpu.VMEM((128, K), BF16),
            pltpu.VMEM((128, T), F32),
            pltpu.VMEM((K, 128), F32),
            pltpu.VMEM((K, 128), F32),
        ],
        engine,
        operands,
        points,
        cid,
        name,
    )


def finish(sums, scale):
    def kernel(*refs):
        for i, o in zip(refs[: len(sums)], refs[len(sums) :]):
            o[...] = i[...] * scale

    return pl.pallas_call(
        kernel, out_shape=[jax.ShapeDtypeStruct(s.shape, F32) for s in sums], name="finish"
    )(*sums)


def moments(values):
    average = jnp.mean(values, -1, keepdims=True)
    centred = values - average
    variance = jnp.mean(centred * centred, -1, keepdims=True)
    inverse = lax.rsqrt(variance + EPS)
    return centred * inverse, inverse


def norm_back(normal, inverse, gain, grad):
    m = grad * gain
    back = inverse * (
        m - jnp.mean(m, -1, keepdims=True) - normal * jnp.mean(m * normal, -1, keepdims=True)
    )
    return back, jnp.sum(grad * normal, 0), jnp.sum(grad, 0)


GELU_A = 0.7978845608028654
GELU_B = 0.044715


def gelu(u):
    return 0.5 * u * (1.0 + jnp.tanh(GELU_A * (u + GELU_B * u * u * u)))


def gelu_slope(u):
    t = jnp.tanh(GELU_A * (u + GELU_B * u * u * u))
    return 0.5 * (1.0 + t) + 0.5 * u * (1.0 - t * t) * (GELU_A * (1.0 + 3.0 * GELU_B * u * u))


def shards(
    tokens,
    context,
    clip_lengths,
    context_frames,
    norm1_gain,
    norm1_bias,
    cross_q,
    cross_k,
    cross_v,
    cross_out,
    norm2_gain,
    norm2_bias,
    attn_qkv,
    attn_out,
    norm3_gain,
    norm3_bias,
    mlp_up,
    mlp_down,
    cotangent,
):
    n = lax.axis_size("fsdp")
    stream_in = tokens[0].astype(F32)
    context_rows = context[0]
    slot_rows = stream_in.shape[0]
    own = norm1_gain.shape[0]
    padding = (jnp.arange(slot_rows) < clip_lengths[0])[:, None]
    norms = jnp.stack([norm1_gain, norm1_bias, norm2_gain, norm2_bias, norm3_gain, norm3_bias])
    norms = jnp.pad(norms, ((0, 10), (0, 256 - own)))

    def flat(arrays):
        return [a.reshape(-1, a.shape[4]) for a in arrays]

    def gather(arrays):
        return Gather([a.shape for a in arrays], n), arrays

    def weight(left, right):
        g = dg(left, right, TN).astype(BF16)
        return g.reshape(n, -1, g.shape[1])

    def scatter(grads):
        arrays = [g.reshape(grid_of(n) + g.shape[1:]) for g, _ in grads]
        return Scatter([a.shape[3:] for a in arrays], [t for _, t in grads], n), arrays

    first, operands = gather([norms, cross_q, cross_k, cross_v])
    norms, *whole = alone(first, operands, 0, "gather_cross")
    w_q, w_k, w_v = flat(whole)
    norms = norms.reshape((n,) + norms.shape[3:])[:, :6, :own].transpose(1, 0, 2).reshape(6, D).astype(F32)
    gain_one, bias_one, gain_two, bias_two, gain_three, bias_three = [norms[i] for i in range(6)]

    normal_one, inverse_one = moments(stream_in)
    h1 = (normal_one * gain_one + bias_one).astype(BF16)
    q1 = dg(h1, w_q, NN).astype(BF16)
    k1 = dg(context_rows, w_k, NN).astype(BF16)
    v1 = dg(context_rows, w_v, NN).astype(BF16)
    second, operands = gather([cross_out, attn_qkv, attn_out])
    (o1, lse1), whole = attn_fwd(
        context_frames, q1, k1, v1, (0, 0, 0), False, FRAME_TOK, 512,
        second, operands, paced(second, 8.0, 4.8, 2.2), 1, "cross_fwd",
    )
    w_o, w_qkv, w_p = flat(whole)
    x1 = stream_in + dg(o1, w_o, NN)
    normal_two, inverse_two = moments(x1)
    h2 = (normal_two * gain_two + bias_two).astype(BF16)
    qkv = dg(h2, w_qkv, NN).astype(BF16)
    third, operands = gather([mlp_up, mlp_down])
    (o2, lse2), whole = attn_fwd(
        clip_lengths, qkv, qkv, qkv, (0, 6, 12), True, 1, 512,
        third, operands, paced(third, 8.0, 4.8, 1.5), 2, "causal_fwd",
    )
    w_up, w_down = flat(whole)
    x2 = x1 + dg(o2, w_p, NN)
    normal_three, inverse_three = moments(x2)
    h3 = (normal_three * gain_three + bias_three).astype(BF16)
    up = dg(h3, w_up, NN)
    hidden = gelu(up).astype(BF16)
    x3 = x2 + dg(hidden, w_down, NN)
    block_out = jnp.where(padding, x3, 0.0).astype(BF16)

    dx3 = jnp.where(padding, cotangent[0].astype(F32), 0.0)
    dz = dx3.astype(BF16)
    dup = (dg(dz, w_down, NT) * gelu_slope(up)).astype(BF16)
    back, g_gain3, g_bias3 = norm_back(normal_three, inverse_three, gain_three, dg(dup, w_up, NT))
    dx2 = dx3 + back
    dy2 = dx2.astype(BF16)
    do2 = dg(dy2, w_p, NT).astype(BF16)
    fourth, operands = scatter([(weight(hidden, dz), (1, 0)), (weight(h3, dup), (0, 0))])
    (dqkv,), (s_up, s_down) = attn_bwd(
        clip_lengths, qkv, qkv, qkv, o2, do2, lse2, (0, 6, 12), True, 1, 256, 512,
        fourth, operands, paced(fourth, 8.0, 4.8, 2.45), 3, "causal_bwd",
    )
    dh2 = sum(dg(dqkv[c], w_qkv[:, c * D : (c + 1) * D], NT) for c in range(3))
    back, g_gain2, g_bias2 = norm_back(normal_two, inverse_two, gain_two, dh2)
    dx1 = dx2 + back
    dy1 = dx1.astype(BF16)
    do1 = dg(dy1, w_o, NT).astype(BF16)
    fifth, operands = scatter(
        [(weight(o2, dy2), (0, 0))]
        + [(weight(h2, dqkv[c]), (1, c * D)) for c in range(3)]
        + [(weight(o1, dy1), (2, 0))]
    )
    (dqkv1,), (s_p, s_qkv, s_o) = attn_bwd(
        context_frames, q1, k1, v1, o1, do1, lse1, (0, 0, 0), False, FRAME_TOK, 1024, 256,
        fifth, operands, paced(fifth, 8.0, 4.8, 3.1), 4, "cross_bwd",
    )
    dh1 = dg(dqkv1[0], w_q, NT)
    back, g_gain1, g_bias1 = norm_back(normal_one, inverse_one, gain_one, dh1)
    input_grad = dx1 + back

    g_norms = jnp.stack([g_gain1, g_bias1, g_gain2, g_bias2, g_gain3, g_bias3]).astype(BF16)
    g_norms = jnp.pad(g_norms.reshape(6, n, own).transpose(1, 0, 2), ((0, 0), (0, 10), (0, 256 - own)))

    sixth, operands = scatter(
        [
            (weight(context_rows, dqkv1[2]), (3, 0)),
            (weight(context_rows, dqkv1[1]), (2, 0)),
            (weight(h1, dqkv1[0]), (1, 0)),
            (g_norms, (0, 0)),
        ]
    )
    s_norms, s_q, s_k, s_v = alone(sixth, operands, 5, "scatter_cross")
    scale = (slot_rows * tokens.shape[0] * n * lax.axis_size("rep")) ** (-0.5)
    vec = [s_norms[i, :own] * scale for i in range(6)]
    done = [None, *finish([s_q, s_k, s_v, s_o, s_qkv, s_p, s_up, s_down], scale)]
    return (
        block_out[None],
        input_grad[None],
        vec[0],
        vec[1],
        done[1],
        done[2],
        done[3],
        done[4],
        vec[2],
        vec[3],
        done[5],
        done[6],
        vec[4],
        vec[5],
        done[7],
        done[8],
    )


def solution(mesh):
    in_specs = (
        P(("fsdp", "rep"), None, None),
        P(("fsdp", "rep"), None, None),
        P(("fsdp", "rep")),
        P(("fsdp", "rep")),
        P("fsdp"),
        P("fsdp"),
        P("fsdp", None),
        P("fsdp", None),
        P("fsdp", None),
        P("fsdp", None),
        P("fsdp"),
        P("fsdp"),
        P("fsdp", None),
        P("fsdp", None),
        P("fsdp"),
        P("fsdp"),
        P("fsdp", None),
        P("fsdp", None),
        P(("fsdp", "rep"), None, None),
    )
    out_specs = (
        P(("fsdp", "rep"), None, None),
        P(("fsdp", "rep"), None, None),
        P("fsdp"),
        P("fsdp"),
        P("fsdp", None),
        P("fsdp", None),
        P("fsdp", None),
        P("fsdp", None),
        P("fsdp"),
        P("fsdp"),
        P("fsdp", None),
        P("fsdp", None),
        P("fsdp"),
        P("fsdp"),
        P("fsdp", None),
        P("fsdp", None),
    )
    return jax.shard_map(shards, mesh=mesh, in_specs=in_specs, out_specs=out_specs, check_vma=False)
```

```python
import functools

import jax
import jax.numpy as jnp
from jax import lax
from jax.experimental import pallas as pl
from jax.experimental.pallas import tpu as pltpu
from jax.sharding import PartitionSpec as P

D = 768
FRAME_TOK = 256
EPS = 1e-05
MESH = pl.DeviceIdType.MESH
VMEM_BYTES = 58 << 20

F32, BF16 = jnp.float32, jnp.bfloat16
NN = (((1,), (0,)), ((), ()))
NT = (((1,), (1,)), ((), ()))
TN = (((0,), (0,)), ((), ()))
def dg(a, b, dims): return lax.dot_general(a, b, dims, preferred_element_type=F32)

def head_sides(side, q2, k2, bias):
    lane = lax.broadcasted_iota(jnp.int32, (1, 128), 1)
    mine = (lane >= 64) if side else (lane < 64)
    extra = lane == (0 if side else 64)
    qa = jnp.where(mine, q2, jnp.where(extra, 1.0, 0.0).astype(BF16))
    ka = jnp.where(mine, k2, jnp.where(extra, bias, 0.0).astype(BF16))
    return qa, ka

def fwd_kernel(n_ref, q_ref, k_ref, v_ref, o_ref, l_ref, vt, *, causal, bq, unit, at):
    T = q_ref.shape[0]; K = k_ref.shape[0]
    live = n_ref[0] * unit
    bias = jnp.where(lax.broadcasted_iota(jnp.int32, (K, 1), 0) < live, 0.0, -1e30).astype(F32)
    q2 = q_ref[...] * BF16(0.125)
    k2 = k_ref[...]
    vt[...] = v_ref[...].T
    for side in range(2):
        at(side)
        qa, ka = head_sides(side, q2, k2, bias)
        for j in range(T // bq):
            span = (j + 1) * bq if causal else K
            s = dg(ka[:span], qa[j * bq:(j + 1) * bq], NT)
            if causal:
                top = j * bq
                diag = s[top:]
                ok = lax.broadcasted_iota(jnp.int32, (bq, bq), 0) <= lax.broadcasted_iota(jnp.int32, (bq, bq), 1)
                diag = jnp.where(ok, diag, -1e30)
                s = diag if top == 0 else jnp.concatenate([s[:top], diag], 0)
            m = jnp.max(s, 0, keepdims=True)
            p = jnp.exp(s - m)
            l = jnp.sum(p, 0, keepdims=True)
            ot = dg(vt[side * 64:(side + 1) * 64, :span], p.astype(BF16), NN) * (1.0 / l)
            o_ref[j * bq:(j + 1) * bq, side * 64:(side + 1) * 64] = ot.T.astype(BF16)
            l_ref[0, side:side + 1, j * bq:(j + 1) * bq] = m + jnp.log(l)


def bwd_kernel(n_ref, q_ref, k_ref, v_ref, o_ref, do_ref, l_ref, g_ref, kt, dqt, dka, dva, *, causal, bq, bk, unit, at):
    T = q_ref.shape[0]; K = k_ref.shape[0]
    live = n_ref[0] * unit
    bias = jnp.where(lax.broadcasted_iota(jnp.int32, (K, 1), 0) < live, 0.0, -1e30).astype(F32)
    q2 = q_ref[...] * BF16(0.125)
    k2 = k_ref[...]; v2 = v_ref[...]
    do2 = do_ref[...]
    kt[...] = k2.T
    prod = (do2.astype(F32) * o_ref[...].astype(F32)).T
    lane = lax.broadcasted_iota(jnp.int32, (1, 128), 1)
    for side in range(2):
        at(side)
        qa, ka = head_sides(side, q2, k2, bias)
        mine = (lane >= 64) if side else (lane < 64)
        va = jnp.where(mine, v2, BF16(0))
        delta = jnp.sum(prod[side * 64:(side + 1) * 64], 0, keepdims=True)
        lse = l_ref[0, side:side + 1, :]
        for i in range(K // bk):
            dk = dv = None
            kb, vb = ka[i * bk:(i + 1) * bk], va[i * bk:(i + 1) * bk]
            for j in range(T // bq):
                if causal and (j + 1) * bq <= i * bk: continue
                cols = slice(j * bq, (j + 1) * bq)
                s = dg(kb, qa[cols], NT)
                p = jnp.exp(s - lse[:, cols])
                if causal and j * bq < (i + 1) * bk:
                    ok = i * bk + lax.broadcasted_iota(jnp.int32, (bk, bq), 0) <= j * bq + lax.broadcasted_iota(jnp.int32, (bk, bq), 1)
                    p = jnp.where(ok, p, 0.0)
                dp = dg(vb, do2[cols], NT)
                ds = (p * (dp - delta[:, cols])).astype(BF16)
                a = dg(p.astype(BF16), do2[cols], NN)
                b = dg(ds, q2[cols], NN)
                dv = a if dv is None else dv + a
                dk = b if dk is None else dk + b
                c = dg(kt[side * 64:(side + 1) * 64, i * bk:(i + 1) * bk], ds, NN)
                if i == 0: dqt[side * 64:(side + 1) * 64, cols] = c
                else: dqt[side * 64:(side + 1) * 64, cols] += c
            rows = slice(i * bk, (i + 1) * bk)
            if side == 0:
                dka[rows] = dk; dva[rows] = dv
            else:
                g_ref[1, rows, :] = jnp.where(lane < 64, dka[rows], dk).astype(BF16)
                g_ref[2, rows, :] = jnp.where(lane < 64, dva[rows], dv).astype(BF16)
    g_ref[0] = (dqt[...] * 0.125).T.astype(BF16)


def grid_of(n):
    if n == 16:
        return 4, 2, 2
    if n == 64:
        return 4, 4, 4
    return n, 1, 1


def cut(shapes):
    out = []
    for i, (rows, cols) in enumerate(shapes):
        step = 256 if rows > cols // 8 and cols == 768 else min(cols, 768)
        out += [(i, c, step) for c in range(0, cols, step)]
    return out


def remote(src, dst, send, recv, dev):
    return pltpu.make_async_remote_copy(
        src_ref=src, dst_ref=dst, send_sem=send, recv_sem=recv, device_id=dev, device_id_type=MESH
    )


class Place:
    def __init__(self, dims):
        self.dims = dims
        self.size = dict(zip("zyx", dims))
        Z, Y, X = dims
        self.me = lax.axis_index("fsdp")
        self.core = lax.axis_index("rep")
        self.mine = {"z": self.me // (Y * X), "y": (self.me // X) % Y, "x": self.me % X}

    def peers(self, axis):
        mine, count = self.mine[axis], self.size[axis]
        out = []
        for k in range(1, count):
            at = dict(self.mine)
            at[axis] = (mine + k) % count
            dev = ((at["z"] * self.size["y"] + at["y"]) * self.size["x"] + at["x"], self.core)
            out.append((at[axis], (mine + count - k) % count, dev))
        return out

    def sibling(self):
        return (self.me, 1 - self.core)

    def greet(self):
        bar = pltpu.get_barrier_semaphore()
        devs = [d for axis in "zyx" for _, _, d in self.peers(axis)] + [self.sibling()]
        for d in devs:
            pl.semaphore_signal(bar, inc=1, device_id=d, device_id_type=MESH)
        pl.semaphore_wait(bar, len(devs))

    def by_core(self, action):
        @pl.when(self.core == 0)
        def _():
            action(0, "x", "y")

        @pl.when(self.core == 1)
        def _():
            action(1, "y", "x")


AHEAD = 3


class Gather:
    def __init__(self, shapes, n):
        self.dims = grid_of(n)
        self.pieces = cut(shapes)
        self.count = len(shapes)
        self.shapes = shapes
        self.steps = len(self.pieces) + 2

    def outs(self):
        return [jax.ShapeDtypeStruct(self.dims + tuple(s), BF16) for s in self.shapes]

    def scratch(self):
        Z, Y, X = self.dims
        M, z, s = len(self.pieces), max(self.dims[0] - 1, 1), max(Y - 1, X - 1, 1)
        sem = pltpu.SemaphoreType.DMA
        return [sem((2, self.count))] + [sem((M, c)) for c in (z, z, s, s, s, s, z, z, s, s, s, s)]

    def bind(self, shards, outs, scratch):
        self.shards, self.out = shards, outs
        self.own, *self.sem = scratch
        self.place = Place(self.dims)

    def half(self, m, side):
        _, c, w = self.pieces[m]
        return pl.ds(c + side * (w // 2), w // 2)

    def view(self, m, side, at):
        z, y, x = [slice(None) if at.get(k) is None else at[k] for k in "zyx"]
        return self.out[self.pieces[m][0]].at[z, y, x, :, self.half(m, side)]

    def hop(self, stage, m, side, axes, coming):
        a, b = axes
        mine = self.place.mine
        axis = ("z", a, b)[stage]
        out = []
        for k, (_, frm, dev) in enumerate(self.place.peers(axis)):
            at = dict(mine)
            for done in ("z", a)[:stage]:
                at[done] = None
            if coming:
                at[axis] = frm
            v = self.view(m, side, at)
            src = v
            if stage == 0 and not coming:
                src = self.shards[self.pieces[m][0]].at[:, self.half(m, side)]
            s, r = self.sem[2 * stage : 2 * stage + 2]
            out.append((at, lambda v=v, src=src, s=s, r=r, k=k, dev=dev: remote(src, v, s.at[m, k], r.at[m, k], dev)))
        return out

    def give(self, stage, m, side, at, k):
        v = self.view(m, side, at)
        s, r = self.sem[6 + 2 * stage : 8 + 2 * stage]
        return remote(v, v, s.at[m, k], r.at[m, k], self.place.sibling())

    def own_copies(self):
        p = self.place.mine
        return [
            remote(s, o.at[p["z"], p["y"], p["x"]], self.own.at[0, i], self.own.at[1, i], self.place.sibling())
            for i, (s, o) in enumerate(zip(self.shards, self.out))
        ]

    def begin(self):
        for c in self.own_copies():
            c.start()

        def go(core, a, b):
            for m in range(min(AHEAD, len(self.pieces))):
                for _, c in self.hop(0, m, core, (a, b), False):
                    c().start()

        self.place.by_core(go)

    def step(self, t):
        if t == 0:
            for c in self.own_copies():
                c.wait()

        def go(core, a, b):
            if t + AHEAD < len(self.pieces):
                for _, c in self.hop(0, t + AHEAD, core, (a, b), False):
                    c().start()
            for stage in range(3):
                m = t - stage
                if not 0 <= m < len(self.pieces):
                    continue
                came = self.hop(stage, m, core, (a, b), True)
                for _, c in came:
                    c().wait_recv()
                if stage < 2:
                    for _, c in self.hop(stage + 1, m, core, (a, b), False):
                        c().start()
                for k, (at, _) in enumerate(came):
                    self.give(stage, m, core, at, k).start()

        self.place.by_core(go)

    def end(self):
        def go(core, a, b):
            for m in range(len(self.pieces)):
                for stage in range(3):
                    for k, (at, c) in enumerate(self.hop(stage, m, core, (a, b), False)):
                        c().wait_send()
                    for k, (at, _) in enumerate(self.hop(stage, m, core, (a, b), True)):
                        self.give(stage, m, core, at, k).wait_send()
                    for k, (at, _) in enumerate(self.hop(stage, m, core, (b, a), True)):
                        self.give(stage, m, 1 - core, at, k).wait_recv()

        self.place.by_core(go)


class Scatter:
    def __init__(self, shapes, targets, n):
        self.dims = grid_of(n)
        self.pieces = [(i, c, w, targets[i][0], targets[i][1] + c) for i, c, w in cut(shapes)]
        self.shapes, self.targets = shapes, targets
        self.steps = len(self.pieces) + 3

    def outs(self):
        width, rows = {}, {}
        for (r, w), (o, c) in zip(self.shapes, self.targets):
            width[o], rows[o] = max(width.get(o, 0), c + w), r
        return [jax.ShapeDtypeStruct((rows[o], width[o]), F32) for o in range(len(width))]

    def scratch(self):
        Z, Y, X = self.dims
        M, S = len(self.pieces), max(Y, X)
        one, z = max(S - 1, 1), max(Z - 1, 1)
        shape = [(self.shapes[i][0], w // 2) for i, _, w, _, _ in self.pieces]
        sem = pltpu.SemaphoreType.DMA
        lead = [(S, S, Z), (S, S, Z), (one, S, Z), (one, Z), (z,)]
        return (
            [[pltpu.VMEM(l + s, BF16) for s in shape] for l in lead]
            + [[pltpu.VMEM((2,) + s, F32) for s in shape]]
            + [sem((M, S * S))] * 3
            + [sem((M, one))] * 4
            + [sem((M, z))] * 2
            + [sem((M,))] * 2
        )

    def bind(self, grads, outs, scratch):
        self.grads, self.out = grads, outs
        self.acc, self.sib, self.got1, self.got2, self.got3, self.fin, self.lsem, *self.sem = scratch
        self.place = Place(self.dims)

    def meet(self, m, core):
        Z, Y, X = self.dims
        i, c, w, _, _ = self.pieces[m]
        for y in range(Y):
            for x in range(X):
                k = y * X + x
                take = [self.grads[i].at[:, y, x, :, pl.ds(c + s * (w // 2), w // 2)] for s in range(2)]
                at = [(y, x), (x, y)]
                yield pltpu.make_async_copy(take[core], self.acc[m].at[at[core]], self.lsem.at[m, k])
                yield remote(
                    take[1 - core],
                    self.sib[m].at[at[1 - core]],
                    self.sem[0].at[m, k],
                    self.sem[1].at[m, k],
                    self.place.sibling(),
                )

    def hop(self, stage, m, axes):
        a, b = axes
        mine = self.place.mine
        s, r = self.sem[2 * stage : 2 * stage + 2]
        got = (None, self.got1, self.got2, self.got3)[stage]
        for k, (there, _, dev) in enumerate(self.place.peers((None, b, a, "z")[stage])):
            at = (mine[b], mine[a])[: stage - 1] + (there,)
            yield remote(self.acc[m].at[at], got[m].at[k], s.at[m, k], r.at[m, k], dev)

    def swap(self, m, side):
        v = self.fin[m].at[side]
        return remote(v, v, self.sem[8].at[m], self.sem[9].at[m], self.place.sibling())

    def add(self, dst, srcs):
        total = dst[...].astype(F32)
        for s in srcs:
            total = total + s[...].astype(F32)
        dst[...] = total.astype(BF16)

    def begin(self):
        def go(core, a, b):
            for m in range(len(self.pieces)):
                for c in self.meet(m, core):
                    c.start()

        self.place.by_core(go)

    def step(self, t):
        def go(core, a, b):
            mine, size = self.place.mine, self.place.size
            for stage in range(4):
                m = t - stage
                if not 0 <= m < len(self.pieces):
                    continue
                acc = self.acc[m]
                if stage == 0:
                    for c in self.meet(m, core):
                        c.wait()
                    for j in range(size[b]):
                        self.add(acc.at[j, : size[a]], [self.sib[m].at[j, : size[a]]])
                else:
                    for c in self.hop(stage, m, (a, b)):
                        c.wait_recv()
                if stage == 1:
                    self.add(
                        acc.at[mine[b], : size[a]],
                        [self.got1[m].at[k, : size[a]] for k in range(size[b] - 1)],
                    )
                if stage == 2:
                    self.add(
                        acc.at[mine[b], mine[a]], [self.got2[m].at[k] for k in range(size[a] - 1)]
                    )
                if stage == 3:
                    total = acc[mine[b], mine[a], mine["z"]].astype(F32)
                    for k in range(size["z"] - 1):
                        total = total + self.got3[m][k].astype(F32)
                    self.fin[m][core] = total
                    self.swap(m, core).start()
                else:
                    for c in self.hop(stage + 1, m, (a, b)):
                        c.start()

        self.place.by_core(go)

    def end(self):
        def go(core, a, b):
            for m in range(len(self.pieces)):
                for stage in range(1, 4):
                    for c in self.hop(stage, m, (a, b)):
                        c.wait_send()
                self.swap(m, core).wait_send()
                self.swap(m, 1 - core).wait_recv()

        self.place.by_core(go)
        for m, (i, c, w, o, at) in enumerate(self.pieces):
            for side in range(2):
                self.out[o][:, at + side * (w // 2) : at + (side + 1) * (w // 2)] = self.fin[m][side]


def alone(engine, operands, cid, name):
    def kernel(*refs):
        count, outs = len(operands), len(engine.outs())
        engine.bind(refs[:count], refs[count : count + outs], refs[count + outs :])
        engine.place.greet()
        engine.begin()
        for t in range(engine.steps):
            engine.step(t)
        engine.end()

    space = pl.ANY if isinstance(engine, Gather) else pltpu.VMEM
    return pl.pallas_call(
        kernel,
        out_shape=engine.outs(),
        in_specs=[pl.BlockSpec(memory_space=pl.ANY)] * len(operands),
        out_specs=[pl.BlockSpec(memory_space=space)] * len(engine.outs()),
        scratch_shapes=engine.scratch(),
        compiler_params=pltpu.CompilerParams(
            collective_id=cid, has_side_effects=True, vmem_limit_bytes=VMEM_BYTES
        ),
        name=name,
    )(*operands)


class Beside:
    def __init__(self, engine, points):
        self.engine = engine
        self.points = points

    def reach(self, i, side):
        e = self.engine
        if side == 0:

            @pl.when(i == 0)
            def _():
                e.place.greet()
                e.begin()

        for t, p in enumerate(self.points):
            if p is not None and p % 2 == side:

                @pl.when(i == p // 2)
                def _(t=t):
                    e.step(t)

    def close(self, i):
        e = self.engine

        @pl.when(i == pl.num_programs(0) - 1)
        def _():
            for t, p in enumerate(self.points):
                if p is None:
                    e.step(t)
            e.end()


def paced(engine, first, each, unit, units=12):
    points = []
    for t in range(engine.steps):
        p = int(-(-(first + t * each) // unit))
        points.append(p if p < units else None)
    return points


def attend_beside(body, attn_in, in_specs, attn_out, out_specs, attn_scratch, engine, operands, points, cid, name):
    nin, nout, nscr = len(attn_in), len(attn_out), len(attn_scratch)
    moved, landed = len(operands), len(engine.outs())

    def kernel(*refs):
        at = 0
        groups = []
        for count in (nin, moved, nout, landed, nscr):
            groups.append(refs[at : at + count])
            at += count
        engine.bind(groups[1], groups[3], refs[at:])
        beside = Beside(engine, points)
        i = pl.program_id(0)
        body(*groups[0], *groups[2], *groups[4], at=lambda side: beside.reach(i, side))
        beside.close(i)

    any_ = pl.BlockSpec(memory_space=pl.ANY)
    space = pl.ANY if isinstance(engine, Gather) else pltpu.VMEM
    outs = pl.pallas_call(
        kernel,
        grid=(6,),
        in_specs=in_specs + [any_] * moved,
        out_specs=out_specs + [pl.BlockSpec(memory_space=space)] * landed,
        out_shape=attn_out + engine.outs(),
        scratch_shapes=attn_scratch + engine.scratch(),
        compiler_params=pltpu.CompilerParams(
            collective_id=cid, has_side_effects=True, vmem_limit_bytes=VMEM_BYTES
        ),
        name=name,
    )(*attn_in, *operands)
    return outs[:nout], outs[nout:]


def attn_fwd(live, q, k, v, cols, causal, unit, bq, engine, operands, points, cid, name):
    T, K = q.shape[0], k.shape[0]
    qo, ko, vo = cols
    return attend_beside(
        functools.partial(fwd_kernel, causal=causal, bq=bq, unit=unit),
        [live, q, k, v],
        [
            pl.BlockSpec(memory_space=pltpu.SMEM),
            pl.BlockSpec((T, 128), lambda i: (0, i + qo)),
            pl.BlockSpec((K, 128), lambda i: (0, i + ko)),
            pl.BlockSpec((K, 128), lambda i: (0, i + vo)),
        ],
        [jax.ShapeDtypeStruct((T, D), BF16), jax.ShapeDtypeStruct((6, 2, T), F32)],
        [pl.BlockSpec((T, 128), lambda i: (0, i)), pl.BlockSpec((1, 2, T), lambda i: (i, 0, 0))],
        [pltpu.VMEM((128, K), BF16)],
        engine,
        operands,
        points,
        cid,
        name,
    )


def attn_bwd(live, q, k, v, o, do, lse, cols, causal, unit, bq, bk, engine, operands, points, cid, name):
    T, K = q.shape[0], k.shape[0]
    qo, ko, vo = cols
    return attend_beside(
        functools.partial(bwd_kernel, causal=causal, bq=bq, bk=bk, unit=unit),
        [live, q, k, v, o, do, lse],
        [
            pl.BlockSpec(memory_space=pltpu.SMEM),
            pl.BlockSpec((T, 128), lambda i: (0, i + qo)),
            pl.BlockSpec((K, 128), lambda i: (0, i + ko)),
            pl.BlockSpec((K, 128), lambda i: (0, i + vo)),
            pl.BlockSpec((T, 128), lambda i: (0, i)),
            pl.BlockSpec((T, 128), lambda i: (0, i)),
            pl.BlockSpec((1, 2, T), lambda i: (i, 0, 0)),
        ],
        [jax.ShapeDtypeStruct((3, T, D), BF16)],
        [pl.BlockSpec((3, T, 128), lambda i: (0, 0, i))],
        [
            pltpu.VMEM((128, K), BF16),
            pltpu.VMEM((128, T), F32),
            pltpu.VMEM((K, 128), F32),
            pltpu.VMEM((K, 128), F32),
        ],
        engine,
        operands,
        points,
        cid,
        name,
    )


def finish(sums, scale):
    def kernel(*refs):
        for i, o in zip(refs[: len(sums)], refs[len(sums) :]):
            o[...] = i[...] * scale

    return pl.pallas_call(
        kernel, out_shape=[jax.ShapeDtypeStruct(s.shape, F32) for s in sums], name="finish"
    )(*sums)


def moments(values):
    average = jnp.mean(values, -1, keepdims=True)
    centred = values - average
    variance = jnp.mean(centred * centred, -1, keepdims=True)
    inverse = lax.rsqrt(variance + EPS)
    return centred * inverse, inverse


def norm_back(normal, inverse, gain, grad):
    m = grad * gain
    back = inverse * (
        m - jnp.mean(m, -1, keepdims=True) - normal * jnp.mean(m * normal, -1, keepdims=True)
    )
    return back, jnp.sum(grad * normal, 0), jnp.sum(grad, 0)


GELU_A = 0.7978845608028654
GELU_B = 0.044715


def gelu(u):
    return 0.5 * u * (1.0 + jnp.tanh(GELU_A * (u + GELU_B * u * u * u)))


def gelu_slope(u):
    t = jnp.tanh(GELU_A * (u + GELU_B * u * u * u))
    return 0.5 * (1.0 + t) + 0.5 * u * (1.0 - t * t) * (GELU_A * (1.0 + 3.0 * GELU_B * u * u))


def shards(
    tokens,
    context,
    clip_lengths,
    context_frames,
    norm1_gain,
    norm1_bias,
    cross_q,
    cross_k,
    cross_v,
    cross_out,
    norm2_gain,
    norm2_bias,
    attn_qkv,
    attn_out,
    norm3_gain,
    norm3_bias,
    mlp_up,
    mlp_down,
    cotangent,
):
    n = lax.axis_size("fsdp")
    stream_in = tokens[0].astype(F32)
    context_rows = context[0]
    slot_rows = stream_in.shape[0]
    own = norm1_gain.shape[0]
    padding = (jnp.arange(slot_rows) < clip_lengths[0])[:, None]
    norms = jnp.stack([norm1_gain, norm1_bias, norm2_gain, norm2_bias, norm3_gain, norm3_bias])
    norms = jnp.pad(norms, ((0, 10), (0, 256 - own)))

    def flat(arrays):
        return [a.reshape(-1, a.shape[4]) for a in arrays]

    def gather(arrays):
        return Gather([a.shape for a in arrays], n), arrays

    def weight(left, right):
        g = dg(left, right, TN).astype(BF16)
        return g.reshape(n, -1, g.shape[1])

    def scatter(grads):
        arrays = [g.reshape(grid_of(n) + g.shape[1:]) for g, _ in grads]
        return Scatter([a.shape[3:] for a in arrays], [t for _, t in grads], n), arrays

    first, operands = gather([norms, cross_q, cross_k, cross_v])
    norms, *whole = alone(first, operands, 0, "gather_cross")
    w_q, w_k, w_v = flat(whole)
    norms = norms.reshape((n,) + norms.shape[3:])[:, :6, :own].transpose(1, 0, 2).reshape(6, D).astype(F32)
    gain_one, bias_one, gain_two, bias_two, gain_three, bias_three = [norms[i] for i in range(6)]

    normal_one, inverse_one = moments(stream_in)
    h1 = (normal_one * gain_one + bias_one).astype(BF16)
    q1 = dg(h1, w_q, NN).astype(BF16)
    k1 = dg(context_rows, w_k, NN).astype(BF16)
    v1 = dg(context_rows, w_v, NN).astype(BF16)
    second, operands = gather([cross_out, attn_qkv, attn_out])
    (o1, lse1), whole = attn_fwd(
        context_frames, q1, k1, v1, (0, 0, 0), False, FRAME_TOK, 512,
        second, operands, paced(second, 8.0, 4.8, 2.2), 1, "cross_fwd",
    )
    w_o, w_qkv, w_p = flat(whole)
    x1 = stream_in + dg(o1, w_o, NN)
    normal_two, inverse_two = moments(x1)
    h2 = (normal_two * gain_two + bias_two).astype(BF16)
    qkv = dg(h2, w_qkv, NN).astype(BF16)
    third, operands = gather([mlp_up, mlp_down])
    (o2, lse2), whole = attn_fwd(
        clip_lengths, qkv, qkv, qkv, (0, 6, 12), True, 1, 512,
        third, operands, paced(third, 8.0, 4.8, 1.5), 2, "causal_fwd",
    )
    w_up, w_down = flat(whole)
    x2 = x1 + dg(o2, w_p, NN)
    normal_three, inverse_three = moments(x2)
    h3 = (normal_three * gain_three + bias_three).astype(BF16)
    up = dg(h3, w_up, NN)
    hidden = gelu(up).astype(BF16)
    x3 = x2 + dg(hidden, w_down, NN)
    block_out = jnp.where(padding, x3, 0.0).astype(BF16)

    dx3 = jnp.where(padding, cotangent[0].astype(F32), 0.0)
    dz = dx3.astype(BF16)
    dup = (dg(dz, w_down, NT) * gelu_slope(up)).astype(BF16)
    back, g_gain3, g_bias3 = norm_back(normal_three, inverse_three, gain_three, dg(dup, w_up, NT))
    dx2 = dx3 + back
    dy2 = dx2.astype(BF16)
    do2 = dg(dy2, w_p, NT).astype(BF16)
    fourth, operands = scatter([(weight(hidden, dz), (1, 0)), (weight(h3, dup), (0, 0))])
    (dqkv,), (s_up, s_down) = attn_bwd(
        clip_lengths, qkv, qkv, qkv, o2, do2, lse2, (0, 6, 12), True, 1, 256, 512,
        fourth, operands, paced(fourth, 8.0, 4.8, 2.45), 3, "causal_bwd",
    )
    dh2 = sum(dg(dqkv[c], w_qkv[:, c * D : (c + 1) * D], NT) for c in range(3))
    back, g_gain2, g_bias2 = norm_back(normal_two, inverse_two, gain_two, dh2)
    dx1 = dx2 + back
    dy1 = dx1.astype(BF16)
    do1 = dg(dy1, w_o, NT).astype(BF16)
    fifth, operands = scatter(
        [(weight(o2, dy2), (0, 0))]
        + [(weight(h2, dqkv[c]), (1, c * D)) for c in range(3)]
        + [(weight(o1, dy1), (2, 0))]
    )
    (dqkv1,), (s_p, s_qkv, s_o) = attn_bwd(
        context_frames, q1, k1, v1, o1, do1, lse1, (0, 0, 0), False, FRAME_TOK, 1024, 256,
        fifth, operands, paced(fifth, 8.0, 4.8, 3.1), 4, "cross_bwd",
    )
    dh1 = dg(dqkv1[0], w_q, NT)
    back, g_gain1, g_bias1 = norm_back(normal_one, inverse_one, gain_one, dh1)
    input_grad = dx1 + back

    g_norms = jnp.stack([g_gain1, g_bias1, g_gain2, g_bias2, g_gain3, g_bias3]).astype(BF16)
    g_norms = jnp.pad(g_norms.reshape(6, n, own).transpose(1, 0, 2), ((0, 0), (0, 10), (0, 256 - own)))

    sixth, operands = scatter(
        [
            (weight(context_rows, dqkv1[2]), (3, 0)),
            (weight(context_rows, dqkv1[1]), (2, 0)),
            (weight(h1, dqkv1[0]), (1, 0)),
            (g_norms, (0, 0)),
        ]
    )
    s_norms, s_q, s_k, s_v = alone(sixth, operands, 5, "scatter_cross")
    scale = (slot_rows * tokens.shape[0] * n * lax.axis_size("rep")) ** (-0.5)
    vec = [s_norms[i, :own] * scale for i in range(6)]
    done = [None, *finish([s_q, s_k, s_v, s_o, s_qkv, s_p, s_up, s_down], scale)]
    return (
        block_out[None],
        input_grad[None],
        vec[0],
        vec[1],
        done[1],
        done[2],
        done[3],
        done[4],
        vec[2],
        vec[3],
        done[5],
        done[6],
        vec[4],
        vec[5],
        done[7],
        done[8],
    )


def solution(mesh):
    in_specs = (
        P(("fsdp", "rep"), None, None),
        P(("fsdp", "rep"), None, None),
        P(("fsdp", "rep")),
        P(("fsdp", "rep")),
        P("fsdp"),
        P("fsdp"),
        P("fsdp", None),
        P("fsdp", None),
        P("fsdp", None),
        P("fsdp", None),
        P("fsdp"),
        P("fsdp"),
        P("fsdp", None),
        P("fsdp", None),
        P("fsdp"),
        P("fsdp"),
        P("fsdp", None),
        P("fsdp", None),
        P(("fsdp", "rep"), None, None),
    )
    out_specs = (
        P(("fsdp", "rep"), None, None),
        P(("fsdp", "rep"), None, None),
        P("fsdp"),
        P("fsdp"),
        P("fsdp", None),
        P("fsdp", None),
        P("fsdp", None),
        P("fsdp", None),
        P("fsdp"),
        P("fsdp"),
        P("fsdp", None),
        P("fsdp", None),
        P("fsdp"),
        P("fsdp"),
        P("fsdp", None),
        P("fsdp", None),
    )
    return jax.shard_map(shards, mesh=mesh, in_specs=in_specs, out_specs=out_specs, check_vma=False)
```

```python
import functools

import jax
import jax.numpy as jnp
from jax import lax
from jax.experimental import pallas as pl
from jax.experimental.pallas import tpu as pltpu
from jax.sharding import PartitionSpec as P

D = 768
FRAME_TOK = 256
EPS = 1e-05
MESH = pl.DeviceIdType.MESH
VMEM_BYTES = 58 << 20

F32, BF16 = jnp.float32, jnp.bfloat16
NN = (((1,), (0,)), ((), ()))
NT = (((1,), (1,)), ((), ()))
TN = (((0,), (0,)), ((), ()))
def dg(a, b, dims): return lax.dot_general(a, b, dims, preferred_element_type=F32)

def head_sides(side, q2, k2, bias):
    lane = lax.broadcasted_iota(jnp.int32, (1, 128), 1)
    mine = (lane >= 64) if side else (lane < 64)
    extra = lane == (0 if side else 64)
    qa = jnp.where(mine, q2, jnp.where(extra, 1.0, 0.0).astype(BF16))
    ka = jnp.where(mine, k2, jnp.where(extra, bias, 0.0).astype(BF16))
    return qa, ka

def fwd_kernel(n_ref, q_ref, k_ref, v_ref, o_ref, l_ref, vt, ot, *, causal, bq, unit, at):
    T = q_ref.shape[0]; K = k_ref.shape[0]
    live = n_ref[0] * unit
    bias = jnp.where(lax.broadcasted_iota(jnp.int32, (K, 1), 0) < live, 0.0, -1e30).astype(F32)
    q2 = q_ref[...] * BF16(0.125)
    k2 = k_ref[...]
    vt[...] = v_ref[...].T
    for side in range(2):
        at(side)
        qa, ka = head_sides(side, q2, k2, bias)
        for j in range(T // bq):
            span = (j + 1) * bq if causal else K
            s = dg(ka[:span], qa[j * bq:(j + 1) * bq], NT)
            if causal:
                top = j * bq
                diag = s[top:]
                ok = lax.broadcasted_iota(jnp.int32, (bq, bq), 0) <= lax.broadcasted_iota(jnp.int32, (bq, bq), 1)
                diag = jnp.where(ok, diag, -1e30)
                s = diag if top == 0 else jnp.concatenate([s[:top], diag], 0)
            m = jnp.max(s, 0, keepdims=True)
            p = jnp.exp(s - m)
            l = jnp.sum(p, 0, keepdims=True)
            ot[side * 64:(side + 1) * 64, j * bq:(j + 1) * bq] = dg(vt[side * 64:(side + 1) * 64, :span], p.astype(BF16), NN) * (1.0 / l)
            l_ref[0, side:side + 1, j * bq:(j + 1) * bq] = m + jnp.log(l)
    o_ref[...] = ot[...].T.astype(BF16)


def bwd_kernel(n_ref, q_ref, k_ref, v_ref, o_ref, do_ref, l_ref, g_ref, kt, dqt, dka, dva, *, causal, bq, bk, unit, at):
    T = q_ref.shape[0]; K = k_ref.shape[0]
    live = n_ref[0] * unit
    bias = jnp.where(lax.broadcasted_iota(jnp.int32, (K, 1), 0) < live, 0.0, -1e30).astype(F32)
    q2 = q_ref[...] * BF16(0.125)
    k2 = k_ref[...]; v2 = v_ref[...]
    do2 = do_ref[...]
    kt[...] = k2.T
    prod = (do2.astype(F32) * o_ref[...].astype(F32)).T
    lane = lax.broadcasted_iota(jnp.int32, (1, 128), 1)
    for side in range(2):
        at(side)
        qa, ka = head_sides(side, q2, k2, bias)
        mine = (lane >= 64) if side else (lane < 64)
        va = jnp.where(mine, v2, BF16(0))
        delta = jnp.sum(prod[side * 64:(side + 1) * 64], 0, keepdims=True)
        lse = l_ref[0, side:side + 1, :]
        for i in range(K // bk):
            dk = dv = None
            kb, vb = ka[i * bk:(i + 1) * bk], va[i * bk:(i + 1) * bk]
            for j in range(T // bq):
                if causal and (j + 1) * bq <= i * bk: continue
                cols = slice(j * bq, (j + 1) * bq)
                s = dg(kb, qa[cols], NT)
                p = jnp.exp(s - lse[:, cols])
                if causal and j * bq < (i + 1) * bk:
                    ok = i * bk + lax.broadcasted_iota(jnp.int32, (bk, bq), 0) <= j * bq + lax.broadcasted_iota(jnp.int32, (bk, bq), 1)
                    p = jnp.where(ok, p, 0.0)
                dp = dg(vb, do2[cols], NT)
                ds = (p * (dp - delta[:, cols])).astype(BF16)
                a = dg(p.astype(BF16), do2[cols], NN)
                b = dg(ds, q2[cols], NN)
                dv = a if dv is None else dv + a
                dk = b if dk is None else dk + b
                c = dg(kt[side * 64:(side + 1) * 64, i * bk:(i + 1) * bk], ds, NN)
                if i == 0: dqt[side * 64:(side + 1) * 64, cols] = c
                else: dqt[side * 64:(side + 1) * 64, cols] += c
            rows = slice(i * bk, (i + 1) * bk)
            if side == 0:
                dka[rows] = dk; dva[rows] = dv
            else:
                g_ref[1, rows, :] = jnp.where(lane < 64, dka[rows], dk).astype(BF16)
                g_ref[2, rows, :] = jnp.where(lane < 64, dva[rows], dv).astype(BF16)
    g_ref[0] = (dqt[...] * 0.125).T.astype(BF16)


def grid_of(n):
    if n == 16:
        return 4, 2, 2
    if n == 64:
        return 4, 4, 4
    return n, 1, 1


def cut(shapes):
    out = []
    for i, (rows, cols) in enumerate(shapes):
        step = 256 if rows > cols // 8 and cols == 768 else min(cols, 768)
        out += [(i, c, step) for c in range(0, cols, step)]
    return out


def remote(src, dst, send, recv, dev):
    return pltpu.make_async_remote_copy(
        src_ref=src, dst_ref=dst, send_sem=send, recv_sem=recv, device_id=dev, device_id_type=MESH
    )


class Place:
    def __init__(self, dims):
        self.dims = dims
        self.size = dict(zip("zyx", dims))
        Z, Y, X = dims
        self.me = lax.axis_index("fsdp")
        self.core = lax.axis_index("rep")
        self.mine = {"z": self.me // (Y * X), "y": (self.me // X) % Y, "x": self.me % X}

    def peers(self, axis):
        mine, count = self.mine[axis], self.size[axis]
        out = []
        for k in range(1, count):
            at = dict(self.mine)
            at[axis] = (mine + k) % count
            dev = ((at["z"] * self.size["y"] + at["y"]) * self.size["x"] + at["x"], self.core)
            out.append((at[axis], (mine + count - k) % count, dev))
        return out

    def sibling(self):
        return (self.me, 1 - self.core)

    def greet(self):
        bar = pltpu.get_barrier_semaphore()
        devs = [d for axis in "zyx" for _, _, d in self.peers(axis)] + [self.sibling()]
        for d in devs:
            pl.semaphore_signal(bar, inc=1, device_id=d, device_id_type=MESH)
        pl.semaphore_wait(bar, len(devs))

    def by_core(self, action):
        @pl.when(self.core == 0)
        def _():
            action(0, "x", "y")

        @pl.when(self.core == 1)
        def _():
            action(1, "y", "x")


AHEAD = 3


class Gather:
    def __init__(self, shapes, n):
        self.dims = grid_of(n)
        self.pieces = cut(shapes)
        self.count = len(shapes)
        self.shapes = shapes
        self.steps = len(self.pieces) + 2

    def outs(self):
        return [jax.ShapeDtypeStruct(self.dims + tuple(s), BF16) for s in self.shapes]

    def scratch(self):
        Z, Y, X = self.dims
        M, z, s = len(self.pieces), max(self.dims[0] - 1, 1), max(Y - 1, X - 1, 1)
        sem = pltpu.SemaphoreType.DMA
        return [sem((2, self.count))] + [sem((M, c)) for c in (z, z, s, s, s, s, z, z, s, s, s, s)]

    def bind(self, shards, outs, scratch):
        self.shards, self.out = shards, outs
        self.own, *self.sem = scratch
        self.place = Place(self.dims)

    def half(self, m, side):
        _, c, w = self.pieces[m]
        return pl.ds(c + side * (w // 2), w // 2)

    def view(self, m, side, at):
        z, y, x = [slice(None) if at.get(k) is None else at[k] for k in "zyx"]
        return self.out[self.pieces[m][0]].at[z, y, x, :, self.half(m, side)]

    def hop(self, stage, m, side, axes, coming):
        a, b = axes
        mine = self.place.mine
        axis = ("z", a, b)[stage]
        out = []
        for k, (_, frm, dev) in enumerate(self.place.peers(axis)):
            at = dict(mine)
            for done in ("z", a)[:stage]:
                at[done] = None
            if coming:
                at[axis] = frm
            v = self.view(m, side, at)
            src = v
            if stage == 0 and not coming:
                src = self.shards[self.pieces[m][0]].at[:, self.half(m, side)]
            s, r = self.sem[2 * stage : 2 * stage + 2]
            out.append((at, lambda v=v, src=src, s=s, r=r, k=k, dev=dev: remote(src, v, s.at[m, k], r.at[m, k], dev)))
        return out

    def give(self, stage, m, side, at, k):
        v = self.view(m, side, at)
        s, r = self.sem[6 + 2 * stage : 8 + 2 * stage]
        return remote(v, v, s.at[m, k], r.at[m, k], self.place.sibling())

    def own_copies(self):
        p = self.place.mine
        return [
            remote(s, o.at[p["z"], p["y"], p["x"]], self.own.at[0, i], self.own.at[1, i], self.place.sibling())
            for i, (s, o) in enumerate(zip(self.shards, self.out))
        ]

    def begin(self):
        for c in self.own_copies():
            c.start()

        def go(core, a, b):
            for m in range(min(AHEAD, len(self.pieces))):
                for _, c in self.hop(0, m, core, (a, b), False):
                    c().start()

        self.place.by_core(go)

    def step(self, t):
        if t == 0:
            for c in self.own_copies():
                c.wait()

        def go(core, a, b):
            if t + AHEAD < len(self.pieces):
                for _, c in self.hop(0, t + AHEAD, core, (a, b), False):
                    c().start()
            for stage in range(3):
                m = t - stage
                if not 0 <= m < len(self.pieces):
                    continue
                came = self.hop(stage, m, core, (a, b), True)
                for _, c in came:
                    c().wait_recv()
                if stage < 2:
                    for _, c in self.hop(stage + 1, m, core, (a, b), False):
                        c().start()
                for k, (at, _) in enumerate(came):
                    self.give(stage, m, core, at, k).start()

        self.place.by_core(go)

    def arrive(self, pieces):
        def go(core, a, b):
            for m in pieces:
                for stage in range(3):
                    for k, (at, _) in enumerate(self.hop(stage, m, core, (b, a), True)):
                        self.give(stage, m, 1 - core, at, k).wait_recv()

        self.place.by_core(go)

    def sent(self):
        def go(core, a, b):
            for m in range(len(self.pieces)):
                for stage in range(3):
                    for _, c in self.hop(stage, m, core, (a, b), False):
                        c().wait_send()
                    for k, (at, _) in enumerate(self.hop(stage, m, core, (a, b), True)):
                        self.give(stage, m, core, at, k).wait_send()

        self.place.by_core(go)

    def end(self):
        self.arrive(range(len(self.pieces)))
        self.sent()


class Scatter:
    def __init__(self, shapes, targets, n):
        self.dims = grid_of(n)
        self.pieces = [(i, c, w, targets[i][0], targets[i][1] + c) for i, c, w in cut(shapes)]
        self.shapes, self.targets = shapes, targets
        self.steps = len(self.pieces) + 3

    def outs(self):
        width, rows = {}, {}
        for (r, w), (o, c) in zip(self.shapes, self.targets):
            width[o], rows[o] = max(width.get(o, 0), c + w), r
        return [jax.ShapeDtypeStruct((rows[o], width[o]), F32) for o in range(len(width))]

    def scratch(self):
        Z, Y, X = self.dims
        M, S = len(self.pieces), max(Y, X)
        one, z = max(S - 1, 1), max(Z - 1, 1)
        shape = [(self.shapes[i][0], w // 2) for i, _, w, _, _ in self.pieces]
        sem = pltpu.SemaphoreType.DMA
        lead = [(S, S, Z), (S, S, Z), (one, S, Z), (one, Z), (z,)]
        return (
            [[pltpu.VMEM(l + s, BF16) for s in shape] for l in lead]
            + [[pltpu.VMEM((2,) + s, F32) for s in shape]]
            + [sem((M, S * S))] * 3
            + [sem((M, one))] * 4
            + [sem((M, z))] * 2
            + [sem((M,))] * 2
        )

    def bind(self, grads, outs, scratch):
        self.grads, self.out = grads, outs
        self.acc, self.sib, self.got1, self.got2, self.got3, self.fin, self.lsem, *self.sem = scratch
        self.place = Place(self.dims)

    def meet(self, m, core):
        Z, Y, X = self.dims
        i, c, w, _, _ = self.pieces[m]
        for y in range(Y):
            for x in range(X):
                k = y * X + x
                take = [self.grads[i].at[:, y, x, :, pl.ds(c + s * (w // 2), w // 2)] for s in range(2)]
                at = [(y, x), (x, y)]
                yield pltpu.make_async_copy(take[core], self.acc[m].at[at[core]], self.lsem.at[m, k])
                yield remote(
                    take[1 - core],
                    self.sib[m].at[at[1 - core]],
                    self.sem[0].at[m, k],
                    self.sem[1].at[m, k],
                    self.place.sibling(),
                )

    def hop(self, stage, m, axes):
        a, b = axes
        mine = self.place.mine
        s, r = self.sem[2 * stage : 2 * stage + 2]
        got = (None, self.got1, self.got2, self.got3)[stage]
        for k, (there, _, dev) in enumerate(self.place.peers((None, b, a, "z")[stage])):
            at = (mine[b], mine[a])[: stage - 1] + (there,)
            yield remote(self.acc[m].at[at], got[m].at[k], s.at[m, k], r.at[m, k], dev)

    def swap(self, m, side):
        v = self.fin[m].at[side]
        return remote(v, v, self.sem[8].at[m], self.sem[9].at[m], self.place.sibling())

    def add(self, dst, srcs):
        total = dst[...].astype(F32)
        for s in srcs:
            total = total + s[...].astype(F32)
        dst[...] = total.astype(BF16)

    def begin(self):
        def go(core, a, b):
            for m in range(len(self.pieces)):
                for c in self.meet(m, core):
                    c.start()

        self.place.by_core(go)

    def step(self, t):
        def go(core, a, b):
            mine, size = self.place.mine, self.place.size
            for stage in range(4):
                m = t - stage
                if not 0 <= m < len(self.pieces):
                    continue
                acc = self.acc[m]
                if stage == 0:
                    for c in self.meet(m, core):
                        c.wait()
                    for j in range(size[b]):
                        self.add(acc.at[j, : size[a]], [self.sib[m].at[j, : size[a]]])
                else:
                    for c in self.hop(stage, m, (a, b)):
                        c.wait_recv()
                if stage == 1:
                    self.add(
                        acc.at[mine[b], : size[a]],
                        [self.got1[m].at[k, : size[a]] for k in range(size[b] - 1)],
                    )
                if stage == 2:
                    self.add(
                        acc.at[mine[b], mine[a]], [self.got2[m].at[k] for k in range(size[a] - 1)]
                    )
                if stage == 3:
                    total = acc[mine[b], mine[a], mine["z"]].astype(F32)
                    for k in range(size["z"] - 1):
                        total = total + self.got3[m][k].astype(F32)
                    self.fin[m][core] = total
                    self.swap(m, core).start()
                else:
                    for c in self.hop(stage + 1, m, (a, b)):
                        c.start()

        self.place.by_core(go)

    def end(self):
        def go(core, a, b):
            for m in range(len(self.pieces)):
                for stage in range(1, 4):
                    for c in self.hop(stage, m, (a, b)):
                        c.wait_send()
                self.swap(m, core).wait_send()
                self.swap(m, 1 - core).wait_recv()

        self.place.by_core(go)
        for m, (i, c, w, o, at) in enumerate(self.pieces):
            for side in range(2):
                self.out[o][:, at + side * (w // 2) : at + (side + 1) * (w // 2)] = self.fin[m][side]


def alone(engine, operands, cid, name):
    def kernel(*refs):
        count, outs = len(operands), len(engine.outs())
        engine.bind(refs[:count], refs[count : count + outs], refs[count + outs :])
        engine.place.greet()
        engine.begin()
        for t in range(engine.steps):
            engine.step(t)
        engine.end()

    space = pl.ANY if isinstance(engine, Gather) else pltpu.VMEM
    return pl.pallas_call(
        kernel,
        out_shape=engine.outs(),
        in_specs=[pl.BlockSpec(memory_space=pl.ANY)] * len(operands),
        out_specs=[pl.BlockSpec(memory_space=space)] * len(engine.outs()),
        scratch_shapes=engine.scratch(),
        compiler_params=pltpu.CompilerParams(
            collective_id=cid, has_side_effects=True, vmem_limit_bytes=VMEM_BYTES
        ),
        name=name,
    )(*operands)


class Beside:
    def __init__(self, engine, points):
        self.engine = engine
        self.points = points

    def reach(self, i, side):
        e = self.engine
        if side == 0:

            @pl.when(i == 0)
            def _():
                e.place.greet()
                e.begin()

        for t, p in enumerate(self.points):
            if p is not None and p % 2 == side:

                @pl.when(i == p // 2)
                def _(t=t):
                    e.step(t)

    def close(self, i):
        e = self.engine

        @pl.when(i == pl.num_programs(0) - 1)
        def _():
            for t, p in enumerate(self.points):
                if p is None:
                    e.step(t)
            e.end()


def paced(engine, first, each, unit, units=12):
    points = []
    for t in range(engine.steps):
        p = int(-(-(first + t * each) // unit))
        points.append(p if p < units else None)
    return points


def attend_beside(body, attn_in, in_specs, attn_out, out_specs, attn_scratch, engine, operands, points, cid, name):
    nin, nout, nscr = len(attn_in), len(attn_out), len(attn_scratch)
    moved, landed = len(operands), len(engine.outs())

    def kernel(*refs):
        at = 0
        groups = []
        for count in (nin, moved, nout, landed, nscr):
            groups.append(refs[at : at + count])
            at += count
        engine.bind(groups[1], groups[3], refs[at:])
        beside = Beside(engine, points)
        i = pl.program_id(0)
        body(*groups[0], *groups[2], *groups[4], at=lambda side: beside.reach(i, side))
        beside.close(i)

    any_ = pl.BlockSpec(memory_space=pl.ANY)
    space = pl.ANY if isinstance(engine, Gather) else pltpu.VMEM
    outs = pl.pallas_call(
        kernel,
        grid=(6,),
        in_specs=in_specs + [any_] * moved,
        out_specs=out_specs + [pl.BlockSpec(memory_space=space)] * landed,
        out_shape=attn_out + engine.outs(),
        scratch_shapes=attn_scratch + engine.scratch(),
        compiler_params=pltpu.CompilerParams(
            collective_id=cid, has_side_effects=True, vmem_limit_bytes=VMEM_BYTES
        ),
        name=name,
    )(*attn_in, *operands)
    return outs[:nout], outs[nout:]


def attn_fwd(live, q, k, v, cols, causal, unit, bq, engine, operands, points, cid, name):
    T, K = q.shape[0], k.shape[0]
    qo, ko, vo = cols
    return attend_beside(
        functools.partial(fwd_kernel, causal=causal, bq=bq, unit=unit),
        [live, q, k, v],
        [
            pl.BlockSpec(memory_space=pltpu.SMEM),
            pl.BlockSpec((T, 128), lambda i: (0, i + qo)),
            pl.BlockSpec((K, 128), lambda i: (0, i + ko)),
            pl.BlockSpec((K, 128), lambda i: (0, i + vo)),
        ],
        [jax.ShapeDtypeStruct((T, D), BF16), jax.ShapeDtypeStruct((6, 2, T), F32)],
        [pl.BlockSpec((T, 128), lambda i: (0, i)), pl.BlockSpec((1, 2, T), lambda i: (i, 0, 0))],
        [pltpu.VMEM((128, K), BF16), pltpu.VMEM((128, T), F32)],
        engine,
        operands,
        points,
        cid,
        name,
    )


def attn_bwd(live, q, k, v, o, do, lse, cols, causal, unit, bq, bk, engine, operands, points, cid, name):
    T, K = q.shape[0], k.shape[0]
    qo, ko, vo = cols
    return attend_beside(
        functools.partial(bwd_kernel, causal=causal, bq=bq, bk=bk, unit=unit),
        [live, q, k, v, o, do, lse],
        [
            pl.BlockSpec(memory_space=pltpu.SMEM),
            pl.BlockSpec((T, 128), lambda i: (0, i + qo)),
            pl.BlockSpec((K, 128), lambda i: (0, i + ko)),
            pl.BlockSpec((K, 128), lambda i: (0, i + vo)),
            pl.BlockSpec((T, 128), lambda i: (0, i)),
            pl.BlockSpec((T, 128), lambda i: (0, i)),
            pl.BlockSpec((1, 2, T), lambda i: (i, 0, 0)),
        ],
        [jax.ShapeDtypeStruct((3, T, D), BF16)],
        [pl.BlockSpec((3, T, 128), lambda i: (0, 0, i))],
        [
            pltpu.VMEM((128, K), BF16),
            pltpu.VMEM((128, T), F32),
            pltpu.VMEM((K, 128), F32),
            pltpu.VMEM((K, 128), F32),
        ],
        engine,
        operands,
        points,
        cid,
        name,
    )


def finish(sums, scale):
    def kernel(*refs):
        for i, o in zip(refs[: len(sums)], refs[len(sums) :]):
            o[...] = i[...] * scale

    return pl.pallas_call(
        kernel, out_shape=[jax.ShapeDtypeStruct(s.shape, F32) for s in sums], name="finish"
    )(*sums)


def moments(values):
    average = jnp.mean(values, -1, keepdims=True)
    centred = values - average
    variance = jnp.mean(centred * centred, -1, keepdims=True)
    inverse = lax.rsqrt(variance + EPS)
    return centred * inverse, inverse


def norm_back(normal, inverse, gain, grad):
    m = grad * gain
    back = inverse * (
        m - jnp.mean(m, -1, keepdims=True) - normal * jnp.mean(m * normal, -1, keepdims=True)
    )
    return back, jnp.sum(grad * normal, 0), jnp.sum(grad, 0)


GELU_A = 0.7978845608028654
GELU_B = 0.044715


def gelu(u):
    return 0.5 * u * (1.0 + jnp.tanh(GELU_A * (u + GELU_B * u * u * u)))


def gelu_slope(u):
    t = jnp.tanh(GELU_A * (u + GELU_B * u * u * u))
    return 0.5 * (1.0 + t) + 0.5 * u * (1.0 - t * t) * (GELU_A * (1.0 + 3.0 * GELU_B * u * u))


def blocks(rows, step, body):
    def go(r, _):
        body(pl.ds(pl.multiple_of(r * step, step), step))
        return 0

    lax.fori_loop(0, rows // step, go, 0)


def pair(ref, i, first=0):
    return ref.at[:, pl.ds(pl.multiple_of(first + i * 128, 128), 128)]


def norm_rows(packed):
    count = packed.shape[0]
    own = D // count
    total = None
    for j in range(count):
        r = lax.broadcasted_iota(jnp.int32, (128, D), 0)
        c = lax.broadcasted_iota(jnp.int32, (128, D), 1)
        spot = jnp.where((c == r + own * j) & (r < own), 1.0, 0.0).astype(BF16)
        part = dg(packed[j, :, :128], spot, NN)
        total = part if total is None else total + part
    return total


def forward_kernel(eng, ticks_cross, ticks_causal, *refs):
    it = iter(refs)

    def take(count):
        return [next(it) for _ in range(count)]

    clip, frames, tok_in, ctx_in = take(4)
    shards = take(eng.count)
    whole = take(eng.count)
    q1_o, k1_o, v1_o, o1_o, h1_o, x1_o, h2_o, qkv_o, o2_o, x2_o, h3_o, lse1_o, lse2_o, norms_o = take(14)
    tok, ctx, q1, k1, v1, o1, h1, x1, h2, qkv, o2, x2, h3, lse1, lse2, norms = take(16)
    packed, wa, wb, wqkv, vt, ot, isem, wsem, osem = take(9)
    eng.bind(shards, whole, list(it))
    T = tok.shape[0]
    eng.place.greet()
    eng.begin()
    loads = [pltpu.make_async_copy(ctx_in, ctx, isem.at[0]), pltpu.make_async_copy(tok_in, tok, isem.at[1])]
    for c in loads:
        c.start()
    saves = []

    def save(ref, out):
        c = pltpu.make_async_copy(ref, out, osem.at[len(saves)])
        c.start()
        saves.append(c)

    def fetch(i, pieces, ref):
        eng.arrive(pieces)
        c = pltpu.make_async_copy(whole[i], ref, wsem)
        c.start()
        c.wait()

    def matrix(ref, c=0):
        return ref[:, :, :, :, c : c + D].reshape(D, D)

    for t in range(3):
        eng.step(t)
    fetch(0, [0], wa)
    loads[0].wait()

    def keys(r):
        k1[r] = dg(ctx[r], matrix(wa), NN).astype(BF16)

    blocks(T, 256, keys)
    save(k1, k1_o)
    eng.step(3)
    fetch(1, [1], wb)

    def values(r):
        v1[r] = dg(ctx[r], matrix(wb), NN).astype(BF16)

    blocks(T, 256, values)
    save(v1, v1_o)
    eng.step(4)
    fetch(2, [2], packed)
    norms[...] = norm_rows(packed[...].reshape((-1,) + packed.shape[3:]))
    save(norms, norms_o)
    loads[1].wait()

    def first_norm(r):
        normal, _ = moments(tok[r].astype(F32))
        h1[r] = (normal * norms[0:1] + norms[1:2]).astype(BF16)

    blocks(T, 128, first_norm)
    save(h1, h1_o)
    eng.step(5)
    fetch(3, [3], wa)

    def queries(r):
        q1[r] = dg(h1[r], matrix(wa), NN).astype(BF16)

    blocks(T, 256, queries)
    save(q1, q1_o)

    def heads(ticks, body):
        def go(i, _):
            def at(side):
                for t, p in ticks:
                    if p % 2 == side:
                        pl.when(i == p // 2)(functools.partial(eng.step, t))

            body(i, at)
            return 0

        lax.fori_loop(0, 6, go, 0)

    heads(
        ticks_cross,
        lambda i, at: fwd_kernel(
            frames, pair(q1, i), pair(k1, i), pair(v1, i), pair(o1, i), lse1.at[pl.ds(i, 1)], vt, ot,
            causal=False, bq=512, unit=FRAME_TOK, at=at,
        ),
    )
    save(o1, o1_o)
    save(lse1, lse1_o)
    fetch(4, [4], wb)
    fetch(5, [5, 6, 7], wqkv)

    def middle(r):
        x = tok[r].astype(F32) + dg(o1[r], matrix(wb), NN)
        x1[r] = x
        normal, _ = moments(x)
        h2[r] = (normal * norms[2:3] + norms[3:4]).astype(BF16)
        for c in range(3):
            qkv[r, c * D : (c + 1) * D] = dg(h2[r], matrix(wqkv, c * D), NN).astype(BF16)

    blocks(T, 256, middle)
    for ref, out in ((x1, x1_o), (h2, h2_o), (qkv, qkv_o)):
        save(ref, out)
    heads(
        ticks_causal,
        lambda i, at: fwd_kernel(
            clip, pair(qkv, i), pair(qkv, i, D), pair(qkv, i, 2 * D), pair(o2, i), lse2.at[pl.ds(i, 1)], vt, ot,
            causal=True, bq=512, unit=1, at=at,
        ),
    )
    save(o2, o2_o)
    save(lse2, lse2_o)
    fetch(6, [8], wa)

    def late(r):
        x = x1[r] + dg(o2[r], matrix(wa), NN)
        x2[r] = x
        normal, _ = moments(x)
        h3[r] = (normal * norms[4:5] + norms[5:6]).astype(BF16)

    blocks(T, 256, late)
    save(x2, x2_o)
    save(h3, h3_o)
    taken = [t for t, _ in ticks_cross + ticks_causal]
    for t in range(6, eng.steps):
        if t not in taken:
            eng.step(t)
    eng.arrive(range(9, len(eng.pieces)))
    eng.sent()
    for c in saves:
        c.wait()


def forward(clip, frames, tok, ctx, shards, n, cid):
    eng = Gather([s.shape for s in shards], n)
    T = tok.shape[0]
    wide = jax.ShapeDtypeStruct((T, D), BF16)
    full = jax.ShapeDtypeStruct((T, D), F32)
    lse = jax.ShapeDtypeStruct((6, 2, T), F32)
    kept = [wide] * 5 + [full, wide, jax.ShapeDtypeStruct((T, 3 * D), BF16), wide, full, wide, lse, lse]
    kept.append(jax.ShapeDtypeStruct((16, D), F32))
    own = shards[0].shape[0]
    square = pltpu.VMEM(eng.dims + (own, D), BF16)
    any_ = pl.BlockSpec(memory_space=pl.ANY)
    smem = pl.BlockSpec(memory_space=pltpu.SMEM)
    sem = pltpu.SemaphoreType.DMA
    ticks_cross = [(6 + k, 2 * k + 1) for k in range(6)]
    ticks_causal = [(12 + k, 3 * k) for k in range(4)]
    outs = pl.pallas_call(
        functools.partial(forward_kernel, eng, ticks_cross, ticks_causal),
        out_shape=eng.outs() + kept,
        in_specs=[smem, smem] + [any_] * (2 + eng.count),
        out_specs=[any_] * (eng.count + len(kept)),
        scratch_shapes=[pltpu.VMEM((T, D), BF16)] * 2
        + [pltpu.VMEM(kept[i].shape, kept[i].dtype) for i in (0, 1, 2, 3, 4, 5, 6, 7, 8, 9, 10, 11, 12, 13)]
        + [pltpu.VMEM(eng.dims + shards[2].shape, BF16), square, square]
        + [pltpu.VMEM(eng.dims + (own, 3 * D), BF16), pltpu.VMEM((128, T), BF16), pltpu.VMEM((128, T), F32)]
        + [sem((2,)), sem, sem((16,))]
        + eng.scratch(),
        compiler_params=pltpu.CompilerParams(
            collective_id=cid, has_side_effects=True, vmem_limit_bytes=VMEM_BYTES
        ),
        name="forward",
    )(clip, frames, tok, ctx, *shards)
    return outs[: eng.count], outs[eng.count :]


def shards(
    tokens,
    context,
    clip_lengths,
    context_frames,
    norm1_gain,
    norm1_bias,
    cross_q,
    cross_k,
    cross_v,
    cross_out,
    norm2_gain,
    norm2_bias,
    attn_qkv,
    attn_out,
    norm3_gain,
    norm3_bias,
    mlp_up,
    mlp_down,
    cotangent,
):
    n = lax.axis_size("fsdp")
    stream_in = tokens[0].astype(F32)
    context_rows = context[0]
    slot_rows = stream_in.shape[0]
    own = norm1_gain.shape[0]
    padding = (jnp.arange(slot_rows) < clip_lengths[0])[:, None]
    norms = jnp.stack([norm1_gain, norm1_bias, norm2_gain, norm2_bias, norm3_gain, norm3_bias])
    norms = jnp.pad(norms, ((0, 10), (0, 256 - own)))

    def flat(arrays):
        return [a.reshape(-1, a.shape[4]) for a in arrays]

    def gather(arrays):
        return Gather([a.shape for a in arrays], n), arrays

    def weight(left, right):
        g = dg(left, right, TN).astype(BF16)
        return g.reshape(n, -1, g.shape[1])

    def scatter(grads):
        arrays = [g.reshape(grid_of(n) + g.shape[1:]) for g, _ in grads]
        return Scatter([a.shape[3:] for a in arrays], [t for _, t in grads], n), arrays

    if own % 16 == 0:
        whole, kept = forward(
            clip_lengths,
            context_frames,
            tokens[0],
            context_rows,
            [cross_k, cross_v, norms, cross_q, cross_out, attn_qkv, attn_out, mlp_up, mlp_down],
            n,
            0,
        )
        w_k, w_v, _, w_q, w_o, w_qkv, w_p, w_up, w_down = flat(whole)
        q1, k1, v1, o1, h1, x1, h2, qkv, o2, x2, h3, lse1, lse2, norms = kept
        gain_one, bias_one, gain_two, bias_two, gain_three, bias_three = [norms[i] for i in range(6)]
        normal_one, inverse_one = moments(stream_in)
        normal_two, inverse_two = moments(x1)
        normal_three, inverse_three = moments(x2)
    else:
        first, operands = gather([norms, cross_q, cross_k, cross_v])
        norms, *whole = alone(first, operands, 0, "gather_cross")
        w_q, w_k, w_v = flat(whole)
        norms = norms.reshape((n,) + norms.shape[3:])[:, :6, :own].transpose(1, 0, 2).reshape(6, D).astype(F32)
        gain_one, bias_one, gain_two, bias_two, gain_three, bias_three = [norms[i] for i in range(6)]

        normal_one, inverse_one = moments(stream_in)
        h1 = (normal_one * gain_one + bias_one).astype(BF16)
        q1 = dg(h1, w_q, NN).astype(BF16)
        k1 = dg(context_rows, w_k, NN).astype(BF16)
        v1 = dg(context_rows, w_v, NN).astype(BF16)
        second, operands = gather([cross_out, attn_qkv, attn_out])
        (o1, lse1), whole = attn_fwd(
            context_frames, q1, k1, v1, (0, 0, 0), False, FRAME_TOK, 512,
            second, operands, paced(second, 8.0, 4.8, 2.2), 1, "cross_fwd",
        )
        w_o, w_qkv, w_p = flat(whole)
        x1 = stream_in + dg(o1, w_o, NN)
        normal_two, inverse_two = moments(x1)
        h2 = (normal_two * gain_two + bias_two).astype(BF16)
        qkv = dg(h2, w_qkv, NN).astype(BF16)
        third, operands = gather([mlp_up, mlp_down])
        (o2, lse2), whole = attn_fwd(
            clip_lengths, qkv, qkv, qkv, (0, 6, 12), True, 1, 512,
            third, operands, paced(third, 8.0, 4.8, 1.5), 2, "causal_fwd",
        )
        w_up, w_down = flat(whole)
        x2 = x1 + dg(o2, w_p, NN)
        normal_three, inverse_three = moments(x2)
        h3 = (normal_three * gain_three + bias_three).astype(BF16)
    up = dg(h3, w_up, NN)
    hidden = gelu(up).astype(BF16)
    x3 = x2 + dg(hidden, w_down, NN)
    block_out = jnp.where(padding, x3, 0.0).astype(BF16)

    dx3 = jnp.where(padding, cotangent[0].astype(F32), 0.0)
    dz = dx3.astype(BF16)
    dup = (dg(dz, w_down, NT) * gelu_slope(up)).astype(BF16)
    back, g_gain3, g_bias3 = norm_back(normal_three, inverse_three, gain_three, dg(dup, w_up, NT))
    dx2 = dx3 + back
    dy2 = dx2.astype(BF16)
    do2 = dg(dy2, w_p, NT).astype(BF16)
    fourth, operands = scatter([(weight(hidden, dz), (1, 0)), (weight(h3, dup), (0, 0))])
    (dqkv,), (s_up, s_down) = attn_bwd(
        clip_lengths, qkv, qkv, qkv, o2, do2, lse2, (0, 6, 12), True, 1, 256, 512,
        fourth, operands, paced(fourth, 8.0, 4.8, 2.45), 3, "causal_bwd",
    )
    dh2 = sum(dg(dqkv[c], w_qkv[:, c * D : (c + 1) * D], NT) for c in range(3))
    back, g_gain2, g_bias2 = norm_back(normal_two, inverse_two, gain_two, dh2)
    dx1 = dx2 + back
    dy1 = dx1.astype(BF16)
    do1 = dg(dy1, w_o, NT).astype(BF16)
    fifth, operands = scatter(
        [(weight(o2, dy2), (0, 0))]
        + [(weight(h2, dqkv[c]), (1, c * D)) for c in range(3)]
        + [(weight(o1, dy1), (2, 0))]
    )
    (dqkv1,), (s_p, s_qkv, s_o) = attn_bwd(
        context_frames, q1, k1, v1, o1, do1, lse1, (0, 0, 0), False, FRAME_TOK, 1024, 256,
        fifth, operands, paced(fifth, 8.0, 4.8, 3.1), 4, "cross_bwd",
    )
    dh1 = dg(dqkv1[0], w_q, NT)
    back, g_gain1, g_bias1 = norm_back(normal_one, inverse_one, gain_one, dh1)
    input_grad = dx1 + back

    g_norms = jnp.stack([g_gain1, g_bias1, g_gain2, g_bias2, g_gain3, g_bias3]).astype(BF16)
    g_norms = jnp.pad(g_norms.reshape(6, n, own).transpose(1, 0, 2), ((0, 0), (0, 10), (0, 256 - own)))

    sixth, operands = scatter(
        [
            (weight(context_rows, dqkv1[2]), (3, 0)),
            (weight(context_rows, dqkv1[1]), (2, 0)),
            (weight(h1, dqkv1[0]), (1, 0)),
            (g_norms, (0, 0)),
        ]
    )
    s_norms, s_q, s_k, s_v = alone(sixth, operands, 5, "scatter_cross")
    scale = (slot_rows * tokens.shape[0] * n * lax.axis_size("rep")) ** (-0.5)
    vec = [s_norms[i, :own] * scale for i in range(6)]
    done = [None, *finish([s_q, s_k, s_v, s_o, s_qkv, s_p, s_up, s_down], scale)]
    return (
        block_out[None],
        input_grad[None],
        vec[0],
        vec[1],
        done[1],
        done[2],
        done[3],
        done[4],
        vec[2],
        vec[3],
        done[5],
        done[6],
        vec[4],
        vec[5],
        done[7],
        done[8],
    )


def solution(mesh):
    in_specs = (
        P(("fsdp", "rep"), None, None),
        P(("fsdp", "rep"), None, None),
        P(("fsdp", "rep")),
        P(("fsdp", "rep")),
        P("fsdp"),
        P("fsdp"),
        P("fsdp", None),
        P("fsdp", None),
        P("fsdp", None),
        P("fsdp", None),
        P("fsdp"),
        P("fsdp"),
        P("fsdp", None),
        P("fsdp", None),
        P("fsdp"),
        P("fsdp"),
        P("fsdp", None),
        P("fsdp", None),
        P(("fsdp", "rep"), None, None),
    )
    out_specs = (
        P(("fsdp", "rep"), None, None),
        P(("fsdp", "rep"), None, None),
        P("fsdp"),
        P("fsdp"),
        P("fsdp", None),
        P("fsdp", None),
        P("fsdp", None),
        P("fsdp", None),
        P("fsdp"),
        P("fsdp"),
        P("fsdp", None),
        P("fsdp", None),
        P("fsdp"),
        P("fsdp"),
        P("fsdp", None),
        P("fsdp", None),
    )
    return jax.shard_map(shards, mesh=mesh, in_specs=in_specs, out_specs=out_specs, check_vma=False)
```

```python
import functools

import jax
import jax.numpy as jnp
from jax import lax
from jax.experimental import pallas as pl
from jax.experimental.pallas import tpu as pltpu
from jax.sharding import PartitionSpec as P

D = 768
FRAME_TOK = 256
EPS = 1e-05
MESH = pl.DeviceIdType.MESH
VMEM_BYTES = 58 << 20

F32, BF16 = jnp.float32, jnp.bfloat16
NN = (((1,), (0,)), ((), ()))
NT = (((1,), (1,)), ((), ()))
TN = (((0,), (0,)), ((), ()))
def dg(a, b, dims): return lax.dot_general(a, b, dims, preferred_element_type=F32)

def head_sides(side, q2, k2, bias):
    lane = lax.broadcasted_iota(jnp.int32, (1, 128), 1)
    mine = (lane >= 64) if side else (lane < 64)
    extra = lane == (0 if side else 64)
    qa = jnp.where(mine, q2, jnp.where(extra, 1.0, 0.0).astype(BF16))
    ka = jnp.where(mine, k2, jnp.where(extra, bias, 0.0).astype(BF16))
    return qa, ka

def fwd_kernel(n_ref, q_ref, k_ref, v_ref, o_ref, l_ref, vt, ot, *, causal, bq, unit, at):
    T = q_ref.shape[0]; K = k_ref.shape[0]
    live = n_ref[0] * unit
    bias = jnp.where(lax.broadcasted_iota(jnp.int32, (K, 1), 0) < live, 0.0, -1e30).astype(F32)
    q2 = q_ref[...] * BF16(0.125)
    k2 = k_ref[...]
    vt[...] = v_ref[...].T
    for side in range(2):
        at(side)
        qa, ka = head_sides(side, q2, k2, bias)
        for j in range(T // bq):
            span = (j + 1) * bq if causal else K
            s = dg(ka[:span], qa[j * bq:(j + 1) * bq], NT)
            if causal:
                top = j * bq
                diag = s[top:]
                ok = lax.broadcasted_iota(jnp.int32, (bq, bq), 0) <= lax.broadcasted_iota(jnp.int32, (bq, bq), 1)
                diag = jnp.where(ok, diag, -1e30)
                s = diag if top == 0 else jnp.concatenate([s[:top], diag], 0)
            m = jnp.max(s, 0, keepdims=True)
            p = jnp.exp(s - m)
            l = jnp.sum(p, 0, keepdims=True)
            ot[side * 64:(side + 1) * 64, j * bq:(j + 1) * bq] = dg(vt[side * 64:(side + 1) * 64, :span], p.astype(BF16), NN) * (1.0 / l)
            l_ref[0, side:side + 1, j * bq:(j + 1) * bq] = m + jnp.log(l)
    o_ref[...] = ot[...].T.astype(BF16)


def bwd_kernel(n_ref, q_ref, k_ref, v_ref, o_ref, do_ref, l_ref, g_ref, kt, dqt, dka, dva, *, causal, bq, bk, unit, at):
    T = q_ref.shape[0]; K = k_ref.shape[0]
    live = n_ref[0] * unit
    bias = jnp.where(lax.broadcasted_iota(jnp.int32, (K, 1), 0) < live, 0.0, -1e30).astype(F32)
    q2 = q_ref[...] * BF16(0.125)
    k2 = k_ref[...]; v2 = v_ref[...]
    do2 = do_ref[...]
    kt[...] = k2.T
    prod = (do2.astype(F32) * o_ref[...].astype(F32)).T
    lane = lax.broadcasted_iota(jnp.int32, (1, 128), 1)
    for side in range(2):
        at(side)
        qa, ka = head_sides(side, q2, k2, bias)
        mine = (lane >= 64) if side else (lane < 64)
        va = jnp.where(mine, v2, BF16(0))
        delta = jnp.sum(prod[side * 64:(side + 1) * 64], 0, keepdims=True)
        lse = l_ref[0, side:side + 1, :]
        for i in range(K // bk):
            dk = dv = None
            kb, vb = ka[i * bk:(i + 1) * bk], va[i * bk:(i + 1) * bk]
            for j in range(T // bq):
                if causal and (j + 1) * bq <= i * bk: continue
                cols = slice(j * bq, (j + 1) * bq)
                s = dg(kb, qa[cols], NT)
                p = jnp.exp(s - lse[:, cols])
                if causal and j * bq < (i + 1) * bk:
                    ok = i * bk + lax.broadcasted_iota(jnp.int32, (bk, bq), 0) <= j * bq + lax.broadcasted_iota(jnp.int32, (bk, bq), 1)
                    p = jnp.where(ok, p, 0.0)
                dp = dg(vb, do2[cols], NT)
                ds = (p * (dp - delta[:, cols])).astype(BF16)
                a = dg(p.astype(BF16), do2[cols], NN)
                b = dg(ds, q2[cols], NN)
                dv = a if dv is None else dv + a
                dk = b if dk is None else dk + b
                c = dg(kt[side * 64:(side + 1) * 64, i * bk:(i + 1) * bk], ds, NN)
                if i == 0: dqt[side * 64:(side + 1) * 64, cols] = c
                else: dqt[side * 64:(side + 1) * 64, cols] += c
            rows = slice(i * bk, (i + 1) * bk)
            if side == 0:
                dka[rows] = dk; dva[rows] = dv
            else:
                g_ref[1, rows, :] = jnp.where(lane < 64, dka[rows], dk).astype(BF16)
                g_ref[2, rows, :] = jnp.where(lane < 64, dva[rows], dv).astype(BF16)
    g_ref[0] = (dqt[...] * 0.125).T.astype(BF16)


def grid_of(n):
    if n == 16:
        return 4, 2, 2
    if n == 64:
        return 4, 4, 4
    return n, 1, 1


def cut(shapes):
    out = []
    for i, (rows, cols) in enumerate(shapes):
        step = 256 if rows > cols // 8 and cols == 768 else min(cols, 768)
        out += [(i, c, step) for c in range(0, cols, step)]
    return out


def remote(src, dst, send, recv, dev):
    return pltpu.make_async_remote_copy(
        src_ref=src, dst_ref=dst, send_sem=send, recv_sem=recv, device_id=dev, device_id_type=MESH
    )


class Place:
    def __init__(self, dims):
        self.dims = dims
        self.size = dict(zip("zyx", dims))
        Z, Y, X = dims
        self.me = lax.axis_index("fsdp")
        self.core = lax.axis_index("rep")
        self.mine = {"z": self.me // (Y * X), "y": (self.me // X) % Y, "x": self.me % X}

    def peers(self, axis):
        mine, count = self.mine[axis], self.size[axis]
        out = []
        for k in range(1, count):
            at = dict(self.mine)
            at[axis] = (mine + k) % count
            dev = ((at["z"] * self.size["y"] + at["y"]) * self.size["x"] + at["x"], self.core)
            out.append((at[axis], (mine + count - k) % count, dev))
        return out

    def sibling(self):
        return (self.me, 1 - self.core)

    def greet(self):
        bar = pltpu.get_barrier_semaphore()
        devs = [d for axis in "zyx" for _, _, d in self.peers(axis)] + [self.sibling()]
        for d in devs:
            pl.semaphore_signal(bar, inc=1, device_id=d, device_id_type=MESH)
        pl.semaphore_wait(bar, len(devs))

    def by_core(self, action):
        @pl.when(self.core == 0)
        def _():
            action(0, "x", "y")

        @pl.when(self.core == 1)
        def _():
            action(1, "y", "x")


AHEAD = 3


class Gather:
    def __init__(self, shapes, n):
        self.dims = grid_of(n)
        self.pieces = cut(shapes)
        self.count = len(shapes)
        self.shapes = shapes
        self.steps = len(self.pieces) + 2

    def outs(self):
        return [jax.ShapeDtypeStruct(self.dims + tuple(s), BF16) for s in self.shapes]

    def scratch(self):
        Z, Y, X = self.dims
        M, z, s = len(self.pieces), max(self.dims[0] - 1, 1), max(Y - 1, X - 1, 1)
        sem = pltpu.SemaphoreType.DMA
        return [sem((2, self.count))] + [sem((M, c)) for c in (z, z, s, s, s, s, z, z, s, s, s, s)]

    def bind(self, shards, outs, scratch):
        self.shards, self.out = shards, outs
        self.own, *self.sem = scratch
        self.place = Place(self.dims)

    def half(self, m, side):
        _, c, w = self.pieces[m]
        return pl.ds(c + side * (w // 2), w // 2)

    def view(self, m, side, at):
        z, y, x = [slice(None) if at.get(k) is None else at[k] for k in "zyx"]
        return self.out[self.pieces[m][0]].at[z, y, x, :, self.half(m, side)]

    def hop(self, stage, m, side, axes, coming):
        a, b = axes
        mine = self.place.mine
        axis = ("z", a, b)[stage]
        out = []
        for k, (_, frm, dev) in enumerate(self.place.peers(axis)):
            at = dict(mine)
            for done in ("z", a)[:stage]:
                at[done] = None
            if coming:
                at[axis] = frm
            v = self.view(m, side, at)
            src = v
            if stage == 0 and not coming:
                src = self.shards[self.pieces[m][0]].at[:, self.half(m, side)]
            s, r = self.sem[2 * stage : 2 * stage + 2]
            out.append((at, lambda v=v, src=src, s=s, r=r, k=k, dev=dev: remote(src, v, s.at[m, k], r.at[m, k], dev)))
        return out

    def give(self, stage, m, side, at, k):
        v = self.view(m, side, at)
        s, r = self.sem[6 + 2 * stage : 8 + 2 * stage]
        return remote(v, v, s.at[m, k], r.at[m, k], self.place.sibling())

    def own_copies(self):
        p = self.place.mine
        return [
            remote(s, o.at[p["z"], p["y"], p["x"]], self.own.at[0, i], self.own.at[1, i], self.place.sibling())
            for i, (s, o) in enumerate(zip(self.shards, self.out))
        ]

    def begin(self):
        for c in self.own_copies():
            c.start()

        def go(core, a, b):
            for m in range(min(AHEAD, len(self.pieces))):
                for _, c in self.hop(0, m, core, (a, b), False):
                    c().start()

        self.place.by_core(go)

    def step(self, t):
        if t == 0:
            for c in self.own_copies():
                c.wait()

        def go(core, a, b):
            if t + AHEAD < len(self.pieces):
                for _, c in self.hop(0, t + AHEAD, core, (a, b), False):
                    c().start()
            for stage in range(3):
                m = t - stage
                if not 0 <= m < len(self.pieces):
                    continue
                came = self.hop(stage, m, core, (a, b), True)
                for _, c in came:
                    c().wait_recv()
                if stage < 2:
                    for _, c in self.hop(stage + 1, m, core, (a, b), False):
                        c().start()
                for k, (at, _) in enumerate(came):
                    self.give(stage, m, core, at, k).start()

        self.place.by_core(go)

    def arrive(self, pieces):
        def go(core, a, b):
            for m in pieces:
                for stage in range(3):
                    for k, (at, _) in enumerate(self.hop(stage, m, core, (b, a), True)):
                        self.give(stage, m, 1 - core, at, k).wait_recv()

        self.place.by_core(go)

    def sent(self):
        def go(core, a, b):
            for m in range(len(self.pieces)):
                for stage in range(3):
                    for _, c in self.hop(stage, m, core, (a, b), False):
                        c().wait_send()
                    for k, (at, _) in enumerate(self.hop(stage, m, core, (a, b), True)):
                        self.give(stage, m, core, at, k).wait_send()

        self.place.by_core(go)

    def end(self):
        self.arrive(range(len(self.pieces)))
        self.sent()


class Scatter:
    def __init__(self, shapes, targets, n, made=(), pieces=None):
        self.dims = grid_of(n)
        self.made = made
        self.count = len(shapes)
        self.pieces = [
            (i, c, w, targets[i][0], targets[i][1] + c) for i, c, w in pieces or cut(shapes)
        ]
        self.shapes, self.targets = shapes, targets
        self.steps = len(self.pieces) + 3

    def outs(self):
        width, rows = {}, {}
        for (r, w), (o, c) in zip(self.shapes, self.targets):
            width[o], rows[o] = max(width.get(o, 0), c + w), r
        return [jax.ShapeDtypeStruct((rows[o], width[o]), F32) for o in range(len(width))]

    def scratch(self):
        Z, Y, X = self.dims
        M, S = len(self.pieces), max(Y, X)
        one, z = max(S - 1, 1), max(Z - 1, 1)
        shape = [(self.shapes[i][0], w // 2) for i, _, w, _, _ in self.pieces]
        sem = pltpu.SemaphoreType.DMA
        lead = [(S, S, Z), (S, S, Z), (one, S, Z), (one, Z), (z,)]
        return (
            [[pltpu.VMEM(l + s, BF16) for s in shape] for l in lead]
            + [[pltpu.VMEM((2,) + s, F32) for s in shape]]
            + [sem((M, S * S))] * 3
            + [sem((M, one))] * 4
            + [sem((M, z))] * 2
            + [sem((M,))] * 2
        )

    def bind(self, grads, outs, scratch):
        self.grads, self.out = grads, outs
        self.acc, self.sib, self.got1, self.got2, self.got3, self.fin, self.lsem, *self.sem = scratch
        self.place = Place(self.dims)

    def meet(self, m, core):
        Z, Y, X = self.dims
        i, c, w, _, _ = self.pieces[m]
        for y in range(Y):
            for x in range(X):
                k = y * X + x
                take = [self.grads[i].at[:, y, x, :, pl.ds(c + s * (w // 2), w // 2)] for s in range(2)]
                at = [(y, x), (x, y)]
                if i not in self.made:
                    yield pltpu.make_async_copy(take[core], self.acc[m].at[at[core]], self.lsem.at[m, k])
                yield remote(
                    take[1 - core],
                    self.sib[m].at[at[1 - core]],
                    self.sem[0].at[m, k],
                    self.sem[1].at[m, k],
                    self.place.sibling(),
                )

    def hop(self, stage, m, axes):
        a, b = axes
        mine = self.place.mine
        s, r = self.sem[2 * stage : 2 * stage + 2]
        got = (None, self.got1, self.got2, self.got3)[stage]
        for k, (there, _, dev) in enumerate(self.place.peers((None, b, a, "z")[stage])):
            at = (mine[b], mine[a])[: stage - 1] + (there,)
            yield remote(self.acc[m].at[at], got[m].at[k], s.at[m, k], r.at[m, k], dev)

    def swap(self, m, side):
        v = self.fin[m].at[side]
        return remote(v, v, self.sem[8].at[m], self.sem[9].at[m], self.place.sibling())

    def add(self, dst, srcs):
        total = dst[...].astype(F32)
        for s in srcs:
            total = total + s[...].astype(F32)
        dst[...] = total.astype(BF16)

    def begin(self):
        def go(core, a, b):
            for m, piece in enumerate(self.pieces):
                if piece[0] not in self.made:
                    for c in self.meet(m, core):
                        c.start()

        self.place.by_core(go)

    def put(self, pieces):
        def go(core, a, b):
            Z, Y, X = self.dims
            for m in pieces:
                i, c, w, _, _ = self.pieces[m]
                for y in range(Y):
                    for x in range(X):
                        at = ((y, x), (x, y))[core]
                        half = self.grads[i][:, y, x, :, c + core * (w // 2) : c + (core + 1) * (w // 2)]
                        self.acc[m][at] = half
                for c in self.meet(m, core):
                    c.start()

        self.place.by_core(go)

    def step(self, t):
        self.act([(stage, t - stage) for stage in range(4) if 0 <= t - stage < len(self.pieces)])

    def act(self, pairs):
        def go(core, a, b):
            mine, size = self.place.mine, self.place.size
            for stage, m in pairs:
                acc = self.acc[m]
                if stage == 0:
                    for c in self.meet(m, core):
                        c.wait()
                    for j in range(size[b]):
                        self.add(acc.at[j, : size[a]], [self.sib[m].at[j, : size[a]]])
                else:
                    for c in self.hop(stage, m, (a, b)):
                        c.wait_recv()
                if stage == 1:
                    self.add(
                        acc.at[mine[b], : size[a]],
                        [self.got1[m].at[k, : size[a]] for k in range(size[b] - 1)],
                    )
                if stage == 2:
                    self.add(
                        acc.at[mine[b], mine[a]], [self.got2[m].at[k] for k in range(size[a] - 1)]
                    )
                if stage == 3:
                    total = acc[mine[b], mine[a], mine["z"]].astype(F32)
                    for k in range(size["z"] - 1):
                        total = total + self.got3[m][k].astype(F32)
                    self.fin[m][core] = total
                    self.swap(m, core).start()
                else:
                    for c in self.hop(stage + 1, m, (a, b)):
                        c.start()

        self.place.by_core(go)

    def end(self):
        def go(core, a, b):
            for m in range(len(self.pieces)):
                for stage in range(1, 4):
                    for c in self.hop(stage, m, (a, b)):
                        c.wait_send()
                self.swap(m, core).wait_send()
                self.swap(m, 1 - core).wait_recv()

        self.place.by_core(go)
        for m, (i, c, w, o, at) in enumerate(self.pieces):
            for side in range(2):
                self.out[o][:, at + side * (w // 2) : at + (side + 1) * (w // 2)] = self.fin[m][side]


def alone(engine, operands, cid, name):
    def kernel(*refs):
        count, outs = len(operands), len(engine.outs())
        engine.bind(refs[:count], refs[count : count + outs], refs[count + outs :])
        engine.place.greet()
        engine.begin()
        for t in range(engine.steps):
            engine.step(t)
        engine.end()

    space = pl.ANY if isinstance(engine, Gather) else pltpu.VMEM
    return pl.pallas_call(
        kernel,
        out_shape=engine.outs(),
        in_specs=[pl.BlockSpec(memory_space=pl.ANY)] * len(operands),
        out_specs=[pl.BlockSpec(memory_space=space)] * len(engine.outs()),
        scratch_shapes=engine.scratch(),
        compiler_params=pltpu.CompilerParams(
            collective_id=cid, has_side_effects=True, vmem_limit_bytes=VMEM_BYTES
        ),
        name=name,
    )(*operands)


class Beside:
    def __init__(self, engine, points):
        self.engine = engine
        self.points = points

    def reach(self, i, side):
        e = self.engine
        if side == 0:

            @pl.when(i == 0)
            def _():
                e.place.greet()
                e.begin()

        for t, p in enumerate(self.points):
            if p is not None and p % 2 == side:

                @pl.when(i == p // 2)
                def _(t=t):
                    e.step(t)

    def close(self, i):
        e = self.engine

        @pl.when(i == pl.num_programs(0) - 1)
        def _():
            for t, p in enumerate(self.points):
                if p is None:
                    e.step(t)
            e.end()


def paced(engine, first, each, unit, units=12):
    points = []
    for t in range(engine.steps):
        p = int(-(-(first + t * each) // unit))
        points.append(p if p < units else None)
    return points


def attend_beside(body, attn_in, in_specs, attn_out, out_specs, attn_scratch, engine, operands, points, cid, name):
    nin, nout, nscr = len(attn_in), len(attn_out), len(attn_scratch)
    moved, landed = len(operands), len(engine.outs())

    def kernel(*refs):
        at = 0
        groups = []
        for count in (nin, moved, nout, landed, nscr):
            groups.append(refs[at : at + count])
            at += count
        engine.bind(groups[1], groups[3], refs[at:])
        beside = Beside(engine, points)
        i = pl.program_id(0)
        body(*groups[0], *groups[2], *groups[4], at=lambda side: beside.reach(i, side))
        beside.close(i)

    any_ = pl.BlockSpec(memory_space=pl.ANY)
    space = pl.ANY if isinstance(engine, Gather) else pltpu.VMEM
    outs = pl.pallas_call(
        kernel,
        grid=(6,),
        in_specs=in_specs + [any_] * moved,
        out_specs=out_specs + [pl.BlockSpec(memory_space=space)] * landed,
        out_shape=attn_out + engine.outs(),
        scratch_shapes=attn_scratch + engine.scratch(),
        compiler_params=pltpu.CompilerParams(
            collective_id=cid, has_side_effects=True, vmem_limit_bytes=VMEM_BYTES
        ),
        name=name,
    )(*attn_in, *operands)
    return outs[:nout], outs[nout:]


def attn_fwd(live, q, k, v, cols, causal, unit, bq, engine, operands, points, cid, name):
    T, K = q.shape[0], k.shape[0]
    qo, ko, vo = cols
    return attend_beside(
        functools.partial(fwd_kernel, causal=causal, bq=bq, unit=unit),
        [live, q, k, v],
        [
            pl.BlockSpec(memory_space=pltpu.SMEM),
            pl.BlockSpec((T, 128), lambda i: (0, i + qo)),
            pl.BlockSpec((K, 128), lambda i: (0, i + ko)),
            pl.BlockSpec((K, 128), lambda i: (0, i + vo)),
        ],
        [jax.ShapeDtypeStruct((T, D), BF16), jax.ShapeDtypeStruct((6, 2, T), F32)],
        [pl.BlockSpec((T, 128), lambda i: (0, i)), pl.BlockSpec((1, 2, T), lambda i: (i, 0, 0))],
        [pltpu.VMEM((128, K), BF16), pltpu.VMEM((128, T), F32)],
        engine,
        operands,
        points,
        cid,
        name,
    )


def attn_bwd(live, q, k, v, o, do, lse, cols, causal, unit, bq, bk, engine, operands, points, cid, name):
    T, K = q.shape[0], k.shape[0]
    qo, ko, vo = cols
    return attend_beside(
        functools.partial(bwd_kernel, causal=causal, bq=bq, bk=bk, unit=unit),
        [live, q, k, v, o, do, lse],
        [
            pl.BlockSpec(memory_space=pltpu.SMEM),
            pl.BlockSpec((T, 128), lambda i: (0, i + qo)),
            pl.BlockSpec((K, 128), lambda i: (0, i + ko)),
            pl.BlockSpec((K, 128), lambda i: (0, i + vo)),
            pl.BlockSpec((T, 128), lambda i: (0, i)),
            pl.BlockSpec((T, 128), lambda i: (0, i)),
            pl.BlockSpec((1, 2, T), lambda i: (i, 0, 0)),
        ],
        [jax.ShapeDtypeStruct((3, T, D), BF16)],
        [pl.BlockSpec((3, T, 128), lambda i: (0, 0, i))],
        [
            pltpu.VMEM((128, K), BF16),
            pltpu.VMEM((128, T), F32),
            pltpu.VMEM((K, 128), F32),
            pltpu.VMEM((K, 128), F32),
        ],
        engine,
        operands,
        points,
        cid,
        name,
    )


def finish(sums, scale):
    def kernel(*refs):
        for i, o in zip(refs[: len(sums)], refs[len(sums) :]):
            o[...] = i[...] * scale

    return pl.pallas_call(
        kernel, out_shape=[jax.ShapeDtypeStruct(s.shape, F32) for s in sums], name="finish"
    )(*sums)


def moments(values):
    average = jnp.mean(values, -1, keepdims=True)
    centred = values - average
    variance = jnp.mean(centred * centred, -1, keepdims=True)
    inverse = lax.rsqrt(variance + EPS)
    return centred * inverse, inverse


def norm_back(normal, inverse, gain, grad):
    m = grad * gain
    back = inverse * (
        m - jnp.mean(m, -1, keepdims=True) - normal * jnp.mean(m * normal, -1, keepdims=True)
    )
    return back, jnp.sum(grad * normal, 0), jnp.sum(grad, 0)


GELU_A = 0.7978845608028654
GELU_B = 0.044715


def gelu(u):
    return 0.5 * u * (1.0 + jnp.tanh(GELU_A * (u + GELU_B * u * u * u)))


def gelu_slope(u):
    t = jnp.tanh(GELU_A * (u + GELU_B * u * u * u))
    return 0.5 * (1.0 + t) + 0.5 * u * (1.0 - t * t) * (GELU_A * (1.0 + 3.0 * GELU_B * u * u))


def blocks(rows, step, body):
    def go(r, _):
        body(pl.ds(pl.multiple_of(r * step, step), step))
        return 0

    lax.fori_loop(0, rows // step, go, 0)


def pair(ref, i, first=0):
    return ref.at[:, pl.ds(pl.multiple_of(first + i * 128, 128), 128)]


def norm_rows(packed):
    count = packed.shape[0]
    own = D // count
    total = None
    for j in range(count):
        r = lax.broadcasted_iota(jnp.int32, (128, D), 0)
        c = lax.broadcasted_iota(jnp.int32, (128, D), 1)
        spot = jnp.where((c == r + own * j) & (r < own), 1.0, 0.0).astype(BF16)
        part = dg(packed[j, :, :128], spot, NN)
        total = part if total is None else total + part
    return total


def forward_kernel(eng, ticks_cross, ticks_causal, *refs):
    it = iter(refs)

    def take(count):
        return [next(it) for _ in range(count)]

    clip, frames, tok_in, ctx_in = take(4)
    shards = take(eng.count)
    whole = take(eng.count)
    q1_o, k1_o, v1_o, o1_o, h1_o, x1_o, h2_o, qkv_o, o2_o, x2_o, h3_o, lse1_o, lse2_o, norms_o = take(14)
    tok, ctx, q1, k1, v1, o1, h1, x1, h2, qkv, o2, x2, h3, lse1, lse2, norms = take(16)
    packed, wa, wb, wqkv, vt, ot, isem, wsem, osem = take(9)
    eng.bind(shards, whole, list(it))
    T = tok.shape[0]
    eng.place.greet()
    eng.begin()
    loads = [pltpu.make_async_copy(ctx_in, ctx, isem.at[0]), pltpu.make_async_copy(tok_in, tok, isem.at[1])]
    for c in loads:
        c.start()
    saves = []

    def save(ref, out):
        c = pltpu.make_async_copy(ref, out, osem.at[len(saves)])
        c.start()
        saves.append(c)

    def fetch(i, pieces, ref):
        eng.arrive(pieces)
        c = pltpu.make_async_copy(whole[i], ref, wsem)
        c.start()
        c.wait()

    def matrix(ref, c=0):
        return ref[:, :, :, :, c : c + D].reshape(D, D)

    for t in range(3):
        eng.step(t)
    fetch(0, [0], wa)
    loads[0].wait()

    def keys(r):
        k1[r] = dg(ctx[r], matrix(wa), NN).astype(BF16)

    blocks(T, 256, keys)
    save(k1, k1_o)
    eng.step(3)
    fetch(1, [1], wb)

    def values(r):
        v1[r] = dg(ctx[r], matrix(wb), NN).astype(BF16)

    blocks(T, 256, values)
    save(v1, v1_o)
    eng.step(4)
    fetch(2, [2], packed)
    norms[...] = norm_rows(packed[...].reshape((-1,) + packed.shape[3:]))
    save(norms, norms_o)
    loads[1].wait()

    def first_norm(r):
        normal, _ = moments(tok[r].astype(F32))
        h1[r] = (normal * norms[0:1] + norms[1:2]).astype(BF16)

    blocks(T, 128, first_norm)
    save(h1, h1_o)
    eng.step(5)
    fetch(3, [3], wa)

    def queries(r):
        q1[r] = dg(h1[r], matrix(wa), NN).astype(BF16)

    blocks(T, 256, queries)
    save(q1, q1_o)

    def heads(ticks, body):
        def go(i, _):
            def at(side):
                for t, p in ticks:
                    if p % 2 == side:
                        pl.when(i == p // 2)(functools.partial(eng.step, t))

            body(i, at)
            return 0

        lax.fori_loop(0, 6, go, 0)

    heads(
        ticks_cross,
        lambda i, at: fwd_kernel(
            frames, pair(q1, i), pair(k1, i), pair(v1, i), pair(o1, i), lse1.at[pl.ds(i, 1)], vt, ot,
            causal=False, bq=512, unit=FRAME_TOK, at=at,
        ),
    )
    save(o1, o1_o)
    save(lse1, lse1_o)
    fetch(4, [4], wb)
    fetch(5, [5, 6, 7], wqkv)

    def middle(r):
        x = tok[r].astype(F32) + dg(o1[r], matrix(wb), NN)
        x1[r] = x
        normal, _ = moments(x)
        h2[r] = (normal * norms[2:3] + norms[3:4]).astype(BF16)
        for c in range(3):
            qkv[r, c * D : (c + 1) * D] = dg(h2[r], matrix(wqkv, c * D), NN).astype(BF16)

    blocks(T, 256, middle)
    for ref, out in ((x1, x1_o), (h2, h2_o), (qkv, qkv_o)):
        save(ref, out)
    heads(
        ticks_causal,
        lambda i, at: fwd_kernel(
            clip, pair(qkv, i), pair(qkv, i, D), pair(qkv, i, 2 * D), pair(o2, i), lse2.at[pl.ds(i, 1)], vt, ot,
            causal=True, bq=512, unit=1, at=at,
        ),
    )
    save(o2, o2_o)
    save(lse2, lse2_o)
    fetch(6, [8], wa)

    def late(r):
        x = x1[r] + dg(o2[r], matrix(wa), NN)
        x2[r] = x
        normal, _ = moments(x)
        h3[r] = (normal * norms[4:5] + norms[5:6]).astype(BF16)

    blocks(T, 256, late)
    save(x2, x2_o)
    save(h3, h3_o)
    taken = [t for t, _ in ticks_cross + ticks_causal]
    for t in range(6, eng.steps):
        if t not in taken:
            eng.step(t)
    eng.arrive(range(9, len(eng.pieces)))
    eng.sent()
    for c in saves:
        c.wait()


def forward(clip, frames, tok, ctx, shards, n, cid):
    eng = Gather([s.shape for s in shards], n)
    T = tok.shape[0]
    wide = jax.ShapeDtypeStruct((T, D), BF16)
    full = jax.ShapeDtypeStruct((T, D), F32)
    lse = jax.ShapeDtypeStruct((6, 2, T), F32)
    kept = [wide] * 5 + [full, wide, jax.ShapeDtypeStruct((T, 3 * D), BF16), wide, full, wide, lse, lse]
    kept.append(jax.ShapeDtypeStruct((16, D), F32))
    own = shards[0].shape[0]
    square = pltpu.VMEM(eng.dims + (own, D), BF16)
    any_ = pl.BlockSpec(memory_space=pl.ANY)
    smem = pl.BlockSpec(memory_space=pltpu.SMEM)
    sem = pltpu.SemaphoreType.DMA
    ticks_cross = [(6 + k, 2 * k + 1) for k in range(6)]
    ticks_causal = [(12 + k, 3 * k) for k in range(4)]
    outs = pl.pallas_call(
        functools.partial(forward_kernel, eng, ticks_cross, ticks_causal),
        out_shape=eng.outs() + kept,
        in_specs=[smem, smem] + [any_] * (2 + eng.count),
        out_specs=[any_] * (eng.count + len(kept)),
        scratch_shapes=[pltpu.VMEM((T, D), BF16)] * 2
        + [pltpu.VMEM(kept[i].shape, kept[i].dtype) for i in (0, 1, 2, 3, 4, 5, 6, 7, 8, 9, 10, 11, 12, 13)]
        + [pltpu.VMEM(eng.dims + shards[2].shape, BF16), square, square]
        + [pltpu.VMEM(eng.dims + (own, 3 * D), BF16), pltpu.VMEM((128, T), BF16), pltpu.VMEM((128, T), F32)]
        + [sem((2,)), sem, sem((16,))]
        + eng.scratch(),
        compiler_params=pltpu.CompilerParams(
            collective_id=cid, has_side_effects=True, vmem_limit_bytes=VMEM_BYTES
        ),
        name="forward",
    )(clip, frames, tok, ctx, *shards)
    return outs[: eng.count], outs[eng.count :]


def back_norm(values, gain, grad):
    normal, inverse = moments(values)
    m = grad * gain
    back = inverse * (
        m - jnp.mean(m, -1, keepdims=True) - normal * jnp.mean(m * normal, -1, keepdims=True)
    )
    return back, jnp.sum(grad * normal, 0, keepdims=True), jnp.sum(grad, 0, keepdims=True)


def mlp_kernel(clip, norms, x2, h3, cot, w_up, w_down, out, dx2, g_up, g_down, g_norm, dz, acc, dh, hid, dup):
    j = pl.program_id(0)
    T = x2.shape[0]

    def live(r):
        at = r.start + lax.broadcasted_iota(jnp.int32, (r.size, 1), 0)
        return at < clip[0]

    @pl.when(j == 0)
    def _():
        def first(r):
            dz[r] = jnp.where(live(r), cot[r], BF16(0))

        blocks(T, 256, first)

    up_w, down_w = w_up[...], w_down[...]

    def forth(r):
        u = dg(h3[r], up_w, NN)
        inner = u * (GELU_A + (GELU_A * GELU_B) * (u * u))
        t = jnp.tanh(inner)
        half = 0.5 + 0.5 * t
        hid[r] = (u * half).astype(BF16)
        slope = half + (0.5 * u) * (1.0 - t * t) * (GELU_A + (3.0 * GELU_A * GELU_B) * (u * u))
        dup[r] = (dg(dz[r], down_w, NT) * slope).astype(BF16)
        a = dg(hid[r], down_w, NN)
        b = dg(dup[r], up_w, NT)

        @pl.when(j == 0)
        def _():
            acc[r] = a
            dh[r] = b

        @pl.when(j > 0)
        def _():
            acc[r] += a
            dh[r] += b

    blocks(T, 256, forth)
    g_up[...] = dg(h3[...], dup[...], TN).astype(BF16)
    g_down[...] = dg(hid[...], dz[...], TN).astype(BF16)

    @pl.when(j == pl.num_programs(0) - 1)
    def _():
        g_norm[...] = jnp.zeros_like(g_norm)

        def last(r):
            x = x2[r]
            out[r] = jnp.where(live(r), x + acc[r], 0.0).astype(BF16)
            back, gain, bias = back_norm(x, norms[4:5], dh[r])
            dx2[r] = jnp.where(live(r), cot[r].astype(F32), 0.0) + back
            g_norm[0:1] += gain
            g_norm[1:2] += bias

        blocks(T, 128, last)


def mlp(clip, norms, x2, h3, cot, w_up, w_down, step=768):
    T = x2.shape[0]
    FF = w_up.shape[1]

    def still(shape):
        return pl.BlockSpec(shape, lambda j: (0, 0))

    return pl.pallas_call(
        mlp_kernel,
        grid=(FF // step,),
        in_specs=[
            pl.BlockSpec(memory_space=pltpu.SMEM),
            still(norms.shape),
            still((T, D)),
            still((T, D)),
            still((T, D)),
            pl.BlockSpec((D, step), lambda j: (0, j)),
            pl.BlockSpec((step, D), lambda j: (j, 0)),
        ],
        out_specs=[
            still((T, D)),
            still((T, D)),
            pl.BlockSpec((D, step), lambda j: (0, j)),
            pl.BlockSpec((step, D), lambda j: (j, 0)),
            still((8, D)),
        ],
        out_shape=[
            jax.ShapeDtypeStruct((T, D), BF16),
            jax.ShapeDtypeStruct((T, D), F32),
            jax.ShapeDtypeStruct((D, FF), BF16),
            jax.ShapeDtypeStruct((FF, D), BF16),
            jax.ShapeDtypeStruct((8, D), F32),
        ],
        scratch_shapes=[
            pltpu.VMEM((T, D), BF16),
            pltpu.VMEM((T, D), F32),
            pltpu.VMEM((T, D), F32),
            pltpu.VMEM((T, step), BF16),
            pltpu.VMEM((T, step), BF16),
        ],
        compiler_params=pltpu.CompilerParams(vmem_limit_bytes=VMEM_BYTES),
        name="mlp",
    )(clip, norms, x2, h3, cot, w_up, w_down)


def spots(j, own):
    r = lax.broadcasted_iota(jnp.int32, (128, D), 0)
    c = lax.broadcasted_iota(jnp.int32, (128, D), 1)
    return jnp.where((c == r + own * j) & (r < own), 1.0, 0.0).astype(BF16)


def load_all(sems, pairs):
    copies = [pltpu.make_async_copy(s, d, sems.at[k]) for k, (s, d) in enumerate(pairs)]
    for c in copies:
        c.start()
    return copies


def square(ref, c=0):
    return ref[:, :, :, :, c : c + D].reshape(D, D)


def causal_kernel(eng, *refs):
    it = iter(refs)

    def take(count):
        return [next(it) for _ in range(count)]

    clip, dx2_in, x1_in, qkv_in, o2_in, h2_in, lse, norms, wp_in, wqkv_in = take(10)
    grads = take(eng.count)
    sums = take(len(eng.outs()))
    dx1_o, gp_o, gqkv_o, gnorm = take(4)
    dx, x1, qkv, o2, h2, wp, wqkv, dy, do, dqkv, gp, gqkv, kt, dqt, dka, dva, isem, osem = take(18)
    eng.bind(grads, sums, list(it))
    T = dx.shape[0]
    eng.place.greet()
    eng.begin()
    loads = load_all(
        isem,
        [(dx2_in, dx), (wp_in, wp), (o2_in, o2), (qkv_in, qkv), (x1_in, x1), (h2_in, h2), (wqkv_in, wqkv)],
    )
    loads[0].wait()
    loads[1].wait()

    def first(r):
        dy[r] = dx[r].astype(BF16)
        do[r] = dg(dy[r], square(wp), NT).astype(BF16)

    blocks(T, 256, first)
    eng.step(0)
    loads[2].wait()

    def weight(left, right, out, c, step=256):
        def go(k, _):
            at = pl.multiple_of(k * step, step)
            g = dg(left[...], right[:, pl.ds(at, step)], TN).astype(BF16)
            out[:, :, :, :, pl.ds(c + at, step)] = g.reshape(out.shape[:4] + (step,))
            return 0

        lax.fori_loop(0, D // step, go, 0)

    weight(o2, dy, gp, 0)
    saves = [pltpu.make_async_copy(gp, gp_o, osem.at[0])]
    saves[0].start()
    eng.step(1)
    loads[3].wait()
    ticks = [(t, 1 + 2 * (t - 2)) for t in range(2, 8)]

    def heads(i, _):
        def at(side):
            for t, p in ticks:
                if p % 2 == side:
                    pl.when(i == p // 2)(functools.partial(eng.step, t))

        cols = pl.ds(pl.multiple_of(i * 128, 128), 128)
        bwd_kernel(
            clip, pair(qkv, i), pair(qkv, i, D), pair(qkv, i, 2 * D), pair(o2, i), pair(do, i),
            lse.at[pl.ds(i, 1)], dqkv.at[:, :, cols], kt, dqt, dka, dva,
            causal=True, bq=256, bk=512, unit=1, at=at,
        )
        return 0

    lax.fori_loop(0, 6, heads, 0)
    for c in loads[4:]:
        c.wait()
    gnorm[...] = jnp.zeros_like(gnorm)

    def back(r):
        dh = sum(dg(dqkv[c, r], square(wqkv, c * D), NT) for c in range(3))
        g, gain, bias = back_norm(x1[r], norms[2:3], dh)
        dx[r] += g
        gnorm[0:1] += gain
        gnorm[1:2] += bias

    blocks(T, 256, back)
    saves.append(pltpu.make_async_copy(dx, dx1_o, osem.at[1]))
    saves[1].start()
    eng.step(8)
    for c in range(3):
        weight(h2, dqkv.at[c], gqkv, c * D)
    saves.append(pltpu.make_async_copy(gqkv, gqkv_o, osem.at[2]))
    saves[2].start()
    for t in range(9, eng.steps):
        eng.step(t)
    eng.end()
    for c in saves:
        c.wait()


def causal_back(clip, dx2, x1, qkv, o2, h2, lse, norms, wp, wqkv, grads, targets, n, cid):
    eng = Scatter([a.shape[3:] for a in grads], targets, n)
    T = dx2.shape[0]
    own = wp.shape[3]
    any_ = pl.BlockSpec(memory_space=pl.ANY)
    smem = pl.BlockSpec(memory_space=pltpu.SMEM)
    vmem = pl.BlockSpec(memory_space=pltpu.VMEM)
    sem = pltpu.SemaphoreType.DMA
    small = jax.ShapeDtypeStruct((8, D), F32)
    one, three = eng.dims + (own, D), eng.dims + (own, 3 * D)

    def vm(shape, dtype=BF16):
        return pltpu.VMEM(shape, dtype)

    sums = eng.outs()
    outs = pl.pallas_call(
        functools.partial(causal_kernel, eng),
        out_shape=sums
        + [jax.ShapeDtypeStruct((T, D), F32), jax.ShapeDtypeStruct(one, BF16), jax.ShapeDtypeStruct(three, BF16), small],
        in_specs=[smem] + [any_] * 5 + [vmem] * 2 + [any_] * (2 + eng.count),
        out_specs=[vmem] * len(sums) + [any_] * 3 + [vmem],
        scratch_shapes=[
            vm((T, D), F32),
            vm((T, D), F32),
            vm((T, 3 * D)),
            vm((T, D)),
            vm((T, D)),
            vm(one),
            vm(three),
            vm((T, D)),
            vm((T, D)),
            vm((3, T, D)),
            vm(one),
            vm(three),
            vm((128, T)),
            vm((128, T), F32),
            vm((T, 128), F32),
            vm((T, 128), F32),
            sem((7,)),
            sem((3,)),
        ]
        + eng.scratch(),
        compiler_params=pltpu.CompilerParams(
            collective_id=cid, has_side_effects=True, vmem_limit_bytes=VMEM_BYTES
        ),
        name="causal_back",
    )(clip, dx2, x1, qkv, o2, h2, lse, norms, wp, wqkv, *grads)
    return outs[: len(sums)], outs[len(sums) :]


def cross_kernel(eng, *refs):
    it = iter(refs)

    def take(count):
        return [next(it) for _ in range(count)]

    frames, dx1_in, tok_in, ctx_in, q1_in, k1_in, v1_in, o1_in, h1_in, lse, norms, gnorm2, gnorm3, wo_in, wq_in = take(15)
    given = take(2)
    sums = take(len(eng.outs()))
    (grad_o,) = take(1)
    dx, tok, ctx, q1, k1, v1, o1, h1, wo, wq, dy, do, dqkv, kt, dqt, dka, dva, gsum, isem, osem = take(20)
    go_, gv, gk, gq, gn = take(5)
    eng.bind(list(given) + [go_, gv, gk, gq, gn], sums, list(it))
    T = dx.shape[0]
    n = gn.shape[0] * gn.shape[1] * gn.shape[2]
    own = D // n
    eng.place.greet()
    eng.begin()
    loads = load_all(
        isem,
        [(dx1_in, dx), (wo_in, wo), (o1_in, o1), (q1_in, q1), (k1_in, k1), (v1_in, v1), (h1_in, h1), (ctx_in, ctx),
         (wq_in, wq), (tok_in, tok)],
    )
    loads[0].wait()
    loads[1].wait()

    def first(r):
        dy[r] = dx[r].astype(BF16)
        do[r] = dg(dy[r], square(wo), NT).astype(BF16)

    blocks(T, 256, first)
    loads[2].wait()

    def weight(left, right, out, at, width=256):
        g = dg(left[...], right[:, pl.ds(at, width)], TN).astype(BF16)
        out[:, :, :, :, pl.ds(at, width)] = g.reshape(out.shape[:4] + (width,))

    def whole(k, _):
        weight(o1, dy, go_, pl.multiple_of(k * 256, 256))
        return 0

    lax.fori_loop(0, 3, whole, 0)
    eng.put([4])
    for c in loads[3:]:
        c.wait()
    third = [[5 + g, 8 + g, 11 + g] for g in range(3)]
    early = [[(s, t - s) for s in range(4) if 0 <= t - s < 5] for t in range(8)]
    plan = {}
    for t, u in enumerate((1, 2, 4, 5, 6, 8, 9, 10)):
        plan.setdefault(u, []).extend(early[t])
    for s, u in enumerate((5, 7, 8, 9)):
        plan.setdefault(u, []).extend((s, m) for m in third[0])
    for s, u in enumerate((9, 11)):
        plan.setdefault(u, []).extend((s, m) for m in third[1])

    def heads(i, _):
        def at(side):
            for u, acts in plan.items():
                if u % 2 == side:
                    pl.when(i == u // 2)(functools.partial(eng.act, acts))

        cols = pl.ds(pl.multiple_of(i * 128, 128), 128)
        bwd_kernel(
            frames, pair(q1, i), pair(k1, i), pair(v1, i), pair(o1, i), pair(do, i),
            lse.at[pl.ds(i, 1)], dqkv.at[:, :, cols], kt, dqt, dka, dva,
            causal=False, bq=1024, bk=256, unit=FRAME_TOK, at=at,
        )

        @pl.when(i % 2 == 1)
        def _():
            c = pl.multiple_of((i // 2) * 256, 256)
            weight(ctx, dqkv.at[2], gv, c)
            weight(ctx, dqkv.at[1], gk, c)
            weight(h1, dqkv.at[0], gq, c)

        for g in range(3):
            pl.when(i == 2 * g + 1)(functools.partial(eng.put, third[g]))
        return 0

    lax.fori_loop(0, 6, heads, 0)
    gsum[...] = jnp.zeros_like(gsum)
    gsum[2:4] = gnorm2[0:2]
    gsum[4:6] = gnorm3[0:2]
    eng.act([(2, m) for m in third[1]] + [(0, m) for m in third[2]])

    def back(r):
        dh = dg(dqkv[0, r], square(wq), NT)
        g, gain, bias = back_norm(tok[r].astype(F32), norms[0:1], dh)
        dx[r] += g
        gsum[0:1] += gain
        gsum[1:2] += bias

    blocks(T, 256, back)
    save = pltpu.make_async_copy(dx, grad_o, osem)
    save.start()
    eng.act([(3, m) for m in third[1]] + [(1, m) for m in third[2]])
    rows = gsum[...].astype(BF16)
    Z, Y, X = gn.shape[:3]
    for j in range(n):
        z, y, x = j // (Y * X), (j // X) % Y, j % X
        gn[z, y, x, :, :128] = dg(rows, spots(j, own), NT).astype(BF16)
        gn[z, y, x, :, 128:] = jnp.zeros((16, 128), BF16)
    eng.put([14])
    eng.act([(0, 14)])
    eng.act([(2, m) for m in third[2]] + [(1, 14)])
    eng.act([(3, m) for m in third[2]] + [(2, 14)])
    eng.act([(3, 14)])
    eng.end()
    save.wait()


def cross_back(frames, dx1, tok, ctx, q1, k1, v1, o1, h1, lse, norms, gnorm2, gnorm3, wo, wq, gp, gqkv, n, cid):
    own = wo.shape[3]
    one = gp.shape
    shapes = [gp.shape[3:], gqkv.shape[3:], one[3:], one[3:], one[3:], one[3:], (16, 256)]
    pieces = [(0, 0, D)] + [(1, c * D, D) for c in range(3)] + [(2, 0, D)]
    pieces += [(i, c * 256, 256) for i in (3, 4, 5) for c in range(3)] + [(6, 0, 256)]
    targets = [(6, 0), (5, 0), (4, 0), (3, 0), (2, 0), (1, 0), (0, 0)]
    eng = Scatter(shapes, targets, n, made=(2, 3, 4, 5, 6), pieces=pieces)
    T = dx1.shape[0]
    any_ = pl.BlockSpec(memory_space=pl.ANY)
    smem = pl.BlockSpec(memory_space=pltpu.SMEM)
    vmem = pl.BlockSpec(memory_space=pltpu.VMEM)
    sem = pltpu.SemaphoreType.DMA

    def vm(shape, dtype=BF16):
        return pltpu.VMEM(shape, dtype)

    sums = eng.outs()
    outs = pl.pallas_call(
        functools.partial(cross_kernel, eng),
        out_shape=sums + [jax.ShapeDtypeStruct((T, D), F32)],
        in_specs=[smem] + [any_] * 8 + [vmem] * 4 + [any_] * 4,
        out_specs=[vmem] * len(sums) + [any_],
        scratch_shapes=[vm((T, D), F32)]
        + [vm((T, D))] * 7
        + [vm(one)] * 2
        + [vm((T, D))] * 2
        + [vm((3, T, D)), vm((128, T)), vm((128, T), F32), vm((T, 128), F32), vm((T, 128), F32), vm((16, D), F32)]
        + [sem((10,)), sem]
        + [vm(one)] * 4
        + [vm(one[:3] + (16, 256))]
        + eng.scratch(),
        compiler_params=pltpu.CompilerParams(
            collective_id=cid, has_side_effects=True, vmem_limit_bytes=VMEM_BYTES
        ),
        name="cross_back",
    )(frames, dx1, tok, ctx, q1, k1, v1, o1, h1, lse, norms, gnorm2, gnorm3, wo, wq, gp, gqkv)
    return outs[: len(sums)], outs[len(sums)]


def shards(
    tokens,
    context,
    clip_lengths,
    context_frames,
    norm1_gain,
    norm1_bias,
    cross_q,
    cross_k,
    cross_v,
    cross_out,
    norm2_gain,
    norm2_bias,
    attn_qkv,
    attn_out,
    norm3_gain,
    norm3_bias,
    mlp_up,
    mlp_down,
    cotangent,
):
    n = lax.axis_size("fsdp")
    stream_in = tokens[0].astype(F32)
    context_rows = context[0]
    slot_rows = stream_in.shape[0]
    own = norm1_gain.shape[0]
    padding = (jnp.arange(slot_rows) < clip_lengths[0])[:, None]
    norms = jnp.stack([norm1_gain, norm1_bias, norm2_gain, norm2_bias, norm3_gain, norm3_bias])
    norms = jnp.pad(norms, ((0, 10), (0, 256 - own)))

    def flat(arrays):
        return [a.reshape(-1, a.shape[4]) for a in arrays]

    def gather(arrays):
        return Gather([a.shape for a in arrays], n), arrays

    def weight(left, right):
        g = dg(left, right, TN).astype(BF16)
        return g.reshape(n, -1, g.shape[1])

    def scatter(grads):
        arrays = [g.reshape(grid_of(n) + g.shape[1:]) for g, _ in grads]
        return Scatter([a.shape[3:] for a in arrays], [t for _, t in grads], n), arrays

    if own % 16 == 0:
        whole, kept = forward(
            clip_lengths,
            context_frames,
            tokens[0],
            context_rows,
            [cross_k, cross_v, norms, cross_q, cross_out, attn_qkv, attn_out, mlp_up, mlp_down],
            n,
            0,
        )
        _, _, _, w_q, w_o, w_qkv, w_p, w_up, w_down = whole
        q1, k1, v1, o1, h1, x1, h2, qkv, o2, x2, h3, lse1, lse2, norms = kept
        block_out, dx2, g_up, g_down, g_norm3 = mlp(
            clip_lengths, norms, x2, h3, cotangent[0], *flat([w_up, w_down])
        )
        grads = [g_down.reshape(w_down.shape), g_up.reshape(w_up.shape)]
        (s_up, s_down), (dx1, g_p, g_qkv, g_norm2) = causal_back(
            clip_lengths, dx2, x1, qkv, o2, h2, lse2, norms, w_p, w_qkv, grads, [(1, 0), (0, 0)], n, 1
        )
        (s_norms, s_q, s_k, s_v, s_o, s_qkv, s_p), input_grad = cross_back(
            context_frames, dx1, tokens[0], context_rows, q1, k1, v1, o1, h1, lse1, norms, g_norm2, g_norm3,
            w_o, w_q, g_p, g_qkv, n, 2
        )
    else:
        first, operands = gather([norms, cross_q, cross_k, cross_v])
        norms, *whole = alone(first, operands, 0, "gather_cross")
        w_q, w_k, w_v = flat(whole)
        norms = norms.reshape((n,) + norms.shape[3:])[:, :6, :own].transpose(1, 0, 2).reshape(6, D).astype(F32)
        gain_one, bias_one, gain_two, bias_two, gain_three, bias_three = [norms[i] for i in range(6)]

        normal_one, inverse_one = moments(stream_in)
        h1 = (normal_one * gain_one + bias_one).astype(BF16)
        q1 = dg(h1, w_q, NN).astype(BF16)
        k1 = dg(context_rows, w_k, NN).astype(BF16)
        v1 = dg(context_rows, w_v, NN).astype(BF16)
        second, operands = gather([cross_out, attn_qkv, attn_out])
        (o1, lse1), whole = attn_fwd(
            context_frames, q1, k1, v1, (0, 0, 0), False, FRAME_TOK, 512,
            second, operands, paced(second, 8.0, 4.8, 2.2), 1, "cross_fwd",
        )
        w_o, w_qkv, w_p = flat(whole)
        x1 = stream_in + dg(o1, w_o, NN)
        normal_two, inverse_two = moments(x1)
        h2 = (normal_two * gain_two + bias_two).astype(BF16)
        qkv = dg(h2, w_qkv, NN).astype(BF16)
        third, operands = gather([mlp_up, mlp_down])
        (o2, lse2), whole = attn_fwd(
            clip_lengths, qkv, qkv, qkv, (0, 6, 12), True, 1, 512,
            third, operands, paced(third, 8.0, 4.8, 1.5), 2, "causal_fwd",
        )
        w_up, w_down = flat(whole)
        x2 = x1 + dg(o2, w_p, NN)
        normal_three, inverse_three = moments(x2)
        h3 = (normal_three * gain_three + bias_three).astype(BF16)
        up = dg(h3, w_up, NN)
        hidden = gelu(up).astype(BF16)
        x3 = x2 + dg(hidden, w_down, NN)
        block_out = jnp.where(padding, x3, 0.0).astype(BF16)

        dx3 = jnp.where(padding, cotangent[0].astype(F32), 0.0)
        dz = dx3.astype(BF16)
        dup = (dg(dz, w_down, NT) * gelu_slope(up)).astype(BF16)
        back, g_gain3, g_bias3 = norm_back(normal_three, inverse_three, gain_three, dg(dup, w_up, NT))
        dx2 = dx3 + back
        dy2 = dx2.astype(BF16)
        do2 = dg(dy2, w_p, NT).astype(BF16)
        fourth, operands = scatter([(weight(hidden, dz), (1, 0)), (weight(h3, dup), (0, 0))])
        (dqkv,), (s_up, s_down) = attn_bwd(
            clip_lengths, qkv, qkv, qkv, o2, do2, lse2, (0, 6, 12), True, 1, 256, 512,
            fourth, operands, paced(fourth, 8.0, 4.8, 2.45), 3, "causal_bwd",
        )
        dh2 = sum(dg(dqkv[c], w_qkv[:, c * D : (c + 1) * D], NT) for c in range(3))
        back, g_gain2, g_bias2 = norm_back(normal_two, inverse_two, gain_two, dh2)
        dx1 = dx2 + back
        dy1 = dx1.astype(BF16)
        do1 = dg(dy1, w_o, NT).astype(BF16)
        fifth, operands = scatter(
            [(weight(o2, dy2), (0, 0))]
            + [(weight(h2, dqkv[c]), (1, c * D)) for c in range(3)]
            + [(weight(o1, dy1), (2, 0))]
        )
        (dqkv1,), (s_p, s_qkv, s_o) = attn_bwd(
            context_frames, q1, k1, v1, o1, do1, lse1, (0, 0, 0), False, FRAME_TOK, 1024, 256,
            fifth, operands, paced(fifth, 8.0, 4.8, 3.1), 4, "cross_bwd",
        )
        dh1 = dg(dqkv1[0], w_q, NT)
        back, g_gain1, g_bias1 = norm_back(normal_one, inverse_one, gain_one, dh1)
        input_grad = dx1 + back

        g_norms = jnp.stack([g_gain1, g_bias1, g_gain2, g_bias2, g_gain3, g_bias3]).astype(BF16)
        g_norms = jnp.pad(g_norms.reshape(6, n, own).transpose(1, 0, 2), ((0, 0), (0, 10), (0, 256 - own)))

        sixth, operands = scatter(
            [
                (weight(context_rows, dqkv1[2]), (3, 0)),
                (weight(context_rows, dqkv1[1]), (2, 0)),
                (weight(h1, dqkv1[0]), (1, 0)),
                (g_norms, (0, 0)),
            ]
        )
        s_norms, s_q, s_k, s_v = alone(sixth, operands, 5, "scatter_cross")
    scale = (slot_rows * tokens.shape[0] * n * lax.axis_size("rep")) ** (-0.5)
    vec = [s_norms[i, :own] * scale for i in range(6)]
    done = [None, *finish([s_q, s_k, s_v, s_o, s_qkv, s_p, s_up, s_down], scale)]
    return (
        block_out[None],
        input_grad[None],
        vec[0],
        vec[1],
        done[1],
        done[2],
        done[3],
        done[4],
        vec[2],
        vec[3],
        done[5],
        done[6],
        vec[4],
        vec[5],
        done[7],
        done[8],
    )


def solution(mesh):
    in_specs = (
        P(("fsdp", "rep"), None, None),
        P(("fsdp", "rep"), None, None),
        P(("fsdp", "rep")),
        P(("fsdp", "rep")),
        P("fsdp"),
        P("fsdp"),
        P("fsdp", None),
        P("fsdp", None),
        P("fsdp", None),
        P("fsdp", None),
        P("fsdp"),
        P("fsdp"),
        P("fsdp", None),
        P("fsdp", None),
        P("fsdp"),
        P("fsdp"),
        P("fsdp", None),
        P("fsdp", None),
        P(("fsdp", "rep"), None, None),
    )
    out_specs = (
        P(("fsdp", "rep"), None, None),
        P(("fsdp", "rep"), None, None),
        P("fsdp"),
        P("fsdp"),
        P("fsdp", None),
        P("fsdp", None),
        P("fsdp", None),
        P("fsdp", None),
        P("fsdp"),
        P("fsdp"),
        P("fsdp", None),
        P("fsdp", None),
        P("fsdp"),
        P("fsdp"),
        P("fsdp", None),
        P("fsdp", None),
    )
    return jax.shard_map(shards, mesh=mesh, in_specs=in_specs, out_specs=out_specs, check_vma=False)
```

```python
import functools

import jax
import jax.numpy as jnp
from jax import lax
from jax.experimental import pallas as pl
from jax.experimental.pallas import tpu as pltpu
from jax.sharding import PartitionSpec as P

D = 768
FRAME_TOK = 256
EPS = 1e-05
MESH = pl.DeviceIdType.MESH
VMEM_BYTES = 58 << 20

F32, BF16 = jnp.float32, jnp.bfloat16
NN = (((1,), (0,)), ((), ()))
NT = (((1,), (1,)), ((), ()))
TN = (((0,), (0,)), ((), ()))
def dg(a, b, dims): return lax.dot_general(a, b, dims, preferred_element_type=F32)

def head_sides(side, q2, k2, bias):
    lane = lax.broadcasted_iota(jnp.int32, (1, 128), 1)
    mine = (lane >= 64) if side else (lane < 64)
    extra = lane == (0 if side else 64)
    qa = jnp.where(mine, q2, jnp.where(extra, 1.0, 0.0).astype(BF16))
    ka = jnp.where(mine, k2, jnp.where(extra, bias, 0.0).astype(BF16))
    return qa, ka

def fwd_kernel(n_ref, q_ref, k_ref, v_ref, o_ref, l_ref, vt, ot, *, causal, bq, unit, at):
    T = q_ref.shape[0]; K = k_ref.shape[0]
    live = n_ref[0] * unit
    bias = jnp.where(lax.broadcasted_iota(jnp.int32, (K, 1), 0) < live, 0.0, -1e30).astype(F32)
    q2 = q_ref[...] * BF16(0.125)
    k2 = k_ref[...]
    vt[...] = v_ref[...].T
    for side in range(2):
        at(side)
        qa, ka = head_sides(side, q2, k2, bias)
        for j in range(T // bq):
            span = (j + 1) * bq if causal else K
            s = dg(ka[:span], qa[j * bq:(j + 1) * bq], NT)
            if causal:
                top = j * bq
                diag = s[top:]
                ok = lax.broadcasted_iota(jnp.int32, (bq, bq), 0) <= lax.broadcasted_iota(jnp.int32, (bq, bq), 1)
                diag = jnp.where(ok, diag, -1e30)
                s = diag if top == 0 else jnp.concatenate([s[:top], diag], 0)
            m = jnp.max(s, 0, keepdims=True)
            p = jnp.exp(s - m)
            l = jnp.sum(p, 0, keepdims=True)
            ot[side * 64:(side + 1) * 64, j * bq:(j + 1) * bq] = dg(vt[side * 64:(side + 1) * 64, :span], p.astype(BF16), NN) * (1.0 / l)
            l_ref[0, side:side + 1, j * bq:(j + 1) * bq] = m + jnp.log(l)
    o_ref[...] = ot[...].T.astype(BF16)


def bwd_kernel(n_ref, q_ref, k_ref, v_ref, o_ref, do_ref, l_ref, g_ref, kt, dqt, dka, dva, *, causal, bq, bk, unit, at):
    T = q_ref.shape[0]; K = k_ref.shape[0]
    live = n_ref[0] * unit
    bias = jnp.where(lax.broadcasted_iota(jnp.int32, (K, 1), 0) < live, 0.0, -1e30).astype(F32)
    q2 = q_ref[...] * BF16(0.125)
    k2 = k_ref[...]; v2 = v_ref[...]
    do2 = do_ref[...]
    kt[...] = k2.T
    prod = (do2.astype(F32) * o_ref[...].astype(F32)).T
    lane = lax.broadcasted_iota(jnp.int32, (1, 128), 1)
    for side in range(2):
        at(side)
        qa, ka = head_sides(side, q2, k2, bias)
        mine = (lane >= 64) if side else (lane < 64)
        va = jnp.where(mine, v2, BF16(0))
        delta = jnp.sum(prod[side * 64:(side + 1) * 64], 0, keepdims=True)
        lse = l_ref[0, side:side + 1, :]
        for i in range(K // bk):
            dk = dv = None
            kb, vb = ka[i * bk:(i + 1) * bk], va[i * bk:(i + 1) * bk]
            for j in range(T // bq):
                if causal and (j + 1) * bq <= i * bk: continue
                cols = slice(j * bq, (j + 1) * bq)
                s = dg(kb, qa[cols], NT)
                p = jnp.exp(s - lse[:, cols])
                if causal and j * bq < (i + 1) * bk:
                    ok = i * bk + lax.broadcasted_iota(jnp.int32, (bk, bq), 0) <= j * bq + lax.broadcasted_iota(jnp.int32, (bk, bq), 1)
                    p = jnp.where(ok, p, 0.0)
                dp = dg(vb, do2[cols], NT)
                ds = (p * (dp - delta[:, cols])).astype(BF16)
                a = dg(p.astype(BF16), do2[cols], NN)
                b = dg(ds, q2[cols], NN)
                dv = a if dv is None else dv + a
                dk = b if dk is None else dk + b
                c = dg(kt[side * 64:(side + 1) * 64, i * bk:(i + 1) * bk], ds, NN)
                if i == 0: dqt[side * 64:(side + 1) * 64, cols] = c
                else: dqt[side * 64:(side + 1) * 64, cols] += c
            rows = slice(i * bk, (i + 1) * bk)
            if side == 0:
                dka[rows] = dk; dva[rows] = dv
            else:
                g_ref[1, rows, :] = jnp.where(lane < 64, dka[rows], dk).astype(BF16)
                g_ref[2, rows, :] = jnp.where(lane < 64, dva[rows], dv).astype(BF16)
    g_ref[0] = (dqt[...] * 0.125).T.astype(BF16)


def grid_of(n):
    if n == 16:
        return 4, 2, 2
    if n == 64:
        return 4, 4, 4
    return n, 1, 1


def cut(shapes):
    out = []
    for i, (rows, cols) in enumerate(shapes):
        step = 256 if rows > cols // 8 and cols == 768 else min(cols, 768)
        out += [(i, c, step) for c in range(0, cols, step)]
    return out


def remote(src, dst, send, recv, dev):
    return pltpu.make_async_remote_copy(
        src_ref=src, dst_ref=dst, send_sem=send, recv_sem=recv, device_id=dev, device_id_type=MESH
    )


class Place:
    def __init__(self, dims):
        self.dims = dims
        self.size = dict(zip("zyx", dims))
        Z, Y, X = dims
        self.me = lax.axis_index("fsdp")
        self.core = lax.axis_index("rep")
        self.mine = {"z": self.me // (Y * X), "y": (self.me // X) % Y, "x": self.me % X}

    def peers(self, axis):
        mine, count = self.mine[axis], self.size[axis]
        out = []
        for k in range(1, count):
            at = dict(self.mine)
            at[axis] = (mine + k) % count
            dev = ((at["z"] * self.size["y"] + at["y"]) * self.size["x"] + at["x"], self.core)
            out.append((at[axis], (mine + count - k) % count, dev))
        return out

    def sibling(self):
        return (self.me, 1 - self.core)

    def greet(self):
        bar = pltpu.get_barrier_semaphore()
        devs = [d for axis in "zyx" for _, _, d in self.peers(axis)] + [self.sibling()]
        for d in devs:
            pl.semaphore_signal(bar, inc=1, device_id=d, device_id_type=MESH)
        pl.semaphore_wait(bar, len(devs))

    def by_core(self, action):
        @pl.when(self.core == 0)
        def _():
            action(0, "x", "y")

        @pl.when(self.core == 1)
        def _():
            action(1, "y", "x")


AHEAD = 3


class Gather:
    def __init__(self, shapes, n):
        self.dims = grid_of(n)
        self.pieces = cut(shapes)
        self.count = len(shapes)
        self.shapes = shapes
        self.steps = len(self.pieces) + 2

    def outs(self):
        return [jax.ShapeDtypeStruct(self.dims + tuple(s), BF16) for s in self.shapes]

    def scratch(self):
        Z, Y, X = self.dims
        M, z, s = len(self.pieces), max(self.dims[0] - 1, 1), max(Y - 1, X - 1, 1)
        sem = pltpu.SemaphoreType.DMA
        return [sem((2, self.count))] + [sem((M, c)) for c in (z, z, s, s, s, s, z, z, s, s, s, s)]

    def bind(self, shards, outs, scratch):
        self.shards, self.out = shards, outs
        self.own, *self.sem = scratch
        self.place = Place(self.dims)

    def half(self, m, side):
        _, c, w = self.pieces[m]
        return pl.ds(c + side * (w // 2), w // 2)

    def view(self, m, side, at):
        z, y, x = [slice(None) if at.get(k) is None else at[k] for k in "zyx"]
        return self.out[self.pieces[m][0]].at[z, y, x, :, self.half(m, side)]

    def hop(self, stage, m, side, axes, coming):
        a, b = axes
        mine = self.place.mine
        axis = ("z", a, b)[stage]
        out = []
        for k, (_, frm, dev) in enumerate(self.place.peers(axis)):
            at = dict(mine)
            for done in ("z", a)[:stage]:
                at[done] = None
            if coming:
                at[axis] = frm
            v = self.view(m, side, at)
            src = v
            if stage == 0 and not coming:
                src = self.shards[self.pieces[m][0]].at[:, self.half(m, side)]
            s, r = self.sem[2 * stage : 2 * stage + 2]
            out.append((at, lambda v=v, src=src, s=s, r=r, k=k, dev=dev: remote(src, v, s.at[m, k], r.at[m, k], dev)))
        return out

    def give(self, stage, m, side, at, k):
        v = self.view(m, side, at)
        s, r = self.sem[6 + 2 * stage : 8 + 2 * stage]
        return remote(v, v, s.at[m, k], r.at[m, k], self.place.sibling())

    def own_copies(self):
        p = self.place.mine
        return [
            remote(s, o.at[p["z"], p["y"], p["x"]], self.own.at[0, i], self.own.at[1, i], self.place.sibling())
            for i, (s, o) in enumerate(zip(self.shards, self.out))
        ]

    def begin(self, ahead):
        for c in self.own_copies():
            c.start()
        self.leave(range(min(ahead, len(self.pieces))))

    def leave(self, pieces):
        def go(core, a, b):
            for m in pieces:
                for _, c in self.hop(0, m, core, (a, b), False):
                    c().start()

        self.place.by_core(go)

    def settle(self):
        for c in self.own_copies():
            c.wait()

    def act(self, pairs):
        def go(core, a, b):
            for stage, m in pairs:
                came = self.hop(stage, m, core, (a, b), True)
                for _, c in came:
                    c().wait_recv()
                if stage < 2:
                    for _, c in self.hop(stage + 1, m, core, (a, b), False):
                        c().start()
                for k, (at, _) in enumerate(came):
                    self.give(stage, m, core, at, k).start()

        self.place.by_core(go)

    def step(self, t):
        if t == 0:
            self.settle()
        if t + AHEAD < len(self.pieces):
            self.leave([t + AHEAD])
        self.act([(s, t - s) for s in range(3) if 0 <= t - s < len(self.pieces)])

    def arrive(self, pieces):
        def go(core, a, b):
            for m in pieces:
                for stage in range(3):
                    for k, (at, _) in enumerate(self.hop(stage, m, core, (b, a), True)):
                        self.give(stage, m, 1 - core, at, k).wait_recv()

        self.place.by_core(go)

    def sent(self):
        def go(core, a, b):
            for m in range(len(self.pieces)):
                for stage in range(3):
                    for _, c in self.hop(stage, m, core, (a, b), False):
                        c().wait_send()
                    for k, (at, _) in enumerate(self.hop(stage, m, core, (a, b), True)):
                        self.give(stage, m, core, at, k).wait_send()

        self.place.by_core(go)

    def end(self):
        self.arrive(range(len(self.pieces)))
        self.sent()


class Scatter:
    def __init__(self, shapes, targets, n, made=(), pieces=None):
        self.dims = grid_of(n)
        self.made = made
        self.count = len(shapes)
        self.pieces = [
            (i, c, w, targets[i][0], targets[i][1] + c) for i, c, w in pieces or cut(shapes)
        ]
        self.shapes, self.targets = shapes, targets
        self.steps = len(self.pieces) + 3

    def outs(self):
        width, rows = {}, {}
        for (r, w), (o, c) in zip(self.shapes, self.targets):
            width[o], rows[o] = max(width.get(o, 0), c + w), r
        return [jax.ShapeDtypeStruct((rows[o], width[o]), F32) for o in range(len(width))]

    def scratch(self):
        Z, Y, X = self.dims
        M, S = len(self.pieces), max(Y, X)
        one, z = max(S - 1, 1), max(Z - 1, 1)
        shape = [(self.shapes[i][0], w // 2) for i, _, w, _, _ in self.pieces]
        sem = pltpu.SemaphoreType.DMA
        lead = [(S, S, Z), (S, S, Z), (one, S, Z), (one, Z), (z,)]
        return (
            [[pltpu.VMEM(l + s, BF16) for s in shape] for l in lead]
            + [[pltpu.VMEM((2,) + s, F32) for s in shape]]
            + [sem((M, S * S))] * 3
            + [sem((M, one))] * 4
            + [sem((M, z))] * 2
            + [sem((M,))] * 2
        )

    def bind(self, grads, outs, scratch):
        self.grads, self.out = grads, outs
        self.acc, self.sib, self.got1, self.got2, self.got3, self.fin, self.lsem, *self.sem = scratch
        self.place = Place(self.dims)

    def meet(self, m, core):
        Z, Y, X = self.dims
        i, c, w, _, _ = self.pieces[m]
        for y in range(Y):
            for x in range(X):
                k = y * X + x
                take = [self.grads[i].at[:, y, x, :, pl.ds(c + s * (w // 2), w // 2)] for s in range(2)]
                at = [(y, x), (x, y)]
                if i not in self.made:
                    yield pltpu.make_async_copy(take[core], self.acc[m].at[at[core]], self.lsem.at[m, k])
                yield remote(
                    take[1 - core],
                    self.sib[m].at[at[1 - core]],
                    self.sem[0].at[m, k],
                    self.sem[1].at[m, k],
                    self.place.sibling(),
                )

    def hop(self, stage, m, axes):
        a, b = axes
        mine = self.place.mine
        s, r = self.sem[2 * stage : 2 * stage + 2]
        got = (None, self.got1, self.got2, self.got3)[stage]
        for k, (there, _, dev) in enumerate(self.place.peers((None, b, a, "z")[stage])):
            at = (mine[b], mine[a])[: stage - 1] + (there,)
            yield remote(self.acc[m].at[at], got[m].at[k], s.at[m, k], r.at[m, k], dev)

    def swap(self, m, side):
        v = self.fin[m].at[side]
        return remote(v, v, self.sem[8].at[m], self.sem[9].at[m], self.place.sibling())

    def add(self, dst, srcs):
        total = dst[...].astype(F32)
        for s in srcs:
            total = total + s[...].astype(F32)
        dst[...] = total.astype(BF16)

    def begin(self, ahead=0):
        def go(core, a, b):
            for m, piece in enumerate(self.pieces):
                if piece[0] not in self.made:
                    for c in self.meet(m, core):
                        c.start()

        self.place.by_core(go)

    def put(self, pieces):
        def go(core, a, b):
            Z, Y, X = self.dims
            for m in pieces:
                i, c, w, _, _ = self.pieces[m]
                for y in range(Y):
                    for x in range(X):
                        at = ((y, x), (x, y))[core]
                        half = self.grads[i][:, y, x, :, c + core * (w // 2) : c + (core + 1) * (w // 2)]
                        self.acc[m][at] = half
                for c in self.meet(m, core):
                    c.start()

        self.place.by_core(go)

    def step(self, t):
        self.act([(stage, t - stage) for stage in range(4) if 0 <= t - stage < len(self.pieces)])

    def act(self, pairs):
        def go(core, a, b):
            mine, size = self.place.mine, self.place.size
            for stage, m in pairs:
                acc = self.acc[m]
                if stage == 0:
                    for c in self.meet(m, core):
                        c.wait()
                    for j in range(size[b]):
                        self.add(acc.at[j, : size[a]], [self.sib[m].at[j, : size[a]]])
                else:
                    for c in self.hop(stage, m, (a, b)):
                        c.wait_recv()
                if stage == 1:
                    self.add(
                        acc.at[mine[b], : size[a]],
                        [self.got1[m].at[k, : size[a]] for k in range(size[b] - 1)],
                    )
                if stage == 2:
                    self.add(
                        acc.at[mine[b], mine[a]], [self.got2[m].at[k] for k in range(size[a] - 1)]
                    )
                if stage == 3:
                    total = acc[mine[b], mine[a], mine["z"]].astype(F32)
                    for k in range(size["z"] - 1):
                        total = total + self.got3[m][k].astype(F32)
                    self.fin[m][core] = total
                    self.swap(m, core).start()
                else:
                    for c in self.hop(stage + 1, m, (a, b)):
                        c.start()

        self.place.by_core(go)

    def end(self):
        def go(core, a, b):
            for m in range(len(self.pieces)):
                for stage in range(1, 4):
                    for c in self.hop(stage, m, (a, b)):
                        c.wait_send()
                self.swap(m, core).wait_send()
                self.swap(m, 1 - core).wait_recv()

        self.place.by_core(go)
        for m, (i, c, w, o, at) in enumerate(self.pieces):
            for side in range(2):
                self.out[o][:, at + side * (w // 2) : at + (side + 1) * (w // 2)] = self.fin[m][side]


class Pace:
    def __init__(self, actions):
        self.todo = sorted(actions, key=lambda a: a[0])
        self.at = {key: t for t, key, _ in actions}

    def until(self, t):
        out = [a[2] for a in self.todo if a[0] <= t]
        self.todo = [a for a in self.todo if a[0] > t]
        return out

    def run(self, t):
        for action in self.until(t):
            action()

    def units(self, start, step, count, gap=0.0, every=1):
        return [self.until(start + u * step + (u // every) * gap) for u in range(count)]

    @staticmethod
    def pick(plan, i, every=1, side=0):
        for u, actions in enumerate(plan):
            if actions and u % every == side:

                @pl.when(i == u // every)
                def _(actions=actions):
                    for action in actions:
                        action()


def alone(engine, operands, cid, name):
    def kernel(*refs):
        count, outs = len(operands), len(engine.outs())
        engine.bind(refs[:count], refs[count : count + outs], refs[count + outs :])
        engine.place.greet()
        engine.begin(AHEAD)
        for t in range(engine.steps):
            engine.step(t)
        engine.end()

    space = pl.ANY if isinstance(engine, Gather) else pltpu.VMEM
    return pl.pallas_call(
        kernel,
        out_shape=engine.outs(),
        in_specs=[pl.BlockSpec(memory_space=pl.ANY)] * len(operands),
        out_specs=[pl.BlockSpec(memory_space=space)] * len(engine.outs()),
        scratch_shapes=engine.scratch(),
        compiler_params=pltpu.CompilerParams(
            collective_id=cid, has_side_effects=True, vmem_limit_bytes=VMEM_BYTES
        ),
        name=name,
    )(*operands)


class Beside:
    def __init__(self, engine, points):
        self.engine = engine
        self.points = points

    def reach(self, i, side):
        e = self.engine
        if side == 0:

            @pl.when(i == 0)
            def _():
                e.place.greet()
                e.begin(AHEAD)

        for t, p in enumerate(self.points):
            if p is not None and p % 2 == side:

                @pl.when(i == p // 2)
                def _(t=t):
                    e.step(t)

    def close(self, i):
        e = self.engine

        @pl.when(i == pl.num_programs(0) - 1)
        def _():
            for t, p in enumerate(self.points):
                if p is None:
                    e.step(t)
            e.end()


def paced(engine, first, each, unit, units=12):
    points = []
    for t in range(engine.steps):
        p = int(-(-(first + t * each) // unit))
        points.append(p if p < units else None)
    return points


def attend_beside(body, attn_in, in_specs, attn_out, out_specs, attn_scratch, engine, operands, points, cid, name):
    nin, nout, nscr = len(attn_in), len(attn_out), len(attn_scratch)
    moved, landed = len(operands), len(engine.outs())

    def kernel(*refs):
        at = 0
        groups = []
        for count in (nin, moved, nout, landed, nscr):
            groups.append(refs[at : at + count])
            at += count
        engine.bind(groups[1], groups[3], refs[at:])
        beside = Beside(engine, points)
        i = pl.program_id(0)
        body(*groups[0], *groups[2], *groups[4], at=lambda side: beside.reach(i, side))
        beside.close(i)

    any_ = pl.BlockSpec(memory_space=pl.ANY)
    space = pl.ANY if isinstance(engine, Gather) else pltpu.VMEM
    outs = pl.pallas_call(
        kernel,
        grid=(6,),
        in_specs=in_specs + [any_] * moved,
        out_specs=out_specs + [pl.BlockSpec(memory_space=space)] * landed,
        out_shape=attn_out + engine.outs(),
        scratch_shapes=attn_scratch + engine.scratch(),
        compiler_params=pltpu.CompilerParams(
            collective_id=cid, has_side_effects=True, vmem_limit_bytes=VMEM_BYTES
        ),
        name=name,
    )(*attn_in, *operands)
    return outs[:nout], outs[nout:]


def attn_fwd(live, q, k, v, cols, causal, unit, bq, engine, operands, points, cid, name):
    T, K = q.shape[0], k.shape[0]
    qo, ko, vo = cols
    return attend_beside(
        functools.partial(fwd_kernel, causal=causal, bq=bq, unit=unit),
        [live, q, k, v],
        [
            pl.BlockSpec(memory_space=pltpu.SMEM),
            pl.BlockSpec((T, 128), lambda i: (0, i + qo)),
            pl.BlockSpec((K, 128), lambda i: (0, i + ko)),
            pl.BlockSpec((K, 128), lambda i: (0, i + vo)),
        ],
        [jax.ShapeDtypeStruct((T, D), BF16), jax.ShapeDtypeStruct((6, 2, T), F32)],
        [pl.BlockSpec((T, 128), lambda i: (0, i)), pl.BlockSpec((1, 2, T), lambda i: (i, 0, 0))],
        [pltpu.VMEM((128, K), BF16), pltpu.VMEM((128, T), F32)],
        engine,
        operands,
        points,
        cid,
        name,
    )


def attn_bwd(live, q, k, v, o, do, lse, cols, causal, unit, bq, bk, engine, operands, points, cid, name):
    T, K = q.shape[0], k.shape[0]
    qo, ko, vo = cols
    return attend_beside(
        functools.partial(bwd_kernel, causal=causal, bq=bq, bk=bk, unit=unit),
        [live, q, k, v, o, do, lse],
        [
            pl.BlockSpec(memory_space=pltpu.SMEM),
            pl.BlockSpec((T, 128), lambda i: (0, i + qo)),
            pl.BlockSpec((K, 128), lambda i: (0, i + ko)),
            pl.BlockSpec((K, 128), lambda i: (0, i + vo)),
            pl.BlockSpec((T, 128), lambda i: (0, i)),
            pl.BlockSpec((T, 128), lambda i: (0, i)),
            pl.BlockSpec((1, 2, T), lambda i: (i, 0, 0)),
        ],
        [jax.ShapeDtypeStruct((3, T, D), BF16)],
        [pl.BlockSpec((3, T, 128), lambda i: (0, 0, i))],
        [
            pltpu.VMEM((128, K), BF16),
            pltpu.VMEM((128, T), F32),
            pltpu.VMEM((K, 128), F32),
            pltpu.VMEM((K, 128), F32),
        ],
        engine,
        operands,
        points,
        cid,
        name,
    )


def finish(sums, scale):
    def kernel(*refs):
        for i, o in zip(refs[: len(sums)], refs[len(sums) :]):
            o[...] = i[...] * scale

    return pl.pallas_call(
        kernel, out_shape=[jax.ShapeDtypeStruct(s.shape, F32) for s in sums], name="finish"
    )(*sums)


def moments(values):
    average = jnp.mean(values, -1, keepdims=True)
    centred = values - average
    variance = jnp.mean(centred * centred, -1, keepdims=True)
    inverse = lax.rsqrt(variance + EPS)
    return centred * inverse, inverse


def norm_back(normal, inverse, gain, grad):
    m = grad * gain
    back = inverse * (
        m - jnp.mean(m, -1, keepdims=True) - normal * jnp.mean(m * normal, -1, keepdims=True)
    )
    return back, jnp.sum(grad * normal, 0), jnp.sum(grad, 0)


GELU_A = 0.7978845608028654
GELU_B = 0.044715


def gelu(u):
    return 0.5 * u * (1.0 + jnp.tanh(GELU_A * (u + GELU_B * u * u * u)))


def gelu_slope(u):
    t = jnp.tanh(GELU_A * (u + GELU_B * u * u * u))
    return 0.5 * (1.0 + t) + 0.5 * u * (1.0 - t * t) * (GELU_A * (1.0 + 3.0 * GELU_B * u * u))


def blocks(rows, step, body, plan=()):
    def go(r, _):
        Pace.pick(plan, r)
        body(pl.ds(pl.multiple_of(r * step, step), step))
        return 0

    lax.fori_loop(0, rows // step, go, 0)


def pair(ref, i, first=0):
    return ref.at[:, pl.ds(pl.multiple_of(first + i * 128, 128), 128)]


def norm_rows(packed):
    count = packed.shape[0]
    own = D // count
    total = None
    for j in range(count):
        r = lax.broadcasted_iota(jnp.int32, (128, D), 0)
        c = lax.broadcasted_iota(jnp.int32, (128, D), 1)
        spot = jnp.where((c == r + own * j) & (r < own), 1.0, 0.0).astype(BF16)
        part = dg(packed[j, :, :128], spot, NN)
        total = part if total is None else total + part
    return total


GATHER_AHEAD = 2
GATHER = dict(first=7.5, rate=3.8, hop=3.5, slack=2.0)


def gather_pace(eng):
    actions = []
    link = 0.0
    for m, (i, _, w) in enumerate(eng.pieces):
        rows = eng.shapes[i][0] * eng.dims[0] * eng.dims[1] * eng.dims[2]
        cost = GATHER["rate"] * rows * w * 2e-6
        slack = GATHER["slack"] if m > 3 else 0.0
        t = GATHER["first"] + link + cost / 2
        if m >= GATHER_AHEAD:
            actions.append((t - cost / 2 - 5.0, ("leave", m), functools.partial(eng.leave, [m])))
        for s, part in enumerate((0.0, 0.33, 0.67)):
            t += (part * cost + GATHER["hop"] + slack) if s else 0.0
            actions.append((t, (s, m), functools.partial(eng.act, [(s, m)])))
        link += cost
    first = min(t for t, key, _ in actions if key == (0, 0))
    actions.append((first - 1e-3, "own", eng.settle))
    pace = Pace(actions)
    return pace, lambda m: pace.at[(2, m)]


def forward_kernel(eng, *refs):
    it = iter(refs)

    def take(count):
        return [next(it) for _ in range(count)]

    clip, frames, tok_in, ctx_in = take(4)
    shards = take(eng.count)
    whole = take(eng.count)
    q1_o, k1_o, v1_o, o1_o, h1_o, x1_o, h2_o, qkv_o, o2_o, x2_o, h3_o, lse1_o, lse2_o, norms_o = take(14)
    tok, ctx, q1, k1, v1, o1, h1, x1, h2, qkv, o2, x2, h3, lse1, lse2, norms = take(16)
    packed, wa, wb, wqkv, vt, ot, isem, wsem, osem = take(9)
    eng.bind(shards, whole, list(it))
    T = tok.shape[0]
    eng.place.greet()
    eng.begin(GATHER_AHEAD)
    pace, ready = gather_pace(eng)
    loads = [pltpu.make_async_copy(ctx_in, ctx, isem.at[0]), pltpu.make_async_copy(tok_in, tok, isem.at[1])]
    for c in loads:
        c.start()
    saves = []

    def save(ref, out):
        c = pltpu.make_async_copy(ref, out, osem.at[len(saves)])
        c.start()
        saves.append(c)

    def fetch(i, pieces, ref):
        eng.arrive(pieces)
        c = pltpu.make_async_copy(whole[i], ref, wsem)
        c.start()
        c.wait()

    def matrix(ref, c=0):
        return ref[:, :, :, :, c : c + D].reshape(D, D)

    clock = ready(0)
    pace.run(clock)
    fetch(0, [0], wa)
    loads[0].wait()

    def keys(r):
        k1[r] = dg(ctx[r], matrix(wa), NN).astype(BF16)

    blocks(T, 256, keys)
    save(k1, k1_o)
    clock = max(clock + 2.5, ready(1))
    pace.run(clock)
    fetch(1, [1], wb)

    def values(r):
        v1[r] = dg(ctx[r], matrix(wb), NN).astype(BF16)

    blocks(T, 256, values)
    save(v1, v1_o)
    clock = max(clock + 2.5, ready(2))
    pace.run(clock)
    fetch(2, [2], packed)
    norms[...] = norm_rows(packed[...].reshape((-1,) + packed.shape[3:]))
    save(norms, norms_o)
    loads[1].wait()

    def first_norm(r):
        normal, _ = moments(tok[r].astype(F32))
        h1[r] = (normal * norms[0:1] + norms[1:2]).astype(BF16)

    blocks(T, 128, first_norm)
    save(h1, h1_o)
    clock = max(clock + 3.5, ready(3))
    pace.run(clock)
    fetch(3, [3], wa)

    def queries(r):
        q1[r] = dg(h1[r], matrix(wa), NN).astype(BF16)

    blocks(T, 256, queries)
    save(q1, q1_o)

    def heads(plan, body):
        def go(i, _):
            body(i, lambda side: Pace.pick(plan, i, 2, side))
            return 0

        lax.fori_loop(0, 6, go, 0)

    clock += 2.5
    heads(
        pace.units(clock, 2.2, 12),
        lambda i, at: fwd_kernel(
            frames, pair(q1, i), pair(k1, i), pair(v1, i), pair(o1, i), lse1.at[pl.ds(i, 1)], vt, ot,
            causal=False, bq=512, unit=FRAME_TOK, at=at,
        ),
    )
    save(o1, o1_o)
    save(lse1, lse1_o)
    clock = max(clock + 26.4, ready(4), ready(7))
    pace.run(clock)
    fetch(4, [4], wb)
    fetch(5, [5, 6, 7], wqkv)

    def middle(r):
        x = tok[r].astype(F32) + dg(o1[r], matrix(wb), NN)
        x1[r] = x
        normal, _ = moments(x)
        h2[r] = (normal * norms[2:3] + norms[3:4]).astype(BF16)
        for c in range(3):
            qkv[r, c * D : (c + 1) * D] = dg(h2[r], matrix(wqkv, c * D), NN).astype(BF16)

    blocks(T, 256, middle, pace.units(clock, 3.0, 4))
    clock += 12.0
    for ref, out in ((x1, x1_o), (h2, h2_o), (qkv, qkv_o)):
        save(ref, out)
    heads(
        pace.units(clock, 1.5, 12),
        lambda i, at: fwd_kernel(
            clip, pair(qkv, i), pair(qkv, i, D), pair(qkv, i, 2 * D), pair(o2, i), lse2.at[pl.ds(i, 1)], vt, ot,
            causal=True, bq=512, unit=1, at=at,
        ),
    )
    save(o2, o2_o)
    save(lse2, lse2_o)
    clock = max(clock + 18.0, ready(8))
    pace.run(clock)
    fetch(6, [8], wa)

    def late(r):
        x = x1[r] + dg(o2[r], matrix(wa), NN)
        x2[r] = x
        normal, _ = moments(x)
        h3[r] = (normal * norms[4:5] + norms[5:6]).astype(BF16)

    blocks(T, 256, late, pace.units(clock, 1.2, 4))
    save(x2, x2_o)
    save(h3, h3_o)
    pace.run(1e9)
    eng.arrive(range(9, len(eng.pieces)))
    eng.sent()
    for c in saves:
        c.wait()


def forward(clip, frames, tok, ctx, shards, n, cid):
    eng = Gather([s.shape for s in shards], n)
    T = tok.shape[0]
    wide = jax.ShapeDtypeStruct((T, D), BF16)
    full = jax.ShapeDtypeStruct((T, D), F32)
    lse = jax.ShapeDtypeStruct((6, 2, T), F32)
    kept = [wide] * 5 + [full, wide, jax.ShapeDtypeStruct((T, 3 * D), BF16), wide, full, wide, lse, lse]
    kept.append(jax.ShapeDtypeStruct((16, D), F32))
    own = shards[0].shape[0]
    square = pltpu.VMEM(eng.dims + (own, D), BF16)
    any_ = pl.BlockSpec(memory_space=pl.ANY)
    smem = pl.BlockSpec(memory_space=pltpu.SMEM)
    sem = pltpu.SemaphoreType.DMA
    outs = pl.pallas_call(
        functools.partial(forward_kernel, eng),
        out_shape=eng.outs() + kept,
        in_specs=[smem, smem] + [any_] * (2 + eng.count),
        out_specs=[any_] * (eng.count + len(kept)),
        scratch_shapes=[pltpu.VMEM((T, D), BF16)] * 2
        + [pltpu.VMEM(kept[i].shape, kept[i].dtype) for i in (0, 1, 2, 3, 4, 5, 6, 7, 8, 9, 10, 11, 12, 13)]
        + [pltpu.VMEM(eng.dims + shards[2].shape, BF16), square, square]
        + [pltpu.VMEM(eng.dims + (own, 3 * D), BF16), pltpu.VMEM((128, T), BF16), pltpu.VMEM((128, T), F32)]
        + [sem((2,)), sem, sem((16,))]
        + eng.scratch(),
        compiler_params=pltpu.CompilerParams(
            collective_id=cid, has_side_effects=True, vmem_limit_bytes=VMEM_BYTES
        ),
        name="forward",
    )(clip, frames, tok, ctx, *shards)
    return outs[: eng.count], outs[eng.count :]


def back_norm(values, gain, grad):
    normal, inverse = moments(values)
    m = grad * gain
    back = inverse * (
        m - jnp.mean(m, -1, keepdims=True) - normal * jnp.mean(m * normal, -1, keepdims=True)
    )
    return back, jnp.sum(grad * normal, 0, keepdims=True), jnp.sum(grad, 0, keepdims=True)


def mlp_kernel(clip, norms, x2, h3, cot, w_up, w_down, out, dx2, g_up, g_down, g_norm, dz, acc, dh, hid, dup):
    j = pl.program_id(0)
    T = x2.shape[0]

    def live(r):
        at = r.start + lax.broadcasted_iota(jnp.int32, (r.size, 1), 0)
        return at < clip[0]

    @pl.when(j == 0)
    def _():
        def first(r):
            dz[r] = jnp.where(live(r), cot[r], BF16(0))

        blocks(T, 256, first)

    up_w, down_w = w_up[...], w_down[...]

    def forth(r):
        u = dg(h3[r], up_w, NN)
        inner = u * (GELU_A + (GELU_A * GELU_B) * (u * u))
        t = jnp.tanh(inner)
        half = 0.5 + 0.5 * t
        hid[r] = (u * half).astype(BF16)
        slope = half + (0.5 * u) * (1.0 - t * t) * (GELU_A + (3.0 * GELU_A * GELU_B) * (u * u))
        dup[r] = (dg(dz[r], down_w, NT) * slope).astype(BF16)
        a = dg(hid[r], down_w, NN)
        b = dg(dup[r], up_w, NT)

        @pl.when(j == 0)
        def _():
            acc[r] = a
            dh[r] = b

        @pl.when(j > 0)
        def _():
            acc[r] += a
            dh[r] += b

    blocks(T, 256, forth)
    g_up[...] = dg(h3[...], dup[...], TN).astype(BF16)
    g_down[...] = dg(hid[...], dz[...], TN).astype(BF16)

    @pl.when(j == pl.num_programs(0) - 1)
    def _():
        g_norm[...] = jnp.zeros_like(g_norm)

        def last(r):
            x = x2[r]
            out[r] = jnp.where(live(r), x + acc[r], 0.0).astype(BF16)
            back, gain, bias = back_norm(x, norms[4:5], dh[r])
            dx2[r] = jnp.where(live(r), cot[r].astype(F32), 0.0) + back
            g_norm[0:1] += gain
            g_norm[1:2] += bias

        blocks(T, 128, last)


def mlp(clip, norms, x2, h3, cot, w_up, w_down, step=768):
    T = x2.shape[0]
    FF = w_up.shape[1]

    def still(shape):
        return pl.BlockSpec(shape, lambda j: (0, 0))

    return pl.pallas_call(
        mlp_kernel,
        grid=(FF // step,),
        in_specs=[
            pl.BlockSpec(memory_space=pltpu.SMEM),
            still(norms.shape),
            still((T, D)),
            still((T, D)),
            still((T, D)),
            pl.BlockSpec((D, step), lambda j: (0, j)),
            pl.BlockSpec((step, D), lambda j: (j, 0)),
        ],
        out_specs=[
            still((T, D)),
            still((T, D)),
            pl.BlockSpec((D, step), lambda j: (0, j)),
            pl.BlockSpec((step, D), lambda j: (j, 0)),
            still((8, D)),
        ],
        out_shape=[
            jax.ShapeDtypeStruct((T, D), BF16),
            jax.ShapeDtypeStruct((T, D), F32),
            jax.ShapeDtypeStruct((D, FF), BF16),
            jax.ShapeDtypeStruct((FF, D), BF16),
            jax.ShapeDtypeStruct((8, D), F32),
        ],
        scratch_shapes=[
            pltpu.VMEM((T, D), BF16),
            pltpu.VMEM((T, D), F32),
            pltpu.VMEM((T, D), F32),
            pltpu.VMEM((T, step), BF16),
            pltpu.VMEM((T, step), BF16),
        ],
        compiler_params=pltpu.CompilerParams(vmem_limit_bytes=VMEM_BYTES),
        name="mlp",
    )(clip, norms, x2, h3, cot, w_up, w_down)


def spots(j, own):
    r = lax.broadcasted_iota(jnp.int32, (128, D), 0)
    c = lax.broadcasted_iota(jnp.int32, (128, D), 1)
    return jnp.where((c == r + own * j) & (r < own), 1.0, 0.0).astype(BF16)


def load_all(sems, pairs):
    copies = [pltpu.make_async_copy(s, d, sems.at[k]) for k, (s, d) in enumerate(pairs)]
    for c in copies:
        c.start()
    return copies


def square(ref, c=0):
    return ref[:, :, :, :, c : c + D].reshape(D, D)


SCATTER = {'first': 6.0, 'rate': 3.8, 'hop': 3.5, 'slack': 2.5, 'lead': 5.0}


def scatter_pace(eng, groups):
    actions = []
    link = SCATTER["first"]
    for at, pieces in groups:
        cost = 0.0
        for m in pieces:
            i, _, w, _, _ = eng.pieces[m]
            rows = eng.shapes[i][0] * eng.dims[0] * eng.dims[1] * eng.dims[2]
            cost += SCATTER["rate"] * rows * w * 2e-6
        link = max(link, at)
        t = max(link - SCATTER["lead"], at + 2.0)
        for s, part in enumerate((0.0, 0.67, 0.33, 0.25)):
            if s == 1:
                t = link
            t += (part * cost + SCATTER["hop"] + SCATTER["slack"]) if s else 0.0
            actions.append((t, (s, pieces[0]), functools.partial(eng.act, [(s, m) for m in pieces])))
        link += cost
    return Pace(actions)


def causal_kernel(eng, *refs):
    it = iter(refs)

    def take(count):
        return [next(it) for _ in range(count)]

    clip, dx2_in, x1_in, qkv_in, o2_in, h2_in, lse, norms, wp_in, wqkv_in = take(10)
    grads = take(eng.count)
    sums = take(len(eng.outs()))
    dx1_o, gp_o, gqkv_o, gnorm = take(4)
    dx, x1, qkv, o2, h2, wp, wqkv, dy, do, dqkv, gp, gqkv, kt, dqt, dka, dva, isem, osem = take(18)
    eng.bind(grads, sums, list(it))
    T = dx.shape[0]
    eng.place.greet()
    eng.begin()
    loads = load_all(
        isem,
        [(dx2_in, dx), (wp_in, wp), (o2_in, o2), (qkv_in, qkv), (x1_in, x1), (h2_in, h2), (wqkv_in, wqkv)],
    )
    loads[0].wait()
    loads[1].wait()

    def first(r):
        dy[r] = dx[r].astype(BF16)
        do[r] = dg(dy[r], square(wp), NT).astype(BF16)

    blocks(T, 256, first)
    eng.step(0)
    loads[2].wait()

    def weight(left, right, out, c, step=256):
        def go(k, _):
            at = pl.multiple_of(k * step, step)
            g = dg(left[...], right[:, pl.ds(at, step)], TN).astype(BF16)
            out[:, :, :, :, pl.ds(c + at, step)] = g.reshape(out.shape[:4] + (step,))
            return 0

        lax.fori_loop(0, D // step, go, 0)

    weight(o2, dy, gp, 0)
    saves = [pltpu.make_async_copy(gp, gp_o, osem.at[0])]
    saves[0].start()
    eng.step(1)
    loads[3].wait()
    ticks = [(t, 1 + 2 * (t - 2)) for t in range(2, 8)]

    def heads(i, _):
        def at(side):
            for t, p in ticks:
                if p % 2 == side:
                    pl.when(i == p // 2)(functools.partial(eng.step, t))

        cols = pl.ds(pl.multiple_of(i * 128, 128), 128)
        bwd_kernel(
            clip, pair(qkv, i), pair(qkv, i, D), pair(qkv, i, 2 * D), pair(o2, i), pair(do, i),
            lse.at[pl.ds(i, 1)], dqkv.at[:, :, cols], kt, dqt, dka, dva,
            causal=True, bq=256, bk=512, unit=1, at=at,
        )
        return 0

    lax.fori_loop(0, 6, heads, 0)
    for c in loads[4:]:
        c.wait()
    gnorm[...] = jnp.zeros_like(gnorm)

    def back(r):
        dh = sum(dg(dqkv[c, r], square(wqkv, c * D), NT) for c in range(3))
        g, gain, bias = back_norm(x1[r], norms[2:3], dh)
        dx[r] += g
        gnorm[0:1] += gain
        gnorm[1:2] += bias

    blocks(T, 256, back)
    saves.append(pltpu.make_async_copy(dx, dx1_o, osem.at[1]))
    saves[1].start()
    eng.step(8)
    for c in range(3):
        weight(h2, dqkv.at[c], gqkv, c * D)
    saves.append(pltpu.make_async_copy(gqkv, gqkv_o, osem.at[2]))
    saves[2].start()
    for t in range(9, eng.steps):
        eng.step(t)
    eng.end()
    for c in saves:
        c.wait()


def causal_back(clip, dx2, x1, qkv, o2, h2, lse, norms, wp, wqkv, grads, targets, n, cid):
    eng = Scatter([a.shape[3:] for a in grads], targets, n)
    T = dx2.shape[0]
    own = wp.shape[3]
    any_ = pl.BlockSpec(memory_space=pl.ANY)
    smem = pl.BlockSpec(memory_space=pltpu.SMEM)
    vmem = pl.BlockSpec(memory_space=pltpu.VMEM)
    sem = pltpu.SemaphoreType.DMA
    small = jax.ShapeDtypeStruct((8, D), F32)
    one, three = eng.dims + (own, D), eng.dims + (own, 3 * D)

    def vm(shape, dtype=BF16):
        return pltpu.VMEM(shape, dtype)

    sums = eng.outs()
    outs = pl.pallas_call(
        functools.partial(causal_kernel, eng),
        out_shape=sums
        + [jax.ShapeDtypeStruct((T, D), F32), jax.ShapeDtypeStruct(one, BF16), jax.ShapeDtypeStruct(three, BF16), small],
        in_specs=[smem] + [any_] * 5 + [vmem] * 2 + [any_] * (2 + eng.count),
        out_specs=[vmem] * len(sums) + [any_] * 3 + [vmem],
        scratch_shapes=[
            vm((T, D), F32),
            vm((T, D), F32),
            vm((T, 3 * D)),
            vm((T, D)),
            vm((T, D)),
            vm(one),
            vm(three),
            vm((T, D)),
            vm((T, D)),
            vm((3, T, D)),
            vm(one),
            vm(three),
            vm((128, T)),
            vm((128, T), F32),
            vm((T, 128), F32),
            vm((T, 128), F32),
            sem((7,)),
            sem((3,)),
        ]
        + eng.scratch(),
        compiler_params=pltpu.CompilerParams(
            collective_id=cid, has_side_effects=True, vmem_limit_bytes=VMEM_BYTES
        ),
        name="causal_back",
    )(clip, dx2, x1, qkv, o2, h2, lse, norms, wp, wqkv, *grads)
    return outs[: len(sums)], outs[len(sums) :]


def cross_kernel(eng, *refs):
    it = iter(refs)

    def take(count):
        return [next(it) for _ in range(count)]

    frames, dx1_in, tok_in, ctx_in, q1_in, k1_in, v1_in, o1_in, h1_in, lse, norms, gnorm2, gnorm3, wo_in, wq_in = take(15)
    given = take(2)
    sums = take(len(eng.outs()))
    (grad_o,) = take(1)
    dx, tok, ctx, q1, k1, v1, o1, h1, wo, wq, dy, do, dqkv, kt, dqt, dka, dva, gsum, isem, osem = take(20)
    go_, gv, gk, gq, gn = take(5)
    eng.bind(list(given) + [go_, gv, gk, gq, gn], sums, list(it))
    T = dx.shape[0]
    n = gn.shape[0] * gn.shape[1] * gn.shape[2]
    own = D // n
    eng.place.greet()
    eng.begin()
    loads = load_all(
        isem,
        [(dx1_in, dx), (wo_in, wo), (o1_in, o1), (q1_in, q1), (k1_in, k1), (v1_in, v1), (h1_in, h1), (ctx_in, ctx),
         (wq_in, wq), (tok_in, tok)],
    )
    loads[0].wait()
    loads[1].wait()

    def first(r):
        dy[r] = dx[r].astype(BF16)
        do[r] = dg(dy[r], square(wo), NT).astype(BF16)

    blocks(T, 256, first)
    loads[2].wait()

    def weight(left, right, out, at, width=256):
        g = dg(left[...], right[:, pl.ds(at, width)], TN).astype(BF16)
        out[:, :, :, :, pl.ds(at, width)] = g.reshape(out.shape[:4] + (width,))

    def whole(k, _):
        weight(o1, dy, go_, pl.multiple_of(k * 256, 256))
        return 0

    lax.fori_loop(0, 3, whole, 0)
    eng.put([4])
    for c in loads[3:]:
        c.wait()
    third = [[5 + g, 8 + g, 11 + g] for g in range(3)]
    start, unit, gap = 9.0, 3.05, 3.0
    made = [start + 4 * (g + 1) * unit + (g + 1) * gap for g in range(3)]
    pace = scatter_pace(
        eng,
        [(0.0, [m]) for m in range(4)]
        + [(start, [4])]
        + [(made[g], third[g]) for g in range(3)]
        + [(made[2] + 6.0, [14])],
    )
    plan = pace.units(start, unit, 12, gap, 4)

    def heads(i, _):
        def at(side):
            Pace.pick(plan, i, 2, side)

        cols = pl.ds(pl.multiple_of(i * 128, 128), 128)
        bwd_kernel(
            frames, pair(q1, i), pair(k1, i), pair(v1, i), pair(o1, i), pair(do, i),
            lse.at[pl.ds(i, 1)], dqkv.at[:, :, cols], kt, dqt, dka, dva,
            causal=False, bq=1024, bk=256, unit=FRAME_TOK, at=at,
        )

        @pl.when(i % 2 == 1)
        def _():
            c = pl.multiple_of((i // 2) * 256, 256)
            weight(ctx, dqkv.at[2], gv, c)
            weight(ctx, dqkv.at[1], gk, c)
            weight(h1, dqkv.at[0], gq, c)

        for g in range(3):
            pl.when(i == 2 * g + 1)(functools.partial(eng.put, third[g]))
        return 0

    lax.fori_loop(0, 6, heads, 0)
    gsum[...] = jnp.zeros_like(gsum)
    gsum[2:4] = gnorm2[0:2]
    gsum[4:6] = gnorm3[0:2]
    pace.run(made[2])

    def back(r):
        dh = dg(dqkv[0, r], square(wq), NT)
        g, gain, bias = back_norm(tok[r].astype(F32), norms[0:1], dh)
        dx[r] += g
        gsum[0:1] += gain
        gsum[1:2] += bias

    blocks(T, 256, back, pace.units(made[2] + 1.0, 1.2, 4))
    save = pltpu.make_async_copy(dx, grad_o, osem)
    save.start()
    pace.run(made[2] + 5.5)
    rows = gsum[...].astype(BF16)
    Z, Y, X = gn.shape[:3]
    for j in range(n):
        z, y, x = j // (Y * X), (j // X) % Y, j % X
        gn[z, y, x, :, :128] = dg(rows, spots(j, own), NT).astype(BF16)
        gn[z, y, x, :, 128:] = jnp.zeros((16, 128), BF16)
    eng.put([14])
    pace.run(1e9)
    eng.end()
    save.wait()


def cross_back(frames, dx1, tok, ctx, q1, k1, v1, o1, h1, lse, norms, gnorm2, gnorm3, wo, wq, gp, gqkv, n, cid):
    own = wo.shape[3]
    one = gp.shape
    shapes = [gp.shape[3:], gqkv.shape[3:], one[3:], one[3:], one[3:], one[3:], (16, 256)]
    pieces = [(0, 0, D)] + [(1, c * D, D) for c in range(3)] + [(2, 0, D)]
    pieces += [(i, c * 256, 256) for i in (3, 4, 5) for c in range(3)] + [(6, 0, 256)]
    targets = [(6, 0), (5, 0), (4, 0), (3, 0), (2, 0), (1, 0), (0, 0)]
    eng = Scatter(shapes, targets, n, made=(2, 3, 4, 5, 6), pieces=pieces)
    T = dx1.shape[0]
    any_ = pl.BlockSpec(memory_space=pl.ANY)
    smem = pl.BlockSpec(memory_space=pltpu.SMEM)
    vmem = pl.BlockSpec(memory_space=pltpu.VMEM)
    sem = pltpu.SemaphoreType.DMA

    def vm(shape, dtype=BF16):
        return pltpu.VMEM(shape, dtype)

    sums = eng.outs()
    outs = pl.pallas_call(
        functools.partial(cross_kernel, eng),
        out_shape=sums + [jax.ShapeDtypeStruct((T, D), F32)],
        in_specs=[smem] + [any_] * 8 + [vmem] * 4 + [any_] * 4,
        out_specs=[vmem] * len(sums) + [any_],
        scratch_shapes=[vm((T, D), F32)]
        + [vm((T, D))] * 7
        + [vm(one)] * 2
        + [vm((T, D))] * 2
        + [vm((3, T, D)), vm((128, T)), vm((128, T), F32), vm((T, 128), F32), vm((T, 128), F32), vm((16, D), F32)]
        + [sem((10,)), sem]
        + [vm(one)] * 4
        + [vm(one[:3] + (16, 256))]
        + eng.scratch(),
        compiler_params=pltpu.CompilerParams(
            collective_id=cid, has_side_effects=True, vmem_limit_bytes=VMEM_BYTES
        ),
        name="cross_back",
    )(frames, dx1, tok, ctx, q1, k1, v1, o1, h1, lse, norms, gnorm2, gnorm3, wo, wq, gp, gqkv)
    return outs[: len(sums)], outs[len(sums)]


def shards(
    tokens,
    context,
    clip_lengths,
    context_frames,
    norm1_gain,
    norm1_bias,
    cross_q,
    cross_k,
    cross_v,
    cross_out,
    norm2_gain,
    norm2_bias,
    attn_qkv,
    attn_out,
    norm3_gain,
    norm3_bias,
    mlp_up,
    mlp_down,
    cotangent,
):
    n = lax.axis_size("fsdp")
    stream_in = tokens[0].astype(F32)
    context_rows = context[0]
    slot_rows = stream_in.shape[0]
    own = norm1_gain.shape[0]
    padding = (jnp.arange(slot_rows) < clip_lengths[0])[:, None]
    norms = jnp.stack([norm1_gain, norm1_bias, norm2_gain, norm2_bias, norm3_gain, norm3_bias])
    norms = jnp.pad(norms, ((0, 10), (0, 256 - own)))

    def flat(arrays):
        return [a.reshape(-1, a.shape[4]) for a in arrays]

    def gather(arrays):
        return Gather([a.shape for a in arrays], n), arrays

    def weight(left, right):
        g = dg(left, right, TN).astype(BF16)
        return g.reshape(n, -1, g.shape[1])

    def scatter(grads):
        arrays = [g.reshape(grid_of(n) + g.shape[1:]) for g, _ in grads]
        return Scatter([a.shape[3:] for a in arrays], [t for _, t in grads], n), arrays

    if own % 16 == 0:
        whole, kept = forward(
            clip_lengths,
            context_frames,
            tokens[0],
            context_rows,
            [cross_k, cross_v, norms, cross_q, cross_out, attn_qkv, attn_out, mlp_up, mlp_down],
            n,
            0,
        )
        _, _, _, w_q, w_o, w_qkv, w_p, w_up, w_down = whole
        q1, k1, v1, o1, h1, x1, h2, qkv, o2, x2, h3, lse1, lse2, norms = kept
        block_out, dx2, g_up, g_down, g_norm3 = mlp(
            clip_lengths, norms, x2, h3, cotangent[0], *flat([w_up, w_down])
        )
        grads = [g_down.reshape(w_down.shape), g_up.reshape(w_up.shape)]
        (s_up, s_down), (dx1, g_p, g_qkv, g_norm2) = causal_back(
            clip_lengths, dx2, x1, qkv, o2, h2, lse2, norms, w_p, w_qkv, grads, [(1, 0), (0, 0)], n, 1
        )
        (s_norms, s_q, s_k, s_v, s_o, s_qkv, s_p), input_grad = cross_back(
            context_frames, dx1, tokens[0], context_rows, q1, k1, v1, o1, h1, lse1, norms, g_norm2, g_norm3,
            w_o, w_q, g_p, g_qkv, n, 2
        )
    else:
        first, operands = gather([norms, cross_q, cross_k, cross_v])
        norms, *whole = alone(first, operands, 0, "gather_cross")
        w_q, w_k, w_v = flat(whole)
        norms = norms.reshape((n,) + norms.shape[3:])[:, :6, :own].transpose(1, 0, 2).reshape(6, D).astype(F32)
        gain_one, bias_one, gain_two, bias_two, gain_three, bias_three = [norms[i] for i in range(6)]

        normal_one, inverse_one = moments(stream_in)
        h1 = (normal_one * gain_one + bias_one).astype(BF16)
        q1 = dg(h1, w_q, NN).astype(BF16)
        k1 = dg(context_rows, w_k, NN).astype(BF16)
        v1 = dg(context_rows, w_v, NN).astype(BF16)
        second, operands = gather([cross_out, attn_qkv, attn_out])
        (o1, lse1), whole = attn_fwd(
            context_frames, q1, k1, v1, (0, 0, 0), False, FRAME_TOK, 512,
            second, operands, paced(second, 8.0, 4.8, 2.2), 1, "cross_fwd",
        )
        w_o, w_qkv, w_p = flat(whole)
        x1 = stream_in + dg(o1, w_o, NN)
        normal_two, inverse_two = moments(x1)
        h2 = (normal_two * gain_two + bias_two).astype(BF16)
        qkv = dg(h2, w_qkv, NN).astype(BF16)
        third, operands = gather([mlp_up, mlp_down])
        (o2, lse2), whole = attn_fwd(
            clip_lengths, qkv, qkv, qkv, (0, 6, 12), True, 1, 512,
            third, operands, paced(third, 8.0, 4.8, 1.5), 2, "causal_fwd",
        )
        w_up, w_down = flat(whole)
        x2 = x1 + dg(o2, w_p, NN)
        normal_three, inverse_three = moments(x2)
        h3 = (normal_three * gain_three + bias_three).astype(BF16)
        up = dg(h3, w_up, NN)
        hidden = gelu(up).astype(BF16)
        x3 = x2 + dg(hidden, w_down, NN)
        block_out = jnp.where(padding, x3, 0.0).astype(BF16)

        dx3 = jnp.where(padding, cotangent[0].astype(F32), 0.0)
        dz = dx3.astype(BF16)
        dup = (dg(dz, w_down, NT) * gelu_slope(up)).astype(BF16)
        back, g_gain3, g_bias3 = norm_back(normal_three, inverse_three, gain_three, dg(dup, w_up, NT))
        dx2 = dx3 + back
        dy2 = dx2.astype(BF16)
        do2 = dg(dy2, w_p, NT).astype(BF16)
        fourth, operands = scatter([(weight(hidden, dz), (1, 0)), (weight(h3, dup), (0, 0))])
        (dqkv,), (s_up, s_down) = attn_bwd(
            clip_lengths, qkv, qkv, qkv, o2, do2, lse2, (0, 6, 12), True, 1, 256, 512,
            fourth, operands, paced(fourth, 8.0, 4.8, 2.45), 3, "causal_bwd",
        )
        dh2 = sum(dg(dqkv[c], w_qkv[:, c * D : (c + 1) * D], NT) for c in range(3))
        back, g_gain2, g_bias2 = norm_back(normal_two, inverse_two, gain_two, dh2)
        dx1 = dx2 + back
        dy1 = dx1.astype(BF16)
        do1 = dg(dy1, w_o, NT).astype(BF16)
        fifth, operands = scatter(
            [(weight(o2, dy2), (0, 0))]
            + [(weight(h2, dqkv[c]), (1, c * D)) for c in range(3)]
            + [(weight(o1, dy1), (2, 0))]
        )
        (dqkv1,), (s_p, s_qkv, s_o) = attn_bwd(
            context_frames, q1, k1, v1, o1, do1, lse1, (0, 0, 0), False, FRAME_TOK, 1024, 256,
            fifth, operands, paced(fifth, 8.0, 4.8, 3.1), 4, "cross_bwd",
        )
        dh1 = dg(dqkv1[0], w_q, NT)
        back, g_gain1, g_bias1 = norm_back(normal_one, inverse_one, gain_one, dh1)
        input_grad = dx1 + back

        g_norms = jnp.stack([g_gain1, g_bias1, g_gain2, g_bias2, g_gain3, g_bias3]).astype(BF16)
        g_norms = jnp.pad(g_norms.reshape(6, n, own).transpose(1, 0, 2), ((0, 0), (0, 10), (0, 256 - own)))

        sixth, operands = scatter(
            [
                (weight(context_rows, dqkv1[2]), (3, 0)),
                (weight(context_rows, dqkv1[1]), (2, 0)),
                (weight(h1, dqkv1[0]), (1, 0)),
                (g_norms, (0, 0)),
            ]
        )
        s_norms, s_q, s_k, s_v = alone(sixth, operands, 5, "scatter_cross")
    scale = (slot_rows * tokens.shape[0] * n * lax.axis_size("rep")) ** (-0.5)
    vec = [s_norms[i, :own] * scale for i in range(6)]
    done = [None, *finish([s_q, s_k, s_v, s_o, s_qkv, s_p, s_up, s_down], scale)]
    return (
        block_out[None],
        input_grad[None],
        vec[0],
        vec[1],
        done[1],
        done[2],
        done[3],
        done[4],
        vec[2],
        vec[3],
        done[5],
        done[6],
        vec[4],
        vec[5],
        done[7],
        done[8],
    )


def solution(mesh):
    in_specs = (
        P(("fsdp", "rep"), None, None),
        P(("fsdp", "rep"), None, None),
        P(("fsdp", "rep")),
        P(("fsdp", "rep")),
        P("fsdp"),
        P("fsdp"),
        P("fsdp", None),
        P("fsdp", None),
        P("fsdp", None),
        P("fsdp", None),
        P("fsdp"),
        P("fsdp"),
        P("fsdp", None),
        P("fsdp", None),
        P("fsdp"),
        P("fsdp"),
        P("fsdp", None),
        P("fsdp", None),
        P(("fsdp", "rep"), None, None),
    )
    out_specs = (
        P(("fsdp", "rep"), None, None),
        P(("fsdp", "rep"), None, None),
        P("fsdp"),
        P("fsdp"),
        P("fsdp", None),
        P("fsdp", None),
        P("fsdp", None),
        P("fsdp", None),
        P("fsdp"),
        P("fsdp"),
        P("fsdp", None),
        P("fsdp", None),
        P("fsdp"),
        P("fsdp"),
        P("fsdp", None),
        P("fsdp", None),
    )
    return jax.shard_map(shards, mesh=mesh, in_specs=in_specs, out_specs=out_specs, check_vma=False)
```

```python
import functools

import jax
import jax.numpy as jnp
from jax import lax
from jax.experimental import pallas as pl
from jax.experimental.pallas import tpu as pltpu
from jax.sharding import PartitionSpec as P

D = 768
FRAME_TOK = 256
EPS = 1e-05
MESH = pl.DeviceIdType.MESH
VMEM_BYTES = 58 << 20

F32, BF16 = jnp.float32, jnp.bfloat16
NN = (((1,), (0,)), ((), ()))
NT = (((1,), (1,)), ((), ()))
TN = (((0,), (0,)), ((), ()))
def dg(a, b, dims): return lax.dot_general(a, b, dims, preferred_element_type=F32)

def lanes_of(side):
    lane = lax.broadcasted_iota(jnp.int32, (1, 128), 1)
    return (lane >= 64 * side) & (lane < 64 * side + 64), lane == 64 * (1 - side)


def head_sides(side, q2, k2, bias):
    mine, extra = lanes_of(side)
    qa = jnp.where(mine, q2, jnp.where(extra, 1.0, 0.0).astype(BF16))
    ka = jnp.where(mine, k2, jnp.where(extra, bias, 0.0).astype(BF16))
    return qa, ka


def key_bias(n_ref, unit, K):
    live = n_ref[0] * unit
    return jnp.where(lax.broadcasted_iota(jnp.int32, (K, 1), 0) < live, 0.0, -1e30).astype(F32)


def fwd_unit(side, n_ref, q_ref, k_ref, v_ref, o_ref, l_ref, vt, ot, *, causal, bq, unit):
    T, K = q_ref.shape[0], k_ref.shape[0]

    @pl.when(side == 0)
    def _():
        vt[...] = v_ref[...].T

    qa, ka = head_sides(side, q_ref[...] * BF16(0.125), k_ref[...], key_bias(n_ref, unit, K))
    rows = pl.ds(pl.multiple_of(side * 64, 64), 64)
    for j in range(T // bq):
        span = (j + 1) * bq if causal else K
        s = dg(ka[:span], qa[j * bq : (j + 1) * bq], NT)
        if causal:
            top = j * bq
            ok = lax.broadcasted_iota(jnp.int32, (bq, bq), 0) <= lax.broadcasted_iota(
                jnp.int32, (bq, bq), 1
            )
            diag = jnp.where(ok, s[top:], -1e30)
            s = diag if top == 0 else jnp.concatenate([s[:top], diag], 0)
        m = jnp.max(s, 0, keepdims=True)
        p = jnp.exp(s - m)
        l = jnp.sum(p, 0, keepdims=True)
        ot[rows, j * bq : (j + 1) * bq] = dg(vt[rows, :span], p.astype(BF16), NN) * (1.0 / l)
        l_ref[0, pl.ds(side, 1), j * bq : (j + 1) * bq] = m + jnp.log(l)

    @pl.when(side == 1)
    def _():
        o_ref[...] = ot[...].T.astype(BF16)


def fwd_kernel(*refs, causal, bq, unit, at):
    def go(side, _):
        at(side)
        fwd_unit(side, *refs, causal=causal, bq=bq, unit=unit)
        return 0

    lax.fori_loop(0, 2, go, 0)


def bwd_unit(
    side, n_ref, q_ref, k_ref, v_ref, o_ref, do_ref, l_ref, g_ref, kt, dqt, dka, dva, dl, *, causal, bq, bk, unit
):
    T, K = q_ref.shape[0], k_ref.shape[0]

    @pl.when(side == 0)
    def _():
        kt[...] = k_ref[...].T
        prod = (do_ref[...].astype(F32) * o_ref[...].astype(F32)).T
        dl[0:1] = jnp.sum(prod[:64], 0, keepdims=True)
        dl[1:2] = jnp.sum(prod[64:], 0, keepdims=True)

    q2 = q_ref[...] * BF16(0.125)
    do2 = do_ref[...]
    qa, ka = head_sides(side, q2, k_ref[...], key_bias(n_ref, unit, K))
    va = jnp.where(lanes_of(side)[0], v_ref[...], BF16(0))
    low = lax.broadcasted_iota(jnp.int32, (1, 128), 1) < 64
    delta = dl[pl.ds(side, 1), :]
    lse = l_ref[0, pl.ds(side, 1), :]
    half = pl.ds(pl.multiple_of(side * 64, 64), 64)
    for i in range(K // bk):
        dk = dv = None
        kb, vb = ka[i * bk : (i + 1) * bk], va[i * bk : (i + 1) * bk]
        for j in range(T // bq):
            if causal and (j + 1) * bq <= i * bk:
                continue
            cols = slice(j * bq, (j + 1) * bq)
            p = jnp.exp(dg(kb, qa[cols], NT) - lse[:, cols])
            if causal and j * bq < (i + 1) * bk:
                ok = i * bk + lax.broadcasted_iota(
                    jnp.int32, (bk, bq), 0
                ) <= j * bq + lax.broadcasted_iota(jnp.int32, (bk, bq), 1)
                p = jnp.where(ok, p, 0.0)
            dp = dg(vb, do2[cols], NT)
            ds = (p * (dp - delta[:, cols])).astype(BF16)
            a = dg(p.astype(BF16), do2[cols], NN)
            b = dg(ds, q2[cols], NN)
            dv = a if dv is None else dv + a
            dk = b if dk is None else dk + b
            c = dg(kt[half, i * bk : (i + 1) * bk], ds, NN)
            if i == 0:
                dqt[half, cols] = c
            else:
                dqt[half, cols] += c
        rows = slice(i * bk, (i + 1) * bk)

        @pl.when(side == 0)
        def _(rows=rows, dk=dk, dv=dv):
            dka[rows] = dk
            dva[rows] = dv

        @pl.when(side == 1)
        def _(rows=rows, dk=dk, dv=dv):
            g_ref[1, rows, :] = jnp.where(low, dka[rows], dk).astype(BF16)
            g_ref[2, rows, :] = jnp.where(low, dva[rows], dv).astype(BF16)

    @pl.when(side == 1)
    def _():
        g_ref[0] = (dqt[...] * 0.125).T.astype(BF16)


def bwd_kernel(*refs, causal, bq, bk, unit, at):
    def go(side, _):
        at(side)
        bwd_unit(side, *refs, causal=causal, bq=bq, bk=bk, unit=unit)
        return 0

    lax.fori_loop(0, 2, go, 0)


def grid_of(n):
    if n == 16:
        return 4, 2, 2
    if n == 64:
        return 4, 4, 4
    return n, 1, 1


def cut(shapes):
    out = []
    for i, (rows, cols) in enumerate(shapes):
        step = 256 if rows > cols // 8 and cols == 768 else min(cols, 768)
        out += [(i, c, step) for c in range(0, cols, step)]
    return out


def remote(src, dst, send, recv, dev):
    return pltpu.make_async_remote_copy(
        src_ref=src, dst_ref=dst, send_sem=send, recv_sem=recv, device_id=dev, device_id_type=MESH
    )


class Place:
    def __init__(self, dims):
        self.dims = dims
        self.size = dict(zip("zyx", dims))
        Z, Y, X = dims
        self.me = lax.axis_index("fsdp")
        self.core = lax.axis_index("rep")
        self.mine = {"z": self.me // (Y * X), "y": (self.me // X) % Y, "x": self.me % X}
        if Y == X:
            y, x = self.mine["y"], self.mine["x"]
            self.size.update(a=X, b=Y)
            self.mine.update(a=self.choose(x, y), b=self.choose(y, x))

    def here(self, axis):
        return {k: self.mine[k] for k in ("zab" if axis in "ab" else "zyx")}

    def peers(self, axis):
        mine, count = self.mine[axis], self.size[axis]
        out = []
        for k in range(1, count):
            at = self.here(axis)
            at[axis] = (mine + k) % count
            y, x = self.plane(at)
            dev = ((at["z"] * self.size["y"] + y) * self.size["x"] + x, self.core)
            out.append((at[axis], (mine + count - k) % count, dev))
        return out

    def sibling(self):
        return (self.me, 1 - self.core)

    def greet(self):
        bar = pltpu.get_barrier_semaphore()
        devs = [d for axis in "zyx" for _, _, d in self.peers(axis)] + [self.sibling()]
        for d in devs:
            pl.semaphore_signal(bar, inc=1, device_id=d, device_id_type=MESH)
        pl.semaphore_wait(bar, len(devs))

    def by_core(self, action):
        if self.size["y"] == self.size["x"]:
            action(self.core, "a", "b")
            return

        @pl.when(self.core == 0)
        def _():
            action(0, "x", "y")

        @pl.when(self.core == 1)
        def _():
            action(1, "y", "x")

    def choose(self, first, second):
        return first + self.core * (second - first)

    def plane(self, at):
        if "a" in at:
            return self.choose(at["b"], at["a"]), self.choose(at["a"], at["b"])
        return at["y"], at["x"]


AHEAD = 3


class Gather:
    def __init__(self, shapes, n):
        self.dims = grid_of(n)
        self.pieces = cut(shapes)
        self.count = len(shapes)
        self.shapes = shapes
        self.steps = len(self.pieces) + 2

    def outs(self):
        return [jax.ShapeDtypeStruct(self.dims + tuple(s), BF16) for s in self.shapes]

    def scratch(self):
        Z, Y, X = self.dims
        M, z, s = len(self.pieces), max(self.dims[0] - 1, 1), max(Y - 1, X - 1, 1)
        t = s * max(Y, X)
        sem = pltpu.SemaphoreType.DMA
        return [sem((2, self.count))] + [sem((M, c)) for c in (z, z, s, s, t, t, z, z, s, s, t, t)]

    def bind(self, shards, outs, scratch):
        self.shards, self.out = shards, outs
        self.own, *self.sem = scratch
        self.place = Place(self.dims)

    def half(self, m, side):
        _, c, w = self.pieces[m]
        return pl.ds(pl.multiple_of(c + side * (w // 2), w // 2), w // 2)

    def view(self, m, side, z, y, x):
        return self.out[self.pieces[m][0]].at[slice(None) if z is None else z, y, x, :, self.half(m, side)]

    def hop(self, stage, m, side, axes, coming):
        a, b = axes
        axis = ("z", a, b)[stage]
        out = []
        for k, (_, frm, dev) in enumerate(self.place.peers(axis)):
            at = self.place.here(a)
            if stage:
                at["z"] = None
            if coming:
                at[axis] = frm
            for e in range(self.place.size[a] if stage == 2 else 1):
                if stage == 2:
                    at = {**at, a: e}
                y, x = self.place.plane(at)
                v = self.view(m, side, at["z"], y, x)
                src = v
                if stage == 0 and not coming:
                    src = self.shards[self.pieces[m][0]].at[:, self.half(m, side)]
                s, r = self.sem[2 * stage : 2 * stage + 2]
                slot = k * self.place.size[a] + e if stage == 2 else k
                out.append(
                    (
                        slot,
                        (at["z"], y, x),
                        lambda v=v, src=src, s=s, r=r, slot=slot, dev=dev: remote(
                            src, v, s.at[m, slot], r.at[m, slot], dev
                        ),
                    )
                )
        return out

    def give(self, stage, m, side, at, k):
        v = self.view(m, side, *at)
        s, r = self.sem[6 + 2 * stage : 8 + 2 * stage]
        return remote(v, v, s.at[m, k], r.at[m, k], self.place.sibling())

    def own_copies(self):
        p = self.place.mine
        return [
            remote(s, o.at[p["z"], p["y"], p["x"]], self.own.at[0, i], self.own.at[1, i], self.place.sibling())
            for i, (s, o) in enumerate(zip(self.shards, self.out))
        ]

    def begin(self, ahead):
        for c in self.own_copies():
            c.start()
        self.leave(range(min(ahead, len(self.pieces))))

    def leave(self, pieces):
        def go(core, a, b):
            for m in pieces:
                for _, _, c in self.hop(0, m, core, (a, b), False):
                    c().start()

        self.place.by_core(go)

    def settle(self):
        for c in self.own_copies():
            c.wait()

    def act(self, pairs):
        def go(core, a, b):
            for stage, m in pairs:
                came = self.hop(stage, m, core, (a, b), True)
                for _, _, c in came:
                    c().wait_recv()
                if stage < 2:
                    for _, _, c in self.hop(stage + 1, m, core, (a, b), False):
                        c().start()
                for k, at, _ in came:
                    self.give(stage, m, core, at, k).start()

        self.place.by_core(go)

    def step(self, t):
        if t == 0:
            self.settle()
        if t + AHEAD < len(self.pieces):
            self.leave([t + AHEAD])
        self.act([(s, t - s) for s in range(3) if 0 <= t - s < len(self.pieces)])

    def arrive(self, pieces):
        def go(core, a, b):
            for m in pieces:
                for stage in range(3):
                    for k, at, _ in self.hop(stage, m, core, (b, a), True):
                        self.give(stage, m, 1 - core, at, k).wait_recv()

        self.place.by_core(go)

    def sent(self):
        def go(core, a, b):
            for m in range(len(self.pieces)):
                for stage in range(3):
                    for _, _, c in self.hop(stage, m, core, (a, b), False):
                        c().wait_send()
                    for k, at, _ in self.hop(stage, m, core, (a, b), True):
                        self.give(stage, m, core, at, k).wait_send()

        self.place.by_core(go)

    def end(self):
        self.arrive(range(len(self.pieces)))
        self.sent()


class Scatter:
    def __init__(self, shapes, targets, n, made=(), pieces=None):
        self.dims = grid_of(n)
        self.made = made
        self.count = len(shapes)
        self.pieces = [
            (i, c, w, targets[i][0], targets[i][1] + c) for i, c, w in pieces or cut(shapes)
        ]
        self.shapes, self.targets = shapes, targets
        self.steps = len(self.pieces) + 3

    def outs(self):
        width, rows = {}, {}
        for i, _, w, o, at in self.pieces:
            width[o], rows[o] = max(width.get(o, 0), at + w), self.shapes[i][0]
        return [jax.ShapeDtypeStruct((rows[o], width[o]), F32) for o in range(len(width))]

    def scratch(self):
        Z, Y, X = self.dims
        M, S = len(self.pieces), max(Y, X)
        one, z = max(S - 1, 1), max(Z - 1, 1)
        shape = [(self.shapes[i][0], w // 2) for i, _, w, _, _ in self.pieces]
        sem = pltpu.SemaphoreType.DMA
        lead = [(S, S, Z), (S, S, Z), (one, S, Z), (one, Z), (z,)]
        return (
            [[pltpu.VMEM(l + s, BF16) for s in shape] for l in lead]
            + [[pltpu.VMEM((2,) + s, F32) for s in shape]]
            + [sem((M, S * S))] * 3
            + [sem((M, one))] * 4
            + [sem((M, z))] * 2
            + [sem((M,))] * 2
        )

    def bind(self, grads, outs, scratch):
        self.grads, self.out = grads, outs
        self.acc, self.sib, self.got1, self.got2, self.got3, self.fin, self.lsem, *self.sem = scratch
        self.place = Place(self.dims)

    def meet(self, m, core):
        Z, Y, X = self.dims
        i, c, w, _, _ = self.pieces[m]
        for y in range(Y):
            for x in range(X):
                k = y * X + x
                mine, theirs = [
                    self.grads[i].at[:, y, x, :, pl.ds(pl.multiple_of(c + s * (w // 2), w // 2), w // 2)]
                    for s in (core, 1 - core)
                ]
                at = self.place.choose(y, x), self.place.choose(x, y)
                if i not in self.made:
                    yield pltpu.make_async_copy(mine, self.acc[m].at[at], self.lsem.at[m, k])
                yield remote(
                    theirs,
                    self.sib[m].at[at[::-1]],
                    self.sem[0].at[m, k],
                    self.sem[1].at[m, k],
                    self.place.sibling(),
                )

    def hop(self, stage, m, axes):
        a, b = axes
        mine = self.place.mine
        s, r = self.sem[2 * stage : 2 * stage + 2]
        got = (None, self.got1, self.got2, self.got3)[stage]
        for k, (there, _, dev) in enumerate(self.place.peers((None, b, a, "z")[stage])):
            at = (mine[b], mine[a])[: stage - 1] + (there,)
            yield remote(self.acc[m].at[at], got[m].at[k], s.at[m, k], r.at[m, k], dev)

    def swap(self, m, side):
        v = self.fin[m].at[side]
        return remote(v, v, self.sem[8].at[m], self.sem[9].at[m], self.place.sibling())

    def add(self, dst, srcs):
        total = dst[...].astype(F32)
        for s in srcs:
            total = total + s[...].astype(F32)
        dst[...] = total.astype(BF16)

    def begin(self, ahead=0):
        def go(core, a, b):
            for m, piece in enumerate(self.pieces):
                if piece[0] not in self.made:
                    for c in self.meet(m, core):
                        c.start()

        self.place.by_core(go)

    def put(self, pieces):
        def go(core, a, b):
            Z, Y, X = self.dims
            for m in pieces:
                i, c, w, _, _ = self.pieces[m]
                for y in range(Y):
                    for x in range(X):
                        at = self.place.choose(y, x), self.place.choose(x, y)
                        side = pl.ds(pl.multiple_of(c + core * (w // 2), w // 2), w // 2)
                        self.acc[m][at] = self.grads[i][:, y, x, :, side]
                for c in self.meet(m, core):
                    c.start()

        self.place.by_core(go)

    def step(self, t):
        self.act([(stage, t - stage) for stage in range(4) if 0 <= t - stage < len(self.pieces)])

    def act(self, pairs):
        def go(core, a, b):
            mine, size = self.place.mine, self.place.size
            for stage, m in pairs:
                acc = self.acc[m]
                if stage == 0:
                    for c in self.meet(m, core):
                        c.wait()
                    for j in range(size[b]):
                        self.add(acc.at[j, : size[a]], [self.sib[m].at[j, : size[a]]])
                else:
                    for c in self.hop(stage, m, (a, b)):
                        c.wait_recv()
                if stage == 1:
                    self.add(
                        acc.at[mine[b], : size[a]],
                        [self.got1[m].at[k, : size[a]] for k in range(size[b] - 1)],
                    )
                if stage == 2:
                    self.add(
                        acc.at[mine[b], mine[a]], [self.got2[m].at[k] for k in range(size[a] - 1)]
                    )
                if stage == 3:
                    total = acc[mine[b], mine[a], mine["z"]].astype(F32)
                    for k in range(size["z"] - 1):
                        total = total + self.got3[m][k].astype(F32)
                    self.fin[m][core] = total
                    self.swap(m, core).start()
                else:
                    for c in self.hop(stage + 1, m, (a, b)):
                        c.start()

        self.place.by_core(go)

    def end(self):
        def go(core, a, b):
            for m in range(len(self.pieces)):
                for stage in range(1, 4):
                    for c in self.hop(stage, m, (a, b)):
                        c.wait_send()
                self.swap(m, core).wait_send()
                self.swap(m, 1 - core).wait_recv()

        self.place.by_core(go)
        for m, (i, c, w, o, at) in enumerate(self.pieces):
            for side in range(2):
                self.out[o][:, at + side * (w // 2) : at + (side + 1) * (w // 2)] = self.fin[m][side]


class Pace:
    def __init__(self, actions):
        self.todo = sorted(actions, key=lambda a: a[0])
        self.at = {key: t for t, key, _ in actions}

    def until(self, t):
        out = [a[2] for a in self.todo if a[0] <= t]
        self.todo = [a for a in self.todo if a[0] > t]
        return out

    def run(self, t):
        for action in self.until(t):
            action()

    def units(self, start, step, count, gap=0.0, every=1):
        return [self.until(start + u * step + (u // every) * gap) for u in range(count)]

    @staticmethod
    def pick(plan, i):
        for u, actions in enumerate(plan):
            if actions:

                @pl.when(i == u)
                def _(actions=actions):
                    for action in actions:
                        action()


def alone(engine, operands, cid, name):
    def kernel(*refs):
        count, outs = len(operands), len(engine.outs())
        engine.bind(refs[:count], refs[count : count + outs], refs[count + outs :])
        engine.place.greet()
        engine.begin(AHEAD)
        for t in range(engine.steps):
            engine.step(t)
        engine.end()

    space = pl.ANY if isinstance(engine, Gather) else pltpu.VMEM
    return pl.pallas_call(
        kernel,
        out_shape=engine.outs(),
        in_specs=[pl.BlockSpec(memory_space=pl.ANY)] * len(operands),
        out_specs=[pl.BlockSpec(memory_space=space)] * len(engine.outs()),
        scratch_shapes=engine.scratch(),
        compiler_params=pltpu.CompilerParams(
            collective_id=cid, has_side_effects=True, vmem_limit_bytes=VMEM_BYTES
        ),
        name=name,
    )(*operands)


class Beside:
    def __init__(self, engine, points):
        self.engine = engine
        self.points = points

    def reach(self, i, side):
        e = self.engine

        @pl.when((i == 0) & (side == 0))
        def _():
            e.place.greet()
            e.begin(AHEAD)

        for t, p in enumerate(self.points):
            if p is not None:

                @pl.when((i == p // 2) & (side == p % 2))
                def _(t=t):
                    e.step(t)

    def close(self, i):
        e = self.engine

        @pl.when(i == pl.num_programs(0) - 1)
        def _():
            for t, p in enumerate(self.points):
                if p is None:
                    e.step(t)
            e.end()


def paced(engine, first, each, unit, units=12):
    points = []
    for t in range(engine.steps):
        p = int(-(-(first + t * each) // unit))
        points.append(p if p < units else None)
    return points


def attend_beside(body, attn_in, in_specs, attn_out, out_specs, attn_scratch, engine, operands, points, cid, name):
    nin, nout, nscr = len(attn_in), len(attn_out), len(attn_scratch)
    moved, landed = len(operands), len(engine.outs())

    def kernel(*refs):
        at = 0
        groups = []
        for count in (nin, moved, nout, landed, nscr):
            groups.append(refs[at : at + count])
            at += count
        engine.bind(groups[1], groups[3], refs[at:])
        beside = Beside(engine, points)
        i = pl.program_id(0)
        body(*groups[0], *groups[2], *groups[4], at=lambda side: beside.reach(i, side))
        beside.close(i)

    any_ = pl.BlockSpec(memory_space=pl.ANY)
    space = pl.ANY if isinstance(engine, Gather) else pltpu.VMEM
    outs = pl.pallas_call(
        kernel,
        grid=(6,),
        in_specs=in_specs + [any_] * moved,
        out_specs=out_specs + [pl.BlockSpec(memory_space=space)] * landed,
        out_shape=attn_out + engine.outs(),
        scratch_shapes=attn_scratch + engine.scratch(),
        compiler_params=pltpu.CompilerParams(
            collective_id=cid, has_side_effects=True, vmem_limit_bytes=VMEM_BYTES
        ),
        name=name,
    )(*attn_in, *operands)
    return outs[:nout], outs[nout:]


def attn_fwd(live, q, k, v, cols, causal, unit, bq, engine, operands, points, cid, name):
    T, K = q.shape[0], k.shape[0]
    qo, ko, vo = cols
    return attend_beside(
        functools.partial(fwd_kernel, causal=causal, bq=bq, unit=unit),
        [live, q, k, v],
        [
            pl.BlockSpec(memory_space=pltpu.SMEM),
            pl.BlockSpec((T, 128), lambda i: (0, i + qo)),
            pl.BlockSpec((K, 128), lambda i: (0, i + ko)),
            pl.BlockSpec((K, 128), lambda i: (0, i + vo)),
        ],
        [jax.ShapeDtypeStruct((T, D), BF16), jax.ShapeDtypeStruct((6, 2, T), F32)],
        [pl.BlockSpec((T, 128), lambda i: (0, i)), pl.BlockSpec((1, 2, T), lambda i: (i, 0, 0))],
        [pltpu.VMEM((128, K), BF16), pltpu.VMEM((128, T), F32)],
        engine,
        operands,
        points,
        cid,
        name,
    )


def attn_bwd(live, q, k, v, o, do, lse, cols, causal, unit, bq, bk, engine, operands, points, cid, name):
    T, K = q.shape[0], k.shape[0]
    qo, ko, vo = cols
    return attend_beside(
        functools.partial(bwd_kernel, causal=causal, bq=bq, bk=bk, unit=unit),
        [live, q, k, v, o, do, lse],
        [
            pl.BlockSpec(memory_space=pltpu.SMEM),
            pl.BlockSpec((T, 128), lambda i: (0, i + qo)),
            pl.BlockSpec((K, 128), lambda i: (0, i + ko)),
            pl.BlockSpec((K, 128), lambda i: (0, i + vo)),
            pl.BlockSpec((T, 128), lambda i: (0, i)),
            pl.BlockSpec((T, 128), lambda i: (0, i)),
            pl.BlockSpec((1, 2, T), lambda i: (i, 0, 0)),
        ],
        [jax.ShapeDtypeStruct((3, T, D), BF16)],
        [pl.BlockSpec((3, T, 128), lambda i: (0, 0, i))],
        [
            pltpu.VMEM((128, K), BF16),
            pltpu.VMEM((128, T), F32),
            pltpu.VMEM((K, 128), F32),
            pltpu.VMEM((K, 128), F32),
            pltpu.VMEM((2, T), F32),
        ],
        engine,
        operands,
        points,
        cid,
        name,
    )


def finish(sums, halves, plain, scale):
    def kernel(*refs):
        count = len(sums)
        for i, o in zip(refs[:count], refs[count + 3 :]):
            o[...] = i[...] * scale
        width = halves[0].shape[1]
        refs[2 * count + 3][:, :width] = refs[count][...] * scale
        refs[2 * count + 3][:, width:] = refs[count + 1][...] * scale
        refs[2 * count + 4][...] = refs[count + 2][...]

    rows, width = halves[0].shape[0], halves[0].shape[1] + halves[1].shape[1]
    shapes = [s.shape for s in sums] + [(rows, width), plain.shape]
    return pl.pallas_call(
        kernel,
        out_shape=[jax.ShapeDtypeStruct(s, F32) for s in shapes],
        compiler_params=pltpu.CompilerParams(vmem_limit_bytes=VMEM_BYTES),
        name="finish",
    )(*sums, *halves, plain)


def moments(values):
    average = jnp.mean(values, -1, keepdims=True)
    centred = values - average
    variance = jnp.mean(centred * centred, -1, keepdims=True)
    inverse = lax.rsqrt(variance + EPS)
    return centred * inverse, inverse


def norm_back(normal, inverse, gain, grad):
    m = grad * gain
    back = inverse * (
        m - jnp.mean(m, -1, keepdims=True) - normal * jnp.mean(m * normal, -1, keepdims=True)
    )
    return back, jnp.sum(grad * normal, 0), jnp.sum(grad, 0)


GELU_A = 0.7978845608028654
GELU_B = 0.044715


def gelu(u):
    return 0.5 * u * (1.0 + jnp.tanh(GELU_A * (u + GELU_B * u * u * u)))


def gelu_slope(u):
    t = jnp.tanh(GELU_A * (u + GELU_B * u * u * u))
    return 0.5 * (1.0 + t) + 0.5 * u * (1.0 - t * t) * (GELU_A * (1.0 + 3.0 * GELU_B * u * u))


def blocks(rows, step, body, plan=()):
    def go(r, _):
        Pace.pick(plan, r)
        body(pl.ds(pl.multiple_of(r * step, step), step))
        return 0

    lax.fori_loop(0, rows // step, go, 0)


def pair(ref, i, first=0):
    return ref.at[:, pl.ds(pl.multiple_of(first + i * 128, 128), 128)]


def norm_rows(packed):
    count = packed.shape[0]
    own = D // count
    total = None
    for j in range(count):
        r = lax.broadcasted_iota(jnp.int32, (128, D), 0)
        c = lax.broadcasted_iota(jnp.int32, (128, D), 1)
        spot = jnp.where((c == r + own * j) & (r < own), 1.0, 0.0).astype(BF16)
        part = dg(packed[j, :, :128], spot, NN)
        total = part if total is None else total + part
    return total


GATHER_AHEAD = 2
GATHER = dict(first=7.5, rate=3.8, hop=3.5, slack=2.0)


def gather_pace(eng):
    actions = []
    link = 0.0
    for m, (i, _, w) in enumerate(eng.pieces):
        rows = eng.shapes[i][0] * eng.dims[0] * eng.dims[1] * eng.dims[2]
        cost = GATHER["rate"] * rows * w * 2e-6
        slack = GATHER["slack"] if m > 3 else 0.0
        t = GATHER["first"] + link + cost / 2
        if m >= GATHER_AHEAD:
            actions.append((t - cost / 2 - 5.0, ("leave", m), functools.partial(eng.leave, [m])))
        for s, part in enumerate((0.0, 0.33, 0.67)):
            t += (part * cost + GATHER["hop"] + slack) if s else 0.0
            actions.append((t, (s, m), functools.partial(eng.act, [(s, m)])))
        link += cost
    first = min(t for t, key, _ in actions if key == (0, 0))
    actions.append((first - 1e-3, "own", eng.settle))
    pace = Pace(actions)
    return pace, lambda m: pace.at[(2, m)]


def forward_kernel(eng, *refs):
    it = iter(refs)

    def take(count):
        return [next(it) for _ in range(count)]

    clip, frames, tok_in, ctx_in = take(4)
    shards = take(eng.count)
    whole = take(eng.count)
    q1_o, k1_o, v1_o, o1_o, h1_o, x1_o, h2_o, qkv_o, o2_o, x2_o, h3_o, lse1_o, lse2_o, norms_o = take(14)
    tok, ctx, q1, k1, v1, o1, h1, x1, h2, qkv, o2, x2, h3, lse1, lse2, norms = take(16)
    packed, wa, wb, wqkv, vt, ot, isem, wsem, osem = take(9)
    eng.bind(shards, whole, list(it))
    T = tok.shape[0]
    eng.place.greet()
    eng.begin(GATHER_AHEAD)
    pace, ready = gather_pace(eng)
    loads = [pltpu.make_async_copy(ctx_in, ctx, isem.at[0]), pltpu.make_async_copy(tok_in, tok, isem.at[1])]
    for c in loads:
        c.start()
    saves = []

    def save(ref, out):
        c = pltpu.make_async_copy(ref, out, osem.at[len(saves)])
        c.start()
        saves.append(c)

    def fetch(i, pieces, ref):
        eng.arrive(pieces)
        c = pltpu.make_async_copy(whole[i], ref, wsem)
        c.start()
        c.wait()

    def matrix(ref, c=0):
        return ref[:, :, :, :, c : c + D].reshape(D, D)

    clock = ready(0)
    pace.run(clock)
    fetch(0, [0], wa)
    loads[0].wait()

    def keys(r):
        k1[r] = dg(ctx[r], matrix(wa), NN).astype(BF16)

    blocks(T, 256, keys)
    save(k1, k1_o)
    clock = max(clock + 2.5, ready(1))
    pace.run(clock)
    fetch(1, [1], wb)

    def values(r):
        v1[r] = dg(ctx[r], matrix(wb), NN).astype(BF16)

    blocks(T, 256, values)
    save(v1, v1_o)
    clock = max(clock + 2.5, ready(2))
    pace.run(clock)
    fetch(2, [2], packed)
    norms[...] = norm_rows(packed[...].reshape((-1,) + packed.shape[3:]))
    save(norms, norms_o)
    loads[1].wait()

    def first_norm(r):
        normal, _ = moments(tok[r].astype(F32))
        h1[r] = (normal * norms[0:1] + norms[1:2]).astype(BF16)

    blocks(T, 128, first_norm)
    save(h1, h1_o)
    clock = max(clock + 3.5, ready(3))
    pace.run(clock)
    fetch(3, [3], wa)

    def queries(r):
        q1[r] = dg(h1[r], matrix(wa), NN).astype(BF16)

    blocks(T, 256, queries)
    save(q1, q1_o)

    def heads(plan, body):
        def go(i, _):
            for side in range(2):
                Pace.pick(plan[side::2], i)
                body(i, side)
            return 0

        lax.fori_loop(0, 6, go, 0)

    clock += 2.5
    heads(
        pace.units(clock, 2.2, 12),
        lambda i, side: fwd_unit(
            side, frames, pair(q1, i), pair(k1, i), pair(v1, i), pair(o1, i), lse1.at[pl.ds(i, 1)], vt, ot,
            causal=False, bq=512, unit=FRAME_TOK,
        ),
    )
    save(o1, o1_o)
    save(lse1, lse1_o)
    clock = max(clock + 26.4, ready(4), ready(7))
    pace.run(clock)
    fetch(4, [4], wb)
    fetch(5, [5, 6, 7], wqkv)

    def middle(r):
        x = tok[r].astype(F32) + dg(o1[r], matrix(wb), NN)
        x1[r] = x
        normal, _ = moments(x)
        h2[r] = (normal * norms[2:3] + norms[3:4]).astype(BF16)
        for c in range(3):
            qkv[r, c * D : (c + 1) * D] = dg(h2[r], matrix(wqkv, c * D), NN).astype(BF16)

    blocks(T, 256, middle, pace.units(clock, 3.0, 4))
    clock += 12.0
    for ref, out in ((x1, x1_o), (h2, h2_o), (qkv, qkv_o)):
        save(ref, out)
    heads(
        pace.units(clock, 1.5, 12),
        lambda i, side: fwd_unit(
            side, clip, pair(qkv, i), pair(qkv, i, D), pair(qkv, i, 2 * D), pair(o2, i), lse2.at[pl.ds(i, 1)], vt, ot,
            causal=True, bq=512, unit=1,
        ),
    )
    save(o2, o2_o)
    save(lse2, lse2_o)
    clock = max(clock + 18.0, ready(8))
    pace.run(clock)
    fetch(6, [8], wa)

    def late(r):
        x = x1[r] + dg(o2[r], matrix(wa), NN)
        x2[r] = x
        normal, _ = moments(x)
        h3[r] = (normal * norms[4:5] + norms[5:6]).astype(BF16)

    blocks(T, 256, late, pace.units(clock, 1.2, 4))
    save(x2, x2_o)
    save(h3, h3_o)
    pace.run(1e9)
    eng.arrive(range(9, len(eng.pieces)))
    eng.sent()
    for c in saves:
        c.wait()


def forward(clip, frames, tok, ctx, shards, n, cid):
    eng = Gather([s.shape for s in shards], n)
    T = tok.shape[0]
    wide = jax.ShapeDtypeStruct((T, D), BF16)
    full = jax.ShapeDtypeStruct((T, D), F32)
    lse = jax.ShapeDtypeStruct((6, 2, T), F32)
    kept = [wide] * 5 + [full, wide, jax.ShapeDtypeStruct((T, 3 * D), BF16), wide, full, wide, lse, lse]
    kept.append(jax.ShapeDtypeStruct((16, D), F32))
    own = shards[0].shape[0]
    square = pltpu.VMEM(eng.dims + (own, D), BF16)
    any_ = pl.BlockSpec(memory_space=pl.ANY)
    smem = pl.BlockSpec(memory_space=pltpu.SMEM)
    sem = pltpu.SemaphoreType.DMA
    outs = pl.pallas_call(
        functools.partial(forward_kernel, eng),
        out_shape=eng.outs() + kept,
        in_specs=[smem, smem] + [any_] * (2 + eng.count),
        out_specs=[any_] * (eng.count + len(kept)),
        scratch_shapes=[pltpu.VMEM((T, D), BF16)] * 2
        + [pltpu.VMEM(kept[i].shape, kept[i].dtype) for i in (0, 1, 2, 3, 4, 5, 6, 7, 8, 9, 10, 11, 12, 13)]
        + [pltpu.VMEM(eng.dims + shards[2].shape, BF16), square, square]
        + [pltpu.VMEM(eng.dims + (own, 3 * D), BF16), pltpu.VMEM((128, T), BF16), pltpu.VMEM((128, T), F32)]
        + [sem((2,)), sem, sem((16,))]
        + eng.scratch(),
        compiler_params=pltpu.CompilerParams(
            collective_id=cid, has_side_effects=True, vmem_limit_bytes=VMEM_BYTES
        ),
        name="forward",
    )(clip, frames, tok, ctx, *shards)
    return outs[: eng.count], outs[eng.count :]


def back_norm(values, gain, grad):
    normal, inverse = moments(values)
    m = grad * gain
    back = inverse * (
        m - jnp.mean(m, -1, keepdims=True) - normal * jnp.mean(m * normal, -1, keepdims=True)
    )
    return back, jnp.sum(grad * normal, 0, keepdims=True), jnp.sum(grad, 0, keepdims=True)


def mlp_kernel(clip, norms, x2, h3, cot, w_up, w_down, out, dx2, g_up, g_down, g_norm, dz, acc, dh, hid, dup):
    j = pl.program_id(0)
    T = x2.shape[0]

    def live(r):
        at = r.start + lax.broadcasted_iota(jnp.int32, (r.size, 1), 0)
        return at < clip[0]

    @pl.when(j == 0)
    def _():
        def first(r):
            dz[r] = jnp.where(live(r), cot[r], BF16(0))
            acc[r] = jnp.zeros((r.size, D), F32)
            dh[r] = jnp.zeros((r.size, D), F32)

        blocks(T, 256, first)

    up_w, down_w = w_up[...], w_down[...]

    def forth(r):
        u = dg(h3[r], up_w, NN)
        inner = u * (GELU_A + (GELU_A * GELU_B) * (u * u))
        t = jnp.tanh(inner)
        half = 0.5 + 0.5 * t
        hid[r] = (u * half).astype(BF16)
        slope = half + (0.5 * u) * (1.0 - t * t) * (GELU_A + (3.0 * GELU_A * GELU_B) * (u * u))
        dup[r] = (dg(dz[r], down_w, NT) * slope).astype(BF16)
        a = dg(hid[r], down_w, NN)
        b = dg(dup[r], up_w, NT)

        acc[r] += a
        dh[r] += b

    blocks(T, T, forth)
    g_up[...] = dg(h3[...], dup[...], TN).astype(BF16)
    g_down[...] = dg(hid[...], dz[...], TN).astype(BF16)

    @pl.when(j == pl.num_programs(0) - 1)
    def _():
        g_norm[...] = jnp.zeros_like(g_norm)

        def last(r):
            x = x2[r]
            out[r] = jnp.where(live(r), x + acc[r], 0.0).astype(BF16)
            back, gain, bias = back_norm(x, norms[4:5], dh[r])
            dx2[r] = jnp.where(live(r), cot[r].astype(F32), 0.0) + back
            g_norm[0:1] += gain
            g_norm[1:2] += bias

        blocks(T, 128, last)


def mlp(clip, norms, x2, h3, cot, w_up, w_down, step=768):
    T = x2.shape[0]
    FF = w_up.shape[1]

    def still(shape):
        return pl.BlockSpec(shape, lambda j: (0, 0))

    return pl.pallas_call(
        mlp_kernel,
        grid=(FF // step,),
        in_specs=[
            pl.BlockSpec(memory_space=pltpu.SMEM),
            still(norms.shape),
            still((T, D)),
            still((T, D)),
            still((T, D)),
            pl.BlockSpec((D, step), lambda j: (0, j)),
            pl.BlockSpec((step, D), lambda j: (j, 0)),
        ],
        out_specs=[
            still((T, D)),
            still((T, D)),
            pl.BlockSpec((D, step), lambda j: (0, j)),
            pl.BlockSpec((step, D), lambda j: (j, 0)),
            still((8, D)),
        ],
        out_shape=[
            jax.ShapeDtypeStruct((T, D), BF16),
            jax.ShapeDtypeStruct((T, D), F32),
            jax.ShapeDtypeStruct((D, FF), BF16),
            jax.ShapeDtypeStruct((FF, D), BF16),
            jax.ShapeDtypeStruct((8, D), F32),
        ],
        scratch_shapes=[
            pltpu.VMEM((T, D), BF16),
            pltpu.VMEM((T, D), F32),
            pltpu.VMEM((T, D), F32),
            pltpu.VMEM((T, step), BF16),
            pltpu.VMEM((T, step), BF16),
        ],
        compiler_params=pltpu.CompilerParams(vmem_limit_bytes=VMEM_BYTES),
        name="mlp",
    )(clip, norms, x2, h3, cot, w_up, w_down)


def spots(j, own):
    r = lax.broadcasted_iota(jnp.int32, (128, D), 0)
    c = lax.broadcasted_iota(jnp.int32, (128, D), 1)
    return jnp.where((c == r + own * j) & (r < own), 1.0, 0.0).astype(BF16)


def load_all(sems, pairs):
    copies = [pltpu.make_async_copy(s, d, sems.at[k]) for k, (s, d) in enumerate(pairs)]
    for c in copies:
        c.start()
    return copies


def square(ref, c=0):
    return ref[:, :, :, :, c : c + D].reshape(D, D)


SCATTER = dict(first=6.0, rate=3.8, hop=3.5, slack=3.5, lead=5.0)


def scatter_pace(eng, groups):
    actions = []
    link = SCATTER["first"]
    for at, pieces in groups:
        cost = 0.0
        for m in pieces:
            i, _, w, _, _ = eng.pieces[m]
            rows = eng.shapes[i][0] * eng.dims[0] * eng.dims[1] * eng.dims[2]
            cost += SCATTER["rate"] * rows * w * 2e-6
        link = max(link, at)
        t = max(link - SCATTER["lead"], at + 2.0)
        for s, part in enumerate((0.0, 0.67, 0.33, 0.25)):
            if s == 1:
                t = link
            t += (part * cost + SCATTER["hop"] + SCATTER["slack"]) if s else 0.0
            actions.append((t, (s, pieces[0]), functools.partial(eng.act, [(s, m) for m in pieces])))
        link += cost
    return Pace(actions)


def causal_kernel(eng, *refs):
    it = iter(refs)

    def take(count):
        return [next(it) for _ in range(count)]

    clip, dx2_in, x1_in, qkv_in, o2_in, h2_in, lse, norms, wp_in, wqkv_in = take(10)
    grads = take(eng.count)
    sums = take(len(eng.outs()))
    dx1_o, gp_o, gqkv_o, gnorm = take(4)
    dx, x1, qkv, o2, h2, wp, wqkv, dy, do, dqkv, gp, gqkv, kt, dqt, dka, dva, dl, isem, osem = take(19)
    eng.bind(grads, sums, list(it))
    T = dx.shape[0]
    eng.place.greet()
    eng.begin()
    loads = load_all(
        isem,
        [(dx2_in, dx), (wp_in, wp), (o2_in, o2), (qkv_in, qkv), (x1_in, x1), (h2_in, h2), (wqkv_in, wqkv)],
    )
    loads[0].wait()
    loads[1].wait()

    def first(r):
        dy[r] = dx[r].astype(BF16)
        do[r] = dg(dy[r], square(wp), NT).astype(BF16)

    pace = scatter_pace(eng, [(0.0, [m]) for m in range(len(eng.pieces))])
    blocks(T, 256, first)
    pace.run(6.0)
    loads[2].wait()

    def weight(left, right, out, c, step=256):
        def go(k, _):
            at = pl.multiple_of(k * step, step)
            g = dg(left[...], right[:, pl.ds(at, step)], TN).astype(BF16)
            out[:, :, :, :, pl.ds(c + at, step)] = g.reshape(out.shape[:4] + (step,))
            return 0

        lax.fori_loop(0, D // step, go, 0)

    weight(o2, dy, gp, 0)
    saves = [pltpu.make_async_copy(gp, gp_o, osem.at[0])]
    saves[0].start()
    loads[3].wait()
    plan = pace.units(9.0, 2.5, 12)

    def unit_of(i, side):
        u = 2 * i + side
        Pace.pick(plan[side::2], i)
        cols = pl.ds(pl.multiple_of(i * 128, 128), 128)
        bwd_unit(
            side, clip, pair(qkv, i), pair(qkv, i, D), pair(qkv, i, 2 * D), pair(o2, i), pair(do, i),
            lse.at[pl.ds(i, 1)], dqkv.at[:, :, cols], kt, dqt, dka, dva, dl,
            causal=True, bq=256, bk=512, unit=1,
        )

    def heads(i, _):
        unit_of(i, 0)
        unit_of(i, 1)
        return 0

    lax.fori_loop(0, 6, heads, 0)
    for c in loads[4:]:
        c.wait()
    gnorm[...] = jnp.zeros_like(gnorm)

    def back(r):
        dh = sum(dg(dqkv[c, r], square(wqkv, c * D), NT) for c in range(3))
        g, gain, bias = back_norm(x1[r], norms[2:3], dh)
        dx[r] += g
        gnorm[0:1] += gain
        gnorm[1:2] += bias

    blocks(T, 256, back, pace.units(39.0, 1.7, 4))
    saves.append(pltpu.make_async_copy(dx, dx1_o, osem.at[1]))
    saves[1].start()
    for c in range(3):
        pace.run(46.0 + 2.0 * c)
        weight(h2, dqkv.at[c], gqkv, c * D)
    saves.append(pltpu.make_async_copy(gqkv, gqkv_o, osem.at[2]))
    saves[2].start()
    pace.run(1e9)
    eng.end()
    for c in saves:
        c.wait()


def causal_back(clip, dx2, x1, qkv, o2, h2, lse, norms, wp, wqkv, grads, targets, n, cid):
    pieces = [(0, c * 256, 256) for c in range(3)] + [(1, c * D, D) for c in range(grads[1].shape[4] // D // 2)]
    eng = Scatter([a.shape[3:] for a in grads], targets, n, pieces=pieces)
    T = dx2.shape[0]
    own = wp.shape[3]
    any_ = pl.BlockSpec(memory_space=pl.ANY)
    smem = pl.BlockSpec(memory_space=pltpu.SMEM)
    vmem = pl.BlockSpec(memory_space=pltpu.VMEM)
    sem = pltpu.SemaphoreType.DMA
    small = jax.ShapeDtypeStruct((8, D), F32)
    one, three = eng.dims + (own, D), eng.dims + (own, 3 * D)

    def vm(shape, dtype=BF16):
        return pltpu.VMEM(shape, dtype)

    sums = eng.outs()
    outs = pl.pallas_call(
        functools.partial(causal_kernel, eng),
        out_shape=sums
        + [jax.ShapeDtypeStruct((T, D), F32), jax.ShapeDtypeStruct(one, BF16), jax.ShapeDtypeStruct(three, BF16), small],
        in_specs=[smem] + [any_] * 5 + [vmem] * 2 + [any_] * (2 + eng.count),
        out_specs=[vmem] * len(sums) + [any_] * 3 + [vmem],
        scratch_shapes=[
            vm((T, D), F32),
            vm((T, D), F32),
            vm((T, 3 * D)),
            vm((T, D)),
            vm((T, D)),
            vm(one),
            vm(three),
            vm((T, D)),
            vm((T, D)),
            vm((3, T, D)),
            vm(one),
            vm(three),
            vm((128, T)),
            vm((128, T), F32),
            vm((T, 128), F32),
            vm((T, 128), F32),
            vm((2, T), F32),
            sem((7,)),
            sem((3,)),
        ]
        + eng.scratch(),
        compiler_params=pltpu.CompilerParams(
            collective_id=cid, has_side_effects=True, vmem_limit_bytes=VMEM_BYTES
        ),
        name="causal_back",
    )(clip, dx2, x1, qkv, o2, h2, lse, norms, wp, wqkv, *grads)
    return outs[: len(sums)], outs[len(sums) :]


def cross_kernel(eng, *refs):
    it = iter(refs)

    def take(count):
        return [next(it) for _ in range(count)]

    frames, dx1_in, tok_in, ctx_in, q1_in, k1_in, v1_in, o1_in, h1_in, lse, norms, gnorm2, gnorm3, wo_in, wq_in = take(15)
    given = take(3)
    sums = take(len(eng.outs()))
    (grad_o,) = take(1)
    dx, tok, ctx, q1, k1, v1, o1, h1, wo, wq, dy, do, dqkv, kt, dqt, dka, dva, dl, gsum, isem, osem = take(21)
    go_, gv, gk, gq, gn = take(5)
    eng.bind(list(given[:2]) + [go_, gv, gk, gq, gn, given[2]], sums, list(it))
    T = dx.shape[0]
    n = gn.shape[0] * gn.shape[1] * gn.shape[2]
    own = D // n
    eng.place.greet()
    eng.begin()
    loads = load_all(
        isem,
        [(dx1_in, dx), (wo_in, wo), (o1_in, o1), (q1_in, q1), (k1_in, k1), (v1_in, v1), (h1_in, h1), (ctx_in, ctx),
         (wq_in, wq), (tok_in, tok)],
    )
    loads[0].wait()
    loads[1].wait()

    def first(r):
        dy[r] = dx[r].astype(BF16)
        do[r] = dg(dy[r], square(wo), NT).astype(BF16)

    blocks(T, 256, first)
    loads[2].wait()

    def weight(left, right, out, at, width=256):
        g = dg(left[...], right[:, pl.ds(at, width)], TN).astype(BF16)
        out[:, :, :, :, pl.ds(at, width)] = g.reshape(out.shape[:4] + (width,))

    def whole(k, _):
        weight(o1, dy, go_, pl.multiple_of(k * 256, 256))
        return 0

    lax.fori_loop(0, 3, whole, 0)
    eng.put([4])
    for c in loads[3:]:
        c.wait()
    third = [[5 + g, 8 + g, 11 + g] for g in range(3)]
    start, unit, gap = 9.0, 3.05, 3.0
    made = [start + 4 * (g + 1) * unit + (g + 1) * gap for g in range(3)]
    pace = scatter_pace(
        eng,
        [(0.0, [m]) for m in [0, *range(15, len(eng.pieces)), 1, 2, 3]]
        + [(start, [4])]
        + [(made[g], third[g]) for g in range(3)]
        + [(made[2] + 6.0, [14])],
    )
    plan = pace.units(start, unit, 12, gap, 4)

    def unit_of(i, side):
        u = 2 * i + side
        Pace.pick(plan[side::2], i)
        cols = pl.ds(pl.multiple_of(i * 128, 128), 128)
        bwd_unit(
            side, frames, pair(q1, i), pair(k1, i), pair(v1, i), pair(o1, i), pair(do, i),
            lse.at[pl.ds(i, 1)], dqkv.at[:, :, cols], kt, dqt, dka, dva, dl,
            causal=False, bq=1024, bk=256, unit=FRAME_TOK,
        )

        if side == 0:
            return

        @pl.when(lax.rem(u, 4) == 3)
        def _():
            c = pl.multiple_of(lax.div(u, 4) * 256, 256)
            weight(ctx, dqkv.at[2], gv, c)
            weight(ctx, dqkv.at[1], gk, c)
            weight(h1, dqkv.at[0], gq, c)

        for g in range(3):
            pl.when(u == 4 * g + 3)(functools.partial(eng.put, third[g]))

    def heads(i, _):
        unit_of(i, 0)
        unit_of(i, 1)
        return 0

    lax.fori_loop(0, 6, heads, 0)
    gsum[...] = jnp.zeros_like(gsum)
    gsum[2:4] = gnorm2[0:2]
    gsum[4:6] = gnorm3[0:2]
    pace.run(made[2])

    def back(r):
        dh = dg(dqkv[0, r], square(wq), NT)
        g, gain, bias = back_norm(tok[r].astype(F32), norms[0:1], dh)
        dx[r] += g
        gsum[0:1] += gain
        gsum[1:2] += bias

    blocks(T, 256, back, pace.units(made[2] + 1.0, 1.2, 4))
    save = pltpu.make_async_copy(dx, grad_o, osem)
    save.start()
    pace.run(made[2] + 5.5)
    rows = gsum[...].astype(BF16)
    Z, Y, X = gn.shape[:3]
    for j in range(n):
        z, y, x = j // (Y * X), (j // X) % Y, j % X
        gn[z, y, x, :, :128] = dg(rows, spots(j, own), NT).astype(BF16)
        gn[z, y, x, :, 128:] = jnp.zeros((16, 128), BF16)
    eng.put([14])
    pace.run(1e9)
    eng.end()
    save.wait()


def cross_back(
    frames, dx1, tok, ctx, q1, k1, v1, o1, h1, lse, norms, gnorm2, gnorm3, wo, wq, gp, gqkv, gup, n, cid
):
    own = wo.shape[3]
    one = gp.shape
    shapes = [gp.shape[3:], gqkv.shape[3:], one[3:], one[3:], one[3:], one[3:], (16, 256), gup.shape[3:]]
    FF = gup.shape[4]
    pieces = [(0, 0, D)] + [(1, c * D, D) for c in range(3)] + [(2, 0, D)]
    pieces += [(i, c * 256, 256) for i in (3, 4, 5) for c in range(3)] + [(6, 0, 256)]
    pieces += [(7, c * D, D) for c in range(FF // D // 2, FF // D)]
    targets = [(6, 0), (5, 0), (4, 0), (3, 0), (2, 0), (1, 0), (0, 0), (7, -(FF // D // 2) * D)]
    eng = Scatter(shapes, targets, n, made=(2, 3, 4, 5, 6), pieces=pieces)
    T = dx1.shape[0]
    any_ = pl.BlockSpec(memory_space=pl.ANY)
    smem = pl.BlockSpec(memory_space=pltpu.SMEM)
    vmem = pl.BlockSpec(memory_space=pltpu.VMEM)
    sem = pltpu.SemaphoreType.DMA

    def vm(shape, dtype=BF16):
        return pltpu.VMEM(shape, dtype)

    sums = eng.outs()
    outs = pl.pallas_call(
        functools.partial(cross_kernel, eng),
        out_shape=sums + [jax.ShapeDtypeStruct((T, D), F32)],
        in_specs=[smem] + [any_] * 8 + [vmem] * 4 + [any_] * 5,
        out_specs=[vmem] * len(sums) + [any_],
        scratch_shapes=[vm((T, D), F32)]
        + [vm((T, D))] * 7
        + [vm(one)] * 2
        + [vm((T, D))] * 2
        + [vm((3, T, D)), vm((128, T)), vm((128, T), F32), vm((T, 128), F32), vm((T, 128), F32), vm((2, T), F32), vm((16, D), F32)]
        + [sem((10,)), sem]
        + [vm(one)] * 4
        + [vm(one[:3] + (16, 256))]
        + eng.scratch(),
        compiler_params=pltpu.CompilerParams(
            collective_id=cid, has_side_effects=True, vmem_limit_bytes=VMEM_BYTES
        ),
        name="cross_back",
    )(frames, dx1, tok, ctx, q1, k1, v1, o1, h1, lse, norms, gnorm2, gnorm3, wo, wq, gp, gqkv, gup)
    return outs[: len(sums)], outs[len(sums)]


def shards(
    tokens,
    context,
    clip_lengths,
    context_frames,
    norm1_gain,
    norm1_bias,
    cross_q,
    cross_k,
    cross_v,
    cross_out,
    norm2_gain,
    norm2_bias,
    attn_qkv,
    attn_out,
    norm3_gain,
    norm3_bias,
    mlp_up,
    mlp_down,
    cotangent,
):
    n = lax.axis_size("fsdp")
    stream_in = tokens[0].astype(F32)
    context_rows = context[0]
    slot_rows = stream_in.shape[0]
    own = norm1_gain.shape[0]
    padding = (jnp.arange(slot_rows) < clip_lengths[0])[:, None]
    norms = jnp.stack([norm1_gain, norm1_bias, norm2_gain, norm2_bias, norm3_gain, norm3_bias])
    norms = jnp.pad(norms, ((0, 10), (0, 256 - own)))

    def flat(arrays):
        return [a.reshape(-1, a.shape[4]) for a in arrays]

    def gather(arrays):
        return Gather([a.shape for a in arrays], n), arrays

    def weight(left, right):
        g = dg(left, right, TN).astype(BF16)
        return g.reshape(n, -1, g.shape[1])

    def scatter(grads):
        arrays = [g.reshape(grid_of(n) + g.shape[1:]) for g, _ in grads]
        return Scatter([a.shape[3:] for a in arrays], [t for _, t in grads], n), arrays

    if own % 16 == 0:
        whole, kept = forward(
            clip_lengths,
            context_frames,
            tokens[0],
            context_rows,
            [cross_k, cross_v, norms, cross_q, cross_out, attn_qkv, attn_out, mlp_up, mlp_down],
            n,
            0,
        )
        _, _, _, w_q, w_o, w_qkv, w_p, w_up, w_down = whole
        q1, k1, v1, o1, h1, x1, h2, qkv, o2, x2, h3, lse1, lse2, norms = kept
        block_out, dx2, g_up, g_down, g_norm3 = mlp(
            clip_lengths, norms, x2, h3, cotangent[0], *flat([w_up, w_down])
        )
        grads = [g_down.reshape(w_down.shape), g_up.reshape(w_up.shape)]
        (s_up, s_down), (dx1, g_p, g_qkv, g_norm2) = causal_back(
            clip_lengths, dx2, x1, qkv, o2, h2, lse2, norms, w_p, w_qkv, grads, [(1, 0), (0, 0)], n, 1
        )
        (s_norms, s_q, s_k, s_v, s_o, s_qkv, s_p, s_up2), input_grad = cross_back(
            context_frames, dx1, tokens[0], context_rows, q1, k1, v1, o1, h1, lse1, norms, g_norm2, g_norm3,
            w_o, w_q, g_p, g_qkv, grads[1], n, 2
        )
    else:
        first, operands = gather([norms, cross_q, cross_k, cross_v])
        norms, *whole = alone(first, operands, 0, "gather_cross")
        w_q, w_k, w_v = flat(whole)
        norms = norms.reshape((n,) + norms.shape[3:])[:, :6, :own].transpose(1, 0, 2).reshape(6, D).astype(F32)
        gain_one, bias_one, gain_two, bias_two, gain_three, bias_three = [norms[i] for i in range(6)]

        normal_one, inverse_one = moments(stream_in)
        h1 = (normal_one * gain_one + bias_one).astype(BF16)
        q1 = dg(h1, w_q, NN).astype(BF16)
        k1 = dg(context_rows, w_k, NN).astype(BF16)
        v1 = dg(context_rows, w_v, NN).astype(BF16)
        second, operands = gather([cross_out, attn_qkv, attn_out])
        (o1, lse1), whole = attn_fwd(
            context_frames, q1, k1, v1, (0, 0, 0), False, FRAME_TOK, 512,
            second, operands, paced(second, 8.0, 4.8, 2.2), 1, "cross_fwd",
        )
        w_o, w_qkv, w_p = flat(whole)
        x1 = stream_in + dg(o1, w_o, NN)
        normal_two, inverse_two = moments(x1)
        h2 = (normal_two * gain_two + bias_two).astype(BF16)
        qkv = dg(h2, w_qkv, NN).astype(BF16)
        third, operands = gather([mlp_up, mlp_down])
        (o2, lse2), whole = attn_fwd(
            clip_lengths, qkv, qkv, qkv, (0, 6, 12), True, 1, 512,
            third, operands, paced(third, 8.0, 4.8, 1.5), 2, "causal_fwd",
        )
        w_up, w_down = flat(whole)
        x2 = x1 + dg(o2, w_p, NN)
        normal_three, inverse_three = moments(x2)
        h3 = (normal_three * gain_three + bias_three).astype(BF16)
        up = dg(h3, w_up, NN)
        hidden = gelu(up).astype(BF16)
        x3 = x2 + dg(hidden, w_down, NN)
        block_out = jnp.where(padding, x3, 0.0).astype(BF16)

        dx3 = jnp.where(padding, cotangent[0].astype(F32), 0.0)
        dz = dx3.astype(BF16)
        dup = (dg(dz, w_down, NT) * gelu_slope(up)).astype(BF16)
        back, g_gain3, g_bias3 = norm_back(normal_three, inverse_three, gain_three, dg(dup, w_up, NT))
        dx2 = dx3 + back
        dy2 = dx2.astype(BF16)
        do2 = dg(dy2, w_p, NT).astype(BF16)
        fourth, operands = scatter([(weight(hidden, dz), (1, 0)), (weight(h3, dup), (0, 0))])
        (dqkv,), (s_up, s_down) = attn_bwd(
            clip_lengths, qkv, qkv, qkv, o2, do2, lse2, (0, 6, 12), True, 1, 256, 512,
            fourth, operands, paced(fourth, 8.0, 4.8, 2.45), 3, "causal_bwd",
        )
        dh2 = sum(dg(dqkv[c], w_qkv[:, c * D : (c + 1) * D], NT) for c in range(3))
        back, g_gain2, g_bias2 = norm_back(normal_two, inverse_two, gain_two, dh2)
        dx1 = dx2 + back
        dy1 = dx1.astype(BF16)
        do1 = dg(dy1, w_o, NT).astype(BF16)
        fifth, operands = scatter(
            [(weight(o2, dy2), (0, 0))]
            + [(weight(h2, dqkv[c]), (1, c * D)) for c in range(3)]
            + [(weight(o1, dy1), (2, 0))]
        )
        (dqkv1,), (s_p, s_qkv, s_o) = attn_bwd(
            context_frames, q1, k1, v1, o1, do1, lse1, (0, 0, 0), False, FRAME_TOK, 1024, 256,
            fifth, operands, paced(fifth, 8.0, 4.8, 3.1), 4, "cross_bwd",
        )
        dh1 = dg(dqkv1[0], w_q, NT)
        back, g_gain1, g_bias1 = norm_back(normal_one, inverse_one, gain_one, dh1)
        input_grad = dx1 + back

        g_norms = jnp.stack([g_gain1, g_bias1, g_gain2, g_bias2, g_gain3, g_bias3]).astype(BF16)
        g_norms = jnp.pad(g_norms.reshape(6, n, own).transpose(1, 0, 2), ((0, 0), (0, 10), (0, 256 - own)))

        sixth, operands = scatter(
            [
                (weight(context_rows, dqkv1[2]), (3, 0)),
                (weight(context_rows, dqkv1[1]), (2, 0)),
                (weight(h1, dqkv1[0]), (1, 0)),
                (g_norms, (0, 0)),
            ]
        )
        s_norms, s_q, s_k, s_v = alone(sixth, operands, 5, "scatter_cross")
    scale = (slot_rows * tokens.shape[0] * n * lax.axis_size("rep")) ** (-0.5)
    vec = [s_norms[i, :own] * scale for i in range(6)]
    halves = (s_up, s_up2) if own % 16 == 0 else jnp.split(s_up, 2, axis=1)
    *done, s_up, input_grad = finish([s_q, s_k, s_v, s_o, s_qkv, s_p, s_down], halves, input_grad, scale)
    done = [None, *done[:6], s_up, done[6]]
    return (
        block_out[None],
        input_grad[None],
        vec[0],
        vec[1],
        done[1],
        done[2],
        done[3],
        done[4],
        vec[2],
        vec[3],
        done[5],
        done[6],
        vec[4],
        vec[5],
        done[7],
        done[8],
    )


def solution(mesh):
    in_specs = (
        P(("fsdp", "rep"), None, None),
        P(("fsdp", "rep"), None, None),
        P(("fsdp", "rep")),
        P(("fsdp", "rep")),
        P("fsdp"),
        P("fsdp"),
        P("fsdp", None),
        P("fsdp", None),
        P("fsdp", None),
        P("fsdp", None),
        P("fsdp"),
        P("fsdp"),
        P("fsdp", None),
        P("fsdp", None),
        P("fsdp"),
        P("fsdp"),
        P("fsdp", None),
        P("fsdp", None),
        P(("fsdp", "rep"), None, None),
    )
    out_specs = (
        P(("fsdp", "rep"), None, None),
        P(("fsdp", "rep"), None, None),
        P("fsdp"),
        P("fsdp"),
        P("fsdp", None),
        P("fsdp", None),
        P("fsdp", None),
        P("fsdp", None),
        P("fsdp"),
        P("fsdp"),
        P("fsdp", None),
        P("fsdp", None),
        P("fsdp"),
        P("fsdp"),
        P("fsdp", None),
        P("fsdp", None),
    )
    return jax.shard_map(shards, mesh=mesh, in_specs=in_specs, out_specs=out_specs, check_vma=False)
```

```python
import functools

import jax
import jax.numpy as jnp
from jax import lax
from jax.experimental import pallas as pl
from jax.experimental.pallas import tpu as pltpu
from jax.sharding import PartitionSpec as P

D = 768
FRAME_TOK = 256
EPS = 1e-05
MESH = pl.DeviceIdType.MESH
VMEM_BYTES = 58 << 20

F32, BF16 = jnp.float32, jnp.bfloat16
NN = (((1,), (0,)), ((), ()))
NT = (((1,), (1,)), ((), ()))
TN = (((0,), (0,)), ((), ()))
def dg(a, b, dims): return lax.dot_general(a, b, dims, preferred_element_type=F32)

def lanes_of(side):
    lane = lax.broadcasted_iota(jnp.int32, (1, 128), 1)
    return (lane >= 64 * side) & (lane < 64 * side + 64), lane == 64 * (1 - side)


def head_sides(side, q2, k2, bias):
    mine, extra = lanes_of(side)
    qa = jnp.where(mine, q2, jnp.where(extra, 1.0, 0.0).astype(BF16))
    ka = jnp.where(mine, k2, jnp.where(extra, bias, 0.0).astype(BF16))
    return qa, ka


def key_bias(n_ref, unit, K):
    live = n_ref[0] * unit
    return jnp.where(lax.broadcasted_iota(jnp.int32, (K, 1), 0) < live, 0.0, -1e30).astype(F32)


def fwd_unit(side, n_ref, q_ref, k_ref, v_ref, o_ref, l_ref, vt, ot, *, causal, bq, unit):
    T, K = q_ref.shape[0], k_ref.shape[0]

    @pl.when(side == 0)
    def _():
        vt[...] = v_ref[...].T

    qa, ka = head_sides(side, q_ref[...] * BF16(0.125), k_ref[...], key_bias(n_ref, unit, K))
    rows = pl.ds(pl.multiple_of(side * 64, 64), 64)
    for j in range(T // bq):
        span = (j + 1) * bq if causal else K
        s = dg(ka[:span], qa[j * bq : (j + 1) * bq], NT)
        if causal:
            top = j * bq
            ok = lax.broadcasted_iota(jnp.int32, (bq, bq), 0) <= lax.broadcasted_iota(
                jnp.int32, (bq, bq), 1
            )
            diag = jnp.where(ok, s[top:], -1e30)
            s = diag if top == 0 else jnp.concatenate([s[:top], diag], 0)
        m = jnp.max(s, 0, keepdims=True)
        p = jnp.exp(s - m)
        l = jnp.sum(p, 0, keepdims=True)
        ot[rows, j * bq : (j + 1) * bq] = dg(vt[rows, :span], p.astype(BF16), NN) * (1.0 / l)
        l_ref[0, pl.ds(side, 1), j * bq : (j + 1) * bq] = m + jnp.log(l)

    @pl.when(side == 1)
    def _():
        o_ref[...] = ot[...].T.astype(BF16)


def fwd_kernel(*refs, causal, bq, unit, at):
    def go(side, _):
        at(side)
        fwd_unit(side, *refs, causal=causal, bq=bq, unit=unit)
        return 0

    lax.fori_loop(0, 2, go, 0)


def bwd_unit(
    side, n_ref, q_ref, k_ref, v_ref, o_ref, do_ref, l_ref, g_ref, kt, dqt, dka, dva, dl, *, causal, bq, bk, unit
):
    T, K = q_ref.shape[0], k_ref.shape[0]

    @pl.when(side == 0)
    def _():
        kt[...] = k_ref[...].T
        prod = (do_ref[...].astype(F32) * o_ref[...].astype(F32)).T
        dl[0:1] = jnp.sum(prod[:64], 0, keepdims=True)
        dl[1:2] = jnp.sum(prod[64:], 0, keepdims=True)

    q2 = q_ref[...] * BF16(0.125)
    do2 = do_ref[...]
    qa, ka = head_sides(side, q2, k_ref[...], key_bias(n_ref, unit, K))
    va = jnp.where(lanes_of(side)[0], v_ref[...], BF16(0))
    low = lax.broadcasted_iota(jnp.int32, (1, 128), 1) < 64
    delta = dl[pl.ds(side, 1), :]
    lse = l_ref[0, pl.ds(side, 1), :]
    half = pl.ds(pl.multiple_of(side * 64, 64), 64)
    for i in range(K // bk):
        dk = dv = None
        kb, vb = ka[i * bk : (i + 1) * bk], va[i * bk : (i + 1) * bk]
        for j in range(T // bq):
            if causal and (j + 1) * bq <= i * bk:
                continue
            cols = slice(j * bq, (j + 1) * bq)
            p = jnp.exp(dg(kb, qa[cols], NT) - lse[:, cols])
            if causal and j * bq < (i + 1) * bk:
                ok = i * bk + lax.broadcasted_iota(
                    jnp.int32, (bk, bq), 0
                ) <= j * bq + lax.broadcasted_iota(jnp.int32, (bk, bq), 1)
                p = jnp.where(ok, p, 0.0)
            dp = dg(vb, do2[cols], NT)
            ds = (p * (dp - delta[:, cols])).astype(BF16)
            a = dg(p.astype(BF16), do2[cols], NN)
            b = dg(ds, q2[cols], NN)
            dv = a if dv is None else dv + a
            dk = b if dk is None else dk + b
            c = dg(kt[half, i * bk : (i + 1) * bk], ds, NN)
            if i == 0:
                dqt[half, cols] = c
            else:
                dqt[half, cols] += c
        rows = slice(i * bk, (i + 1) * bk)

        @pl.when(side == 0)
        def _(rows=rows, dk=dk, dv=dv):
            dka[rows] = dk
            dva[rows] = dv

        @pl.when(side == 1)
        def _(rows=rows, dk=dk, dv=dv):
            g_ref[1, rows, :] = jnp.where(low, dka[rows], dk).astype(BF16)
            g_ref[2, rows, :] = jnp.where(low, dva[rows], dv).astype(BF16)

    @pl.when(side == 1)
    def _():
        g_ref[0] = (dqt[...] * 0.125).T.astype(BF16)


def bwd_kernel(*refs, causal, bq, bk, unit, at):
    def go(side, _):
        at(side)
        bwd_unit(side, *refs, causal=causal, bq=bq, bk=bk, unit=unit)
        return 0

    lax.fori_loop(0, 2, go, 0)


def grid_of(n):
    if n == 16:
        return 4, 2, 2
    if n == 64:
        return 4, 4, 4
    return n, 1, 1


def cut(shapes):
    out = []
    for i, (rows, cols) in enumerate(shapes):
        step = 256 if rows > cols // 8 and cols == 768 else min(cols, 768)
        out += [(i, c, step) for c in range(0, cols, step)]
    return out


def remote(src, dst, send, recv, dev):
    return pltpu.make_async_remote_copy(
        src_ref=src, dst_ref=dst, send_sem=send, recv_sem=recv, device_id=dev, device_id_type=MESH
    )


class Place:
    def __init__(self, dims):
        self.dims = dims
        self.size = dict(zip("zyx", dims))
        Z, Y, X = dims
        self.me = lax.axis_index("fsdp")
        self.core = lax.axis_index("rep")
        self.mine = {"z": self.me // (Y * X), "y": (self.me // X) % Y, "x": self.me % X}
        if Y == X:
            y, x = self.mine["y"], self.mine["x"]
            self.size.update(a=X, b=Y)
            self.mine.update(a=self.choose(x, y), b=self.choose(y, x))

    def here(self, axis):
        return {k: self.mine[k] for k in ("zab" if axis in "ab" else "zyx")}

    def peers(self, axis):
        mine, count = self.mine[axis], self.size[axis]
        out = []
        for k in range(1, count):
            at = self.here(axis)
            at[axis] = (mine + k) % count
            y, x = self.plane(at)
            dev = ((at["z"] * self.size["y"] + y) * self.size["x"] + x, self.core)
            out.append((at[axis], (mine + count - k) % count, dev))
        return out

    def sibling(self):
        return (self.me, 1 - self.core)

    def greet(self):
        bar = pltpu.get_barrier_semaphore()
        devs = [d for axis in "zyx" for _, _, d in self.peers(axis)] + [self.sibling()]
        for d in devs:
            pl.semaphore_signal(bar, inc=1, device_id=d, device_id_type=MESH)
        pl.semaphore_wait(bar, len(devs))

    def by_core(self, action):
        if self.size["y"] == self.size["x"]:
            action(self.core, "a", "b")
            return

        @pl.when(self.core == 0)
        def _():
            action(0, "x", "y")

        @pl.when(self.core == 1)
        def _():
            action(1, "y", "x")

    def choose(self, first, second):
        return first + self.core * (second - first)

    def plane(self, at):
        if "a" in at:
            return self.choose(at["b"], at["a"]), self.choose(at["a"], at["b"])
        return at["y"], at["x"]


AHEAD = 3


class Gather:
    def __init__(self, shapes, n):
        self.dims = grid_of(n)
        self.pieces = cut(shapes)
        self.count = len(shapes)
        self.shapes = shapes
        self.steps = len(self.pieces) + 2

    def outs(self):
        return [jax.ShapeDtypeStruct(self.dims + tuple(s), BF16) for s in self.shapes]

    def scratch(self):
        Z, Y, X = self.dims
        M, z, s = len(self.pieces), max(self.dims[0] - 1, 1), max(Y - 1, X - 1, 1)
        t = s * max(Y, X)
        sem = pltpu.SemaphoreType.DMA
        return [sem((2, self.count))] + [sem((M, c)) for c in (z, z, s, s, t, t, z, z, s, s, t, t)]

    def bind(self, shards, outs, scratch):
        self.shards, self.out = shards, outs
        self.own, *self.sem = scratch
        self.place = Place(self.dims)

    def half(self, m, side):
        _, c, w = self.pieces[m]
        return pl.ds(pl.multiple_of(c + side * (w // 2), w // 2), w // 2)

    def view(self, m, side, z, y, x):
        return self.out[self.pieces[m][0]].at[slice(None) if z is None else z, y, x, :, self.half(m, side)]

    def hop(self, stage, m, side, axes, coming):
        a, b = axes
        axis = ("z", a, b)[stage]
        out = []
        for k, (_, frm, dev) in enumerate(self.place.peers(axis)):
            at = self.place.here(a)
            if stage:
                at["z"] = None
            if coming:
                at[axis] = frm
            for e in range(self.place.size[a] if stage == 2 else 1):
                if stage == 2:
                    at = {**at, a: e}
                y, x = self.place.plane(at)
                v = self.view(m, side, at["z"], y, x)
                src = v
                if stage == 0 and not coming:
                    src = self.shards[self.pieces[m][0]].at[:, self.half(m, side)]
                s, r = self.sem[2 * stage : 2 * stage + 2]
                slot = k * self.place.size[a] + e if stage == 2 else k
                out.append(
                    (
                        slot,
                        (at["z"], y, x),
                        lambda v=v, src=src, s=s, r=r, slot=slot, dev=dev: remote(
                            src, v, s.at[m, slot], r.at[m, slot], dev
                        ),
                    )
                )
        return out

    def give(self, stage, m, side, at, k):
        v = self.view(m, side, *at)
        s, r = self.sem[6 + 2 * stage : 8 + 2 * stage]
        return remote(v, v, s.at[m, k], r.at[m, k], self.place.sibling())

    def own_copies(self):
        p = self.place.mine
        return [
            remote(s, o.at[p["z"], p["y"], p["x"]], self.own.at[0, i], self.own.at[1, i], self.place.sibling())
            for i, (s, o) in enumerate(zip(self.shards, self.out))
        ]

    def begin(self, ahead):
        for c in self.own_copies():
            c.start()
        self.leave(range(min(ahead, len(self.pieces))))

    def leave(self, pieces):
        def go(core, a, b):
            for m in pieces:
                for _, _, c in self.hop(0, m, core, (a, b), False):
                    c().start()

        self.place.by_core(go)

    def settle(self):
        for c in self.own_copies():
            c.wait()

    def act(self, pairs):
        def go(core, a, b):
            for stage, m in pairs:
                came = self.hop(stage, m, core, (a, b), True)
                for _, _, c in came:
                    c().wait_recv()
                if stage < 2:
                    for _, _, c in self.hop(stage + 1, m, core, (a, b), False):
                        c().start()
                for k, at, _ in came:
                    self.give(stage, m, core, at, k).start()

        self.place.by_core(go)

    def step(self, t):
        if t == 0:
            self.settle()
        if t + AHEAD < len(self.pieces):
            self.leave([t + AHEAD])
        self.act([(s, t - s) for s in range(3) if 0 <= t - s < len(self.pieces)])

    def arrive(self, pieces):
        def go(core, a, b):
            for m in pieces:
                for stage in range(3):
                    for k, at, _ in self.hop(stage, m, core, (b, a), True):
                        self.give(stage, m, 1 - core, at, k).wait_recv()

        self.place.by_core(go)

    def sent(self):
        def go(core, a, b):
            for m in range(len(self.pieces)):
                for stage in range(3):
                    for _, _, c in self.hop(stage, m, core, (a, b), False):
                        c().wait_send()
                    for k, at, _ in self.hop(stage, m, core, (a, b), True):
                        self.give(stage, m, core, at, k).wait_send()

        self.place.by_core(go)

    def end(self):
        self.arrive(range(len(self.pieces)))
        self.sent()


class Scatter:
    def __init__(self, shapes, targets, n, made=(), pieces=None):
        self.dims = grid_of(n)
        self.made = made
        self.count = len(shapes)
        self.pieces = [
            (i, c, w, targets[i][0], targets[i][1] + c) for i, c, w in pieces or cut(shapes)
        ]
        self.shapes, self.targets = shapes, targets
        self.steps = len(self.pieces) + 3

    def outs(self):
        width, rows = {}, {}
        for i, _, w, o, at in self.pieces:
            width[o], rows[o] = max(width.get(o, 0), at + w), self.shapes[i][0]
        return [jax.ShapeDtypeStruct((rows[o], width[o]), F32) for o in range(len(width))]

    def scratch(self):
        Z, Y, X = self.dims
        M, S = len(self.pieces), max(Y, X)
        one, z = max(S - 1, 1), max(Z - 1, 1)
        shape = [(self.shapes[i][0], w // 2) for i, _, w, _, _ in self.pieces]
        sem = pltpu.SemaphoreType.DMA
        lead = [(S, S, Z), (S, S, Z), (one, S, Z), (one, Z), (z,)]
        return (
            [[pltpu.VMEM(l + s, BF16) for s in shape] for l in lead]
            + [[pltpu.VMEM((2,) + s, F32) for s in shape]]
            + [sem((M, S * S))] * 3
            + [sem((M, one))] * 4
            + [sem((M, z))] * 2
            + [sem((M,))] * 2
        )

    def bind(self, grads, outs, scratch):
        self.grads, self.out = grads, outs
        self.acc, self.sib, self.got1, self.got2, self.got3, self.fin, self.lsem, *self.sem = scratch
        self.place = Place(self.dims)

    def meet(self, m, core):
        Z, Y, X = self.dims
        i, c, w, _, _ = self.pieces[m]
        for y in range(Y):
            for x in range(X):
                k = y * X + x
                mine, theirs = [
                    self.grads[i].at[:, y, x, :, pl.ds(pl.multiple_of(c + s * (w // 2), w // 2), w // 2)]
                    for s in (core, 1 - core)
                ]
                at = self.place.choose(y, x), self.place.choose(x, y)
                if i not in self.made:
                    yield pltpu.make_async_copy(mine, self.acc[m].at[at], self.lsem.at[m, k])
                yield remote(
                    theirs,
                    self.sib[m].at[at[::-1]],
                    self.sem[0].at[m, k],
                    self.sem[1].at[m, k],
                    self.place.sibling(),
                )

    def hop(self, stage, m, axes):
        a, b = axes
        mine = self.place.mine
        s, r = self.sem[2 * stage : 2 * stage + 2]
        got = (None, self.got1, self.got2, self.got3)[stage]
        for k, (there, _, dev) in enumerate(self.place.peers((None, b, a, "z")[stage])):
            at = (mine[b], mine[a])[: stage - 1] + (there,)
            yield remote(self.acc[m].at[at], got[m].at[k], s.at[m, k], r.at[m, k], dev)

    def swap(self, m, side):
        v = self.fin[m].at[side]
        return remote(v, v, self.sem[8].at[m], self.sem[9].at[m], self.place.sibling())

    def add(self, dst, srcs):
        total = dst[...].astype(F32)
        for s in srcs:
            total = total + s[...].astype(F32)
        dst[...] = total.astype(BF16)

    def begin(self, ahead=0):
        def go(core, a, b):
            for m, piece in enumerate(self.pieces):
                if piece[0] not in self.made:
                    for c in self.meet(m, core):
                        c.start()

        self.place.by_core(go)

    def put(self, pieces):
        def go(core, a, b):
            Z, Y, X = self.dims
            for m in pieces:
                i, c, w, _, _ = self.pieces[m]
                for y in range(Y):
                    for x in range(X):
                        at = self.place.choose(y, x), self.place.choose(x, y)
                        side = pl.ds(pl.multiple_of(c + core * (w // 2), w // 2), w // 2)
                        self.acc[m][at] = self.grads[i][:, y, x, :, side]
                for c in self.meet(m, core):
                    c.start()

        self.place.by_core(go)

    def step(self, t):
        self.act([(stage, t - stage) for stage in range(4) if 0 <= t - stage < len(self.pieces)])

    def act(self, pairs):
        def go(core, a, b):
            mine, size = self.place.mine, self.place.size
            for stage, m in pairs:
                acc = self.acc[m]
                if stage == 0:
                    for c in self.meet(m, core):
                        c.wait()
                    for j in range(size[b]):
                        self.add(acc.at[j, : size[a]], [self.sib[m].at[j, : size[a]]])
                else:
                    for c in self.hop(stage, m, (a, b)):
                        c.wait_recv()
                if stage == 1:
                    self.add(
                        acc.at[mine[b], : size[a]],
                        [self.got1[m].at[k, : size[a]] for k in range(size[b] - 1)],
                    )
                if stage == 2:
                    self.add(
                        acc.at[mine[b], mine[a]], [self.got2[m].at[k] for k in range(size[a] - 1)]
                    )
                if stage == 3:
                    total = acc[mine[b], mine[a], mine["z"]].astype(F32)
                    for k in range(size["z"] - 1):
                        total = total + self.got3[m][k].astype(F32)
                    self.fin[m][core] = total
                    self.swap(m, core).start()
                else:
                    for c in self.hop(stage + 1, m, (a, b)):
                        c.start()

        self.place.by_core(go)

    def end(self):
        def go(core, a, b):
            for m in range(len(self.pieces)):
                for stage in range(1, 4):
                    for c in self.hop(stage, m, (a, b)):
                        c.wait_send()
                self.swap(m, core).wait_send()
                self.swap(m, 1 - core).wait_recv()

        self.place.by_core(go)
        for m, (i, c, w, o, at) in enumerate(self.pieces):
            for side in range(2):
                self.out[o][:, at + side * (w // 2) : at + (side + 1) * (w // 2)] = self.fin[m][side]


class Pace:
    def __init__(self, actions):
        self.todo = sorted(actions, key=lambda a: a[0])
        self.at = {key: t for t, key, _ in actions}

    def until(self, t):
        out = [a[2] for a in self.todo if a[0] <= t]
        self.todo = [a for a in self.todo if a[0] > t]
        return out

    def run(self, t):
        for action in self.until(t):
            action()

    def units(self, start, step, count, gap=0.0, every=1):
        return [self.until(start + u * step + (u // every) * gap) for u in range(count)]

    @staticmethod
    def pick(plan, i):
        for u, actions in enumerate(plan):
            if actions:

                @pl.when(i == u)
                def _(actions=actions):
                    for action in actions:
                        action()


def alone(engine, operands, cid, name):
    def kernel(*refs):
        count, outs = len(operands), len(engine.outs())
        engine.bind(refs[:count], refs[count : count + outs], refs[count + outs :])
        engine.place.greet()
        engine.begin(AHEAD)
        for t in range(engine.steps):
            engine.step(t)
        engine.end()

    space = pl.ANY if isinstance(engine, Gather) else pltpu.VMEM
    return pl.pallas_call(
        kernel,
        out_shape=engine.outs(),
        in_specs=[pl.BlockSpec(memory_space=pl.ANY)] * len(operands),
        out_specs=[pl.BlockSpec(memory_space=space)] * len(engine.outs()),
        scratch_shapes=engine.scratch(),
        compiler_params=pltpu.CompilerParams(
            collective_id=cid, has_side_effects=True, vmem_limit_bytes=VMEM_BYTES
        ),
        name=name,
    )(*operands)


class Beside:
    def __init__(self, engine, points):
        self.engine = engine
        self.points = points

    def reach(self, i, side):
        e = self.engine

        @pl.when((i == 0) & (side == 0))
        def _():
            e.place.greet()
            e.begin(AHEAD)

        for t, p in enumerate(self.points):
            if p is not None:

                @pl.when((i == p // 2) & (side == p % 2))
                def _(t=t):
                    e.step(t)

    def close(self, i):
        e = self.engine

        @pl.when(i == pl.num_programs(0) - 1)
        def _():
            for t, p in enumerate(self.points):
                if p is None:
                    e.step(t)
            e.end()


def paced(engine, first, each, unit, units=12):
    points = []
    for t in range(engine.steps):
        p = int(-(-(first + t * each) // unit))
        points.append(p if p < units else None)
    return points


def attend_beside(body, attn_in, in_specs, attn_out, out_specs, attn_scratch, engine, operands, points, cid, name):
    nin, nout, nscr = len(attn_in), len(attn_out), len(attn_scratch)
    moved, landed = len(operands), len(engine.outs())

    def kernel(*refs):
        at = 0
        groups = []
        for count in (nin, moved, nout, landed, nscr):
            groups.append(refs[at : at + count])
            at += count
        engine.bind(groups[1], groups[3], refs[at:])
        beside = Beside(engine, points)
        i = pl.program_id(0)
        body(*groups[0], *groups[2], *groups[4], at=lambda side: beside.reach(i, side))
        beside.close(i)

    any_ = pl.BlockSpec(memory_space=pl.ANY)
    space = pl.ANY if isinstance(engine, Gather) else pltpu.VMEM
    outs = pl.pallas_call(
        kernel,
        grid=(6,),
        in_specs=in_specs + [any_] * moved,
        out_specs=out_specs + [pl.BlockSpec(memory_space=space)] * landed,
        out_shape=attn_out + engine.outs(),
        scratch_shapes=attn_scratch + engine.scratch(),
        compiler_params=pltpu.CompilerParams(
            collective_id=cid, has_side_effects=True, vmem_limit_bytes=VMEM_BYTES
        ),
        name=name,
    )(*attn_in, *operands)
    return outs[:nout], outs[nout:]


def attn_fwd(live, q, k, v, cols, causal, unit, bq, engine, operands, points, cid, name):
    T, K = q.shape[0], k.shape[0]
    qo, ko, vo = cols
    return attend_beside(
        functools.partial(fwd_kernel, causal=causal, bq=bq, unit=unit),
        [live, q, k, v],
        [
            pl.BlockSpec(memory_space=pltpu.SMEM),
            pl.BlockSpec((T, 128), lambda i: (0, i + qo)),
            pl.BlockSpec((K, 128), lambda i: (0, i + ko)),
            pl.BlockSpec((K, 128), lambda i: (0, i + vo)),
        ],
        [jax.ShapeDtypeStruct((T, D), BF16), jax.ShapeDtypeStruct((6, 2, T), F32)],
        [pl.BlockSpec((T, 128), lambda i: (0, i)), pl.BlockSpec((1, 2, T), lambda i: (i, 0, 0))],
        [pltpu.VMEM((128, K), BF16), pltpu.VMEM((128, T), F32)],
        engine,
        operands,
        points,
        cid,
        name,
    )


def attn_bwd(live, q, k, v, o, do, lse, cols, causal, unit, bq, bk, engine, operands, points, cid, name):
    T, K = q.shape[0], k.shape[0]
    qo, ko, vo = cols
    return attend_beside(
        functools.partial(bwd_kernel, causal=causal, bq=bq, bk=bk, unit=unit),
        [live, q, k, v, o, do, lse],
        [
            pl.BlockSpec(memory_space=pltpu.SMEM),
            pl.BlockSpec((T, 128), lambda i: (0, i + qo)),
            pl.BlockSpec((K, 128), lambda i: (0, i + ko)),
            pl.BlockSpec((K, 128), lambda i: (0, i + vo)),
            pl.BlockSpec((T, 128), lambda i: (0, i)),
            pl.BlockSpec((T, 128), lambda i: (0, i)),
            pl.BlockSpec((1, 2, T), lambda i: (i, 0, 0)),
        ],
        [jax.ShapeDtypeStruct((3, T, D), BF16)],
        [pl.BlockSpec((3, T, 128), lambda i: (0, 0, i))],
        [
            pltpu.VMEM((128, K), BF16),
            pltpu.VMEM((128, T), F32),
            pltpu.VMEM((K, 128), F32),
            pltpu.VMEM((K, 128), F32),
            pltpu.VMEM((2, T), F32),
        ],
        engine,
        operands,
        points,
        cid,
        name,
    )


def finish(sums, halves, plain, scale):
    def kernel(*refs):
        count = len(sums)
        for i, o in zip(refs[:count], refs[count + 3 :]):
            o[...] = i[...] * scale
        width = halves[0].shape[1]
        refs[2 * count + 3][:, :width] = refs[count][...] * scale
        refs[2 * count + 3][:, width:] = refs[count + 1][...] * scale
        refs[2 * count + 4][...] = refs[count + 2][...]

    rows, width = halves[0].shape[0], halves[0].shape[1] + halves[1].shape[1]
    shapes = [s.shape for s in sums] + [(rows, width), plain.shape]
    return pl.pallas_call(
        kernel,
        out_shape=[jax.ShapeDtypeStruct(s, F32) for s in shapes],
        compiler_params=pltpu.CompilerParams(vmem_limit_bytes=VMEM_BYTES),
        name="finish",
    )(*sums, *halves, plain)


def moments(values):
    average = jnp.mean(values, -1, keepdims=True)
    centred = values - average
    variance = jnp.mean(centred * centred, -1, keepdims=True)
    inverse = lax.rsqrt(variance + EPS)
    return centred * inverse, inverse


def norm_back(normal, inverse, gain, grad):
    m = grad * gain
    back = inverse * (
        m - jnp.mean(m, -1, keepdims=True) - normal * jnp.mean(m * normal, -1, keepdims=True)
    )
    return back, jnp.sum(grad * normal, 0), jnp.sum(grad, 0)


GELU_A = 0.7978845608028654
GELU_B = 0.044715


def gelu(u):
    return 0.5 * u * (1.0 + jnp.tanh(GELU_A * (u + GELU_B * u * u * u)))


def gelu_slope(u):
    t = jnp.tanh(GELU_A * (u + GELU_B * u * u * u))
    return 0.5 * (1.0 + t) + 0.5 * u * (1.0 - t * t) * (GELU_A * (1.0 + 3.0 * GELU_B * u * u))


def blocks(rows, step, body, plan=()):
    def go(r, _):
        Pace.pick(plan, r)
        body(pl.ds(pl.multiple_of(r * step, step), step))
        return 0

    lax.fori_loop(0, rows // step, go, 0)


def pair(ref, i, first=0):
    return ref.at[:, pl.ds(pl.multiple_of(first + i * 128, 128), 128)]


def norm_rows(packed):
    count = packed.shape[0]
    own = D // count
    total = None
    for j in range(count):
        r = lax.broadcasted_iota(jnp.int32, (128, D), 0)
        c = lax.broadcasted_iota(jnp.int32, (128, D), 1)
        spot = jnp.where((c == r + own * j) & (r < own), 1.0, 0.0).astype(BF16)
        part = dg(packed[j, :, :128], spot, NN)
        total = part if total is None else total + part
    return total


GATHER_AHEAD = 2
GATHER = dict(first=6.5, rate=3.7, hop=3.5, slack=2.5)


def gather_pace(eng):
    actions = []
    link = 0.0
    for m, (i, _, w) in enumerate(eng.pieces):
        rows = eng.shapes[i][0] * eng.dims[0] * eng.dims[1] * eng.dims[2]
        cost = GATHER["rate"] * rows * w * 2e-6
        slack = GATHER["slack"] if m > 3 else 0.0
        t = GATHER["first"] + link + cost / 2
        if m >= GATHER_AHEAD:
            actions.append((t - cost / 2 - 5.0, ("leave", m), functools.partial(eng.leave, [m])))
        for s, part in enumerate((0.0, 0.33, 0.67)):
            t += (part * cost + GATHER["hop"] + slack) if s else 0.0
            actions.append((t, (s, m), functools.partial(eng.act, [(s, m)])))
        link += cost
    first = min(t for t, key, _ in actions if key == (0, 0))
    actions.append((first - 1e-3, "own", eng.settle))
    pace = Pace(actions)
    return pace, lambda m: pace.at[(2, m)]


def forward_kernel(eng, *refs):
    it = iter(refs)

    def take(count):
        return [next(it) for _ in range(count)]

    clip, frames, tok_in, ctx_in = take(4)
    shards = take(eng.count)
    whole = take(eng.count)
    q1_o, k1_o, v1_o, o1_o, h1_o, x1_o, h2_o, qkv_o, o2_o, x2_o, h3_o, lse1_o, lse2_o, norms_o = take(14)
    tok, ctx, q1, k1, v1, o1, h1, x1, h2, qkv, o2, x2, h3, lse1, lse2, norms = take(16)
    packed, wa, wb, wqkv, vt, ot, isem, wsem, osem = take(9)
    eng.bind(shards, whole, list(it))
    T = tok.shape[0]
    eng.place.greet()
    eng.begin(GATHER_AHEAD)
    pace, ready = gather_pace(eng)
    loads = [pltpu.make_async_copy(ctx_in, ctx, isem.at[0]), pltpu.make_async_copy(tok_in, tok, isem.at[1])]
    for c in loads:
        c.start()
    saves = []

    def save(ref, out):
        c = pltpu.make_async_copy(ref, out, osem.at[len(saves)])
        c.start()
        saves.append(c)

    def fetch(i, pieces, ref):
        eng.arrive(pieces)
        c = pltpu.make_async_copy(whole[i], ref, wsem)
        c.start()
        c.wait()

    def matrix(ref, c=0):
        return ref[:, :, :, :, c : c + D].reshape(D, D)

    clock = ready(0)
    pace.run(clock)
    fetch(0, [0], wa)
    loads[0].wait()

    def keys(r):
        k1[r] = dg(ctx[r], matrix(wa), NN).astype(BF16)

    blocks(T, 256, keys)
    save(k1, k1_o)
    clock = max(clock + 2.5, ready(1))
    pace.run(clock)
    fetch(1, [1], wb)

    def values(r):
        v1[r] = dg(ctx[r], matrix(wb), NN).astype(BF16)

    blocks(T, 256, values)
    save(v1, v1_o)
    clock = max(clock + 2.5, ready(2))
    pace.run(clock)
    fetch(2, [2], packed)
    norms[...] = norm_rows(packed[...].reshape((-1,) + packed.shape[3:]))
    save(norms, norms_o)
    loads[1].wait()

    def first_norm(r):
        normal, _ = moments(tok[r].astype(F32))
        h1[r] = (normal * norms[0:1] + norms[1:2]).astype(BF16)

    blocks(T, 128, first_norm)
    save(h1, h1_o)
    clock = max(clock + 3.5, ready(3))
    pace.run(clock)
    fetch(3, [3], wa)

    def queries(r):
        q1[r] = dg(h1[r], matrix(wa), NN).astype(BF16)

    blocks(T, 256, queries)
    save(q1, q1_o)

    def heads(plan, body):
        def go(i, _):
            for side in range(2):
                Pace.pick(plan[side::2], i)
                body(i, side)
            return 0

        lax.fori_loop(0, 6, go, 0)

    clock += 2.5
    heads(
        pace.units(clock, 2.2, 12),
        lambda i, side: fwd_unit(
            side, frames, pair(q1, i), pair(k1, i), pair(v1, i), pair(o1, i), lse1.at[pl.ds(i, 1)], vt, ot,
            causal=False, bq=512, unit=FRAME_TOK,
        ),
    )
    save(o1, o1_o)
    save(lse1, lse1_o)
    clock = max(clock + 26.4, ready(4), ready(7))
    pace.run(clock)
    fetch(4, [4], wb)
    fetch(5, [5, 6, 7], wqkv)

    def middle(r):
        x = tok[r].astype(F32) + dg(o1[r], matrix(wb), NN)
        x1[r] = x
        normal, _ = moments(x)
        h2[r] = (normal * norms[2:3] + norms[3:4]).astype(BF16)
        for c in range(3):
            qkv[r, c * D : (c + 1) * D] = dg(h2[r], matrix(wqkv, c * D), NN).astype(BF16)

    blocks(T, 256, middle, pace.units(clock, 3.0, 4))
    clock += 12.0
    for ref, out in ((x1, x1_o), (h2, h2_o), (qkv, qkv_o)):
        save(ref, out)
    heads(
        pace.units(clock, 1.5, 12),
        lambda i, side: fwd_unit(
            side, clip, pair(qkv, i), pair(qkv, i, D), pair(qkv, i, 2 * D), pair(o2, i), lse2.at[pl.ds(i, 1)], vt, ot,
            causal=True, bq=512, unit=1,
        ),
    )
    save(o2, o2_o)
    save(lse2, lse2_o)
    clock = max(clock + 18.0, ready(8))
    pace.run(clock)
    fetch(6, [8], wa)

    def late(r):
        x = x1[r] + dg(o2[r], matrix(wa), NN)
        x2[r] = x
        normal, _ = moments(x)
        h3[r] = (normal * norms[4:5] + norms[5:6]).astype(BF16)

    blocks(T, 256, late, pace.units(clock, 1.2, 4))
    save(x2, x2_o)
    save(h3, h3_o)
    pace.run(1e9)
    eng.arrive(range(9, len(eng.pieces)))
    eng.sent()
    for c in saves:
        c.wait()


def forward(clip, frames, tok, ctx, shards, n, cid):
    eng = Gather([s.shape for s in shards], n)
    T = tok.shape[0]
    wide = jax.ShapeDtypeStruct((T, D), BF16)
    full = jax.ShapeDtypeStruct((T, D), F32)
    lse = jax.ShapeDtypeStruct((6, 2, T), F32)
    kept = [wide] * 5 + [full, wide, jax.ShapeDtypeStruct((T, 3 * D), BF16), wide, full, wide, lse, lse]
    kept.append(jax.ShapeDtypeStruct((16, D), F32))
    own = shards[0].shape[0]
    square = pltpu.VMEM(eng.dims + (own, D), BF16)
    any_ = pl.BlockSpec(memory_space=pl.ANY)
    smem = pl.BlockSpec(memory_space=pltpu.SMEM)
    sem = pltpu.SemaphoreType.DMA
    outs = pl.pallas_call(
        functools.partial(forward_kernel, eng),
        out_shape=eng.outs() + kept,
        in_specs=[smem, smem] + [any_] * (2 + eng.count),
        out_specs=[any_] * (eng.count + len(kept)),
        scratch_shapes=[pltpu.VMEM((T, D), BF16)] * 2
        + [pltpu.VMEM(kept[i].shape, kept[i].dtype) for i in (0, 1, 2, 3, 4, 5, 6, 7, 8, 9, 10, 11, 12, 13)]
        + [pltpu.VMEM(eng.dims + shards[2].shape, BF16), square, square]
        + [pltpu.VMEM(eng.dims + (own, 3 * D), BF16), pltpu.VMEM((128, T), BF16), pltpu.VMEM((128, T), F32)]
        + [sem((2,)), sem, sem((16,))]
        + eng.scratch(),
        compiler_params=pltpu.CompilerParams(
            collective_id=cid, has_side_effects=True, vmem_limit_bytes=VMEM_BYTES
        ),
        name="forward",
    )(clip, frames, tok, ctx, *shards)
    return outs[: eng.count], outs[eng.count :]


def back_norm(values, gain, grad):
    normal, inverse = moments(values)
    m = grad * gain
    back = inverse * (
        m - jnp.mean(m, -1, keepdims=True) - normal * jnp.mean(m * normal, -1, keepdims=True)
    )
    return back, jnp.sum(grad * normal, 0, keepdims=True), jnp.sum(grad, 0, keepdims=True)


def mlp_kernel(clip, norms, x2, h3, cot, w_up, w_down, out, dx2, g_up, g_down, g_norm, dz, acc, dh, hid, dup):
    j = pl.program_id(0)
    T = x2.shape[0]

    def live(r):
        at = r.start + lax.broadcasted_iota(jnp.int32, (r.size, 1), 0)
        return at < clip[0]

    @pl.when(j == 0)
    def _():
        def first(r):
            dz[r] = jnp.where(live(r), cot[r], BF16(0))
            acc[r] = jnp.zeros((r.size, D), F32)
            dh[r] = jnp.zeros((r.size, D), F32)

        blocks(T, 256, first)

    up_w, down_w = w_up[...], w_down[...]

    def forth(r):
        u = dg(h3[r], up_w, NN)
        inner = u * (GELU_A + (GELU_A * GELU_B) * (u * u))
        t = jnp.tanh(inner)
        half = 0.5 + 0.5 * t
        hid[r] = (u * half).astype(BF16)
        slope = half + (0.5 * u) * (1.0 - t * t) * (GELU_A + (3.0 * GELU_A * GELU_B) * (u * u))
        dup[r] = (dg(dz[r], down_w, NT) * slope).astype(BF16)
        a = dg(hid[r], down_w, NN)
        b = dg(dup[r], up_w, NT)

        acc[r] += a
        dh[r] += b

    blocks(T, T, forth)
    g_up[...] = dg(h3[...], dup[...], TN).astype(BF16)
    g_down[...] = dg(hid[...], dz[...], TN).astype(BF16)

    @pl.when(j == pl.num_programs(0) - 1)
    def _():
        g_norm[...] = jnp.zeros_like(g_norm)

        def last(r):
            x = x2[r]
            out[r] = jnp.where(live(r), x + acc[r], 0.0).astype(BF16)
            back, gain, bias = back_norm(x, norms[4:5], dh[r])
            dx2[r] = jnp.where(live(r), cot[r].astype(F32), 0.0) + back
            g_norm[0:1] += gain
            g_norm[1:2] += bias

        blocks(T, 128, last)


def mlp(clip, norms, x2, h3, cot, w_up, w_down, step=768):
    T = x2.shape[0]
    FF = w_up.shape[1]

    def still(shape):
        return pl.BlockSpec(shape, lambda j: (0, 0))

    return pl.pallas_call(
        mlp_kernel,
        grid=(FF // step,),
        in_specs=[
            pl.BlockSpec(memory_space=pltpu.SMEM),
            still(norms.shape),
            still((T, D)),
            still((T, D)),
            still((T, D)),
            pl.BlockSpec((D, step), lambda j: (0, j)),
            pl.BlockSpec((step, D), lambda j: (j, 0)),
        ],
        out_specs=[
            still((T, D)),
            still((T, D)),
            pl.BlockSpec((D, step), lambda j: (0, j)),
            pl.BlockSpec((step, D), lambda j: (j, 0)),
            still((8, D)),
        ],
        out_shape=[
            jax.ShapeDtypeStruct((T, D), BF16),
            jax.ShapeDtypeStruct((T, D), F32),
            jax.ShapeDtypeStruct((D, FF), BF16),
            jax.ShapeDtypeStruct((FF, D), BF16),
            jax.ShapeDtypeStruct((8, D), F32),
        ],
        scratch_shapes=[
            pltpu.VMEM((T, D), BF16),
            pltpu.VMEM((T, D), F32),
            pltpu.VMEM((T, D), F32),
            pltpu.VMEM((T, step), BF16),
            pltpu.VMEM((T, step), BF16),
        ],
        compiler_params=pltpu.CompilerParams(vmem_limit_bytes=VMEM_BYTES),
        name="mlp",
    )(clip, norms, x2, h3, cot, w_up, w_down)


def spots(j, own):
    r = lax.broadcasted_iota(jnp.int32, (128, D), 0)
    c = lax.broadcasted_iota(jnp.int32, (128, D), 1)
    return jnp.where((c == r + own * j) & (r < own), 1.0, 0.0).astype(BF16)


def load_all(sems, pairs):
    copies = [pltpu.make_async_copy(s, d, sems.at[k]) for k, (s, d) in enumerate(pairs)]
    for c in copies:
        c.start()
    return copies


def square(ref, c=0):
    return ref[:, :, :, :, c : c + D].reshape(D, D)


SCATTER = dict(first=6.0, rate=3.8, hop=3.5, slack=3.5, lead=5.0)


def scatter_pace(eng, groups):
    actions = []
    link = SCATTER["first"]
    for at, pieces in groups:
        cost = 0.0
        for m in pieces:
            i, _, w, _, _ = eng.pieces[m]
            rows = eng.shapes[i][0] * eng.dims[0] * eng.dims[1] * eng.dims[2]
            cost += SCATTER["rate"] * rows * w * 2e-6
        link = max(link, at)
        t = max(link - SCATTER["lead"], at + 2.0)
        for s, part in enumerate((0.0, 0.67, 0.33, 0.25)):
            if s == 1:
                t = link
            t += (part * cost + SCATTER["hop"] + SCATTER["slack"]) if s else 0.0
            actions.append((t, (s, pieces[0]), functools.partial(eng.act, [(s, m) for m in pieces])))
        link += cost
    return Pace(actions)


def causal_kernel(eng, *refs):
    it = iter(refs)

    def take(count):
        return [next(it) for _ in range(count)]

    clip, dx2_in, x1_in, qkv_in, o2_in, h2_in, lse, norms, wp_in, wqkv_in = take(10)
    grads = take(eng.count)
    sums = take(len(eng.outs()))
    dx1_o, gp_o, gqkv_o, gnorm = take(4)
    dx, x1, qkv, o2, h2, wp, wqkv, dy, do, dqkv, gp, gqkv, kt, dqt, dka, dva, dl, isem, osem = take(19)
    eng.bind(grads, sums, list(it))
    T = dx.shape[0]
    eng.place.greet()
    eng.begin()
    loads = load_all(
        isem,
        [(dx2_in, dx), (wp_in, wp), (o2_in, o2), (qkv_in, qkv), (x1_in, x1), (h2_in, h2), (wqkv_in, wqkv)],
    )
    loads[0].wait()
    loads[1].wait()

    def first(r):
        dy[r] = dx[r].astype(BF16)
        do[r] = dg(dy[r], square(wp), NT).astype(BF16)

    pace = scatter_pace(eng, [(0.0, [m]) for m in range(len(eng.pieces))])
    blocks(T, 256, first)
    pace.run(6.0)
    loads[2].wait()

    def weight(left, right, out, c, step=256):
        def go(k, _):
            at = pl.multiple_of(k * step, step)
            g = dg(left[...], right[:, pl.ds(at, step)], TN).astype(BF16)
            out[:, :, :, :, pl.ds(c + at, step)] = g.reshape(out.shape[:4] + (step,))
            return 0

        lax.fori_loop(0, D // step, go, 0)

    weight(o2, dy, gp, 0)
    saves = [pltpu.make_async_copy(gp, gp_o, osem.at[0])]
    saves[0].start()
    loads[3].wait()
    plan = pace.units(9.0, 2.5, 12)

    def unit_of(i, side):
        u = 2 * i + side
        Pace.pick(plan[side::2], i)
        cols = pl.ds(pl.multiple_of(i * 128, 128), 128)
        bwd_unit(
            side, clip, pair(qkv, i), pair(qkv, i, D), pair(qkv, i, 2 * D), pair(o2, i), pair(do, i),
            lse.at[pl.ds(i, 1)], dqkv.at[:, :, cols], kt, dqt, dka, dva, dl,
            causal=True, bq=256, bk=512, unit=1,
        )

    def heads(i, _):
        unit_of(i, 0)
        unit_of(i, 1)
        return 0

    lax.fori_loop(0, 6, heads, 0)
    for c in loads[4:]:
        c.wait()
    gnorm[...] = jnp.zeros_like(gnorm)

    def back(r):
        dh = sum(dg(dqkv[c, r], square(wqkv, c * D), NT) for c in range(3))
        g, gain, bias = back_norm(x1[r], norms[2:3], dh)
        dx[r] += g
        gnorm[0:1] += gain
        gnorm[1:2] += bias

    blocks(T, 256, back, pace.units(39.0, 1.7, 4))
    saves.append(pltpu.make_async_copy(dx, dx1_o, osem.at[1]))
    saves[1].start()
    for c in range(3):
        pace.run(46.0 + 2.0 * c)
        weight(h2, dqkv.at[c], gqkv, c * D)
    saves.append(pltpu.make_async_copy(gqkv, gqkv_o, osem.at[2]))
    saves[2].start()
    pace.run(1e9)
    eng.end()
    for c in saves:
        c.wait()


def causal_back(clip, dx2, x1, qkv, o2, h2, lse, norms, wp, wqkv, grads, targets, n, cid):
    pieces = [(0, c * 256, 256) for c in range(3)] + [(1, c * D, D) for c in range(grads[1].shape[4] // D // 2)]
    eng = Scatter([a.shape[3:] for a in grads], targets, n, pieces=pieces)
    T = dx2.shape[0]
    own = wp.shape[3]
    any_ = pl.BlockSpec(memory_space=pl.ANY)
    smem = pl.BlockSpec(memory_space=pltpu.SMEM)
    vmem = pl.BlockSpec(memory_space=pltpu.VMEM)
    sem = pltpu.SemaphoreType.DMA
    small = jax.ShapeDtypeStruct((8, D), F32)
    one, three = eng.dims + (own, D), eng.dims + (own, 3 * D)

    def vm(shape, dtype=BF16):
        return pltpu.VMEM(shape, dtype)

    sums = eng.outs()
    outs = pl.pallas_call(
        functools.partial(causal_kernel, eng),
        out_shape=sums
        + [jax.ShapeDtypeStruct((T, D), F32), jax.ShapeDtypeStruct(one, BF16), jax.ShapeDtypeStruct(three, BF16), small],
        in_specs=[smem] + [any_] * 5 + [vmem] * 2 + [any_] * (2 + eng.count),
        out_specs=[vmem] * len(sums) + [any_] * 3 + [vmem],
        scratch_shapes=[
            vm((T, D), F32),
            vm((T, D), F32),
            vm((T, 3 * D)),
            vm((T, D)),
            vm((T, D)),
            vm(one),
            vm(three),
            vm((T, D)),
            vm((T, D)),
            vm((3, T, D)),
            vm(one),
            vm(three),
            vm((128, T)),
            vm((128, T), F32),
            vm((T, 128), F32),
            vm((T, 128), F32),
            vm((2, T), F32),
            sem((7,)),
            sem((3,)),
        ]
        + eng.scratch(),
        compiler_params=pltpu.CompilerParams(
            collective_id=cid, has_side_effects=True, vmem_limit_bytes=VMEM_BYTES
        ),
        name="causal_back",
    )(clip, dx2, x1, qkv, o2, h2, lse, norms, wp, wqkv, *grads)
    return outs[: len(sums)], outs[len(sums) :]


def cross_kernel(eng, *refs):
    it = iter(refs)

    def take(count):
        return [next(it) for _ in range(count)]

    frames, dx1_in, tok_in, ctx_in, q1_in, k1_in, v1_in, o1_in, h1_in, lse, norms, gnorm2, gnorm3, wo_in, wq_in = take(15)
    given = take(3)
    sums = take(len(eng.outs()))
    (grad_o,) = take(1)
    dx, tok, ctx, q1, k1, v1, o1, h1, wo, wq, dy, do, dqkv, kt, dqt, dka, dva, dl, gsum, isem, osem = take(21)
    go_, gv, gk, gq, gn = take(5)
    eng.bind(list(given[:2]) + [go_, gv, gk, gq, gn, given[2]], sums, list(it))
    T = dx.shape[0]
    n = gn.shape[0] * gn.shape[1] * gn.shape[2]
    own = D // n
    eng.place.greet()
    eng.begin()
    loads = load_all(
        isem,
        [(dx1_in, dx), (wo_in, wo), (o1_in, o1), (q1_in, q1), (k1_in, k1), (v1_in, v1), (h1_in, h1), (ctx_in, ctx),
         (wq_in, wq), (tok_in, tok)],
    )
    loads[0].wait()
    loads[1].wait()

    def first(r):
        dy[r] = dx[r].astype(BF16)
        do[r] = dg(dy[r], square(wo), NT).astype(BF16)

    blocks(T, 256, first)
    loads[2].wait()

    def weight(left, right, out, at, width=256):
        g = dg(left[...], right[:, pl.ds(at, width)], TN).astype(BF16)
        out[:, :, :, :, pl.ds(at, width)] = g.reshape(out.shape[:4] + (width,))

    def whole(k, _):
        weight(o1, dy, go_, pl.multiple_of(k * 256, 256))
        return 0

    lax.fori_loop(0, 3, whole, 0)
    eng.put([4])
    for c in loads[3:]:
        c.wait()
    third = [[5 + g, 8 + g, 11 + g] for g in range(3)]
    start, unit, gap = 9.0, 3.05, 3.0
    made = [start + 4 * (g + 1) * unit + (g + 1) * gap for g in range(3)]
    pace = scatter_pace(
        eng,
        [(0.0, [m]) for m in [0, *range(15, len(eng.pieces)), 1, 2, 3]]
        + [(start, [4])]
        + [(made[g], third[g]) for g in range(3)]
        + [(made[2] + 6.0, [14])],
    )
    plan = pace.units(start, unit, 12, gap, 4)

    def unit_of(i, side):
        u = 2 * i + side
        Pace.pick(plan[side::2], i)
        cols = pl.ds(pl.multiple_of(i * 128, 128), 128)
        bwd_unit(
            side, frames, pair(q1, i), pair(k1, i), pair(v1, i), pair(o1, i), pair(do, i),
            lse.at[pl.ds(i, 1)], dqkv.at[:, :, cols], kt, dqt, dka, dva, dl,
            causal=False, bq=1024, bk=256, unit=FRAME_TOK,
        )

        if side == 0:
            return

        @pl.when(lax.rem(u, 4) == 3)
        def _():
            c = pl.multiple_of(lax.div(u, 4) * 256, 256)
            weight(ctx, dqkv.at[2], gv, c)
            weight(ctx, dqkv.at[1], gk, c)
            weight(h1, dqkv.at[0], gq, c)

        for g in range(3):
            pl.when(u == 4 * g + 3)(functools.partial(eng.put, third[g]))

    def heads(i, _):
        unit_of(i, 0)
        unit_of(i, 1)
        return 0

    lax.fori_loop(0, 6, heads, 0)
    gsum[...] = jnp.zeros_like(gsum)
    gsum[2:4] = gnorm2[0:2]
    gsum[4:6] = gnorm3[0:2]
    pace.run(made[2])

    def back(r):
        dh = dg(dqkv[0, r], square(wq), NT)
        g, gain, bias = back_norm(tok[r].astype(F32), norms[0:1], dh)
        dx[r] += g
        gsum[0:1] += gain
        gsum[1:2] += bias

    blocks(T, 256, back, pace.units(made[2] + 1.0, 1.2, 4))
    save = pltpu.make_async_copy(dx, grad_o, osem)
    save.start()
    pace.run(made[2] + 5.5)
    rows = gsum[...].astype(BF16)
    Z, Y, X = gn.shape[:3]
    for j in range(n):
        z, y, x = j // (Y * X), (j // X) % Y, j % X
        gn[z, y, x, :, :128] = dg(rows, spots(j, own), NT).astype(BF16)
        gn[z, y, x, :, 128:] = jnp.zeros((16, 128), BF16)
    eng.put([14])
    pace.run(1e9)
    eng.end()
    save.wait()


def cross_back(
    frames, dx1, tok, ctx, q1, k1, v1, o1, h1, lse, norms, gnorm2, gnorm3, wo, wq, gp, gqkv, gup, n, cid
):
    own = wo.shape[3]
    one = gp.shape
    shapes = [gp.shape[3:], gqkv.shape[3:], one[3:], one[3:], one[3:], one[3:], (16, 256), gup.shape[3:]]
    FF = gup.shape[4]
    pieces = [(0, 0, D)] + [(1, c * D, D) for c in range(3)] + [(2, 0, D)]
    pieces += [(i, c * 256, 256) for i in (3, 4, 5) for c in range(3)] + [(6, 0, 256)]
    pieces += [(7, c * D, D) for c in range(FF // D // 2, FF // D)]
    targets = [(6, 0), (5, 0), (4, 0), (3, 0), (2, 0), (1, 0), (0, 0), (7, -(FF // D // 2) * D)]
    eng = Scatter(shapes, targets, n, made=(2, 3, 4, 5, 6), pieces=pieces)
    T = dx1.shape[0]
    any_ = pl.BlockSpec(memory_space=pl.ANY)
    smem = pl.BlockSpec(memory_space=pltpu.SMEM)
    vmem = pl.BlockSpec(memory_space=pltpu.VMEM)
    sem = pltpu.SemaphoreType.DMA

    def vm(shape, dtype=BF16):
        return pltpu.VMEM(shape, dtype)

    sums = eng.outs()
    outs = pl.pallas_call(
        functools.partial(cross_kernel, eng),
        out_shape=sums + [jax.ShapeDtypeStruct((T, D), F32)],
        in_specs=[smem] + [any_] * 8 + [vmem] * 4 + [any_] * 5,
        out_specs=[vmem] * len(sums) + [any_],
        scratch_shapes=[vm((T, D), F32)]
        + [vm((T, D))] * 7
        + [vm(one)] * 2
        + [vm((T, D))] * 2
        + [vm((3, T, D)), vm((128, T)), vm((128, T), F32), vm((T, 128), F32), vm((T, 128), F32), vm((2, T), F32), vm((16, D), F32)]
        + [sem((10,)), sem]
        + [vm(one)] * 4
        + [vm(one[:3] + (16, 256))]
        + eng.scratch(),
        compiler_params=pltpu.CompilerParams(
            collective_id=cid, has_side_effects=True, vmem_limit_bytes=VMEM_BYTES
        ),
        name="cross_back",
    )(frames, dx1, tok, ctx, q1, k1, v1, o1, h1, lse, norms, gnorm2, gnorm3, wo, wq, gp, gqkv, gup)
    return outs[: len(sums)], outs[len(sums)]


def shards(
    tokens,
    context,
    clip_lengths,
    context_frames,
    norm1_gain,
    norm1_bias,
    cross_q,
    cross_k,
    cross_v,
    cross_out,
    norm2_gain,
    norm2_bias,
    attn_qkv,
    attn_out,
    norm3_gain,
    norm3_bias,
    mlp_up,
    mlp_down,
    cotangent,
):
    n = lax.axis_size("fsdp")
    stream_in = tokens[0].astype(F32)
    context_rows = context[0]
    slot_rows = stream_in.shape[0]
    own = norm1_gain.shape[0]
    padding = (jnp.arange(slot_rows) < clip_lengths[0])[:, None]
    norms = jnp.stack([norm1_gain, norm1_bias, norm2_gain, norm2_bias, norm3_gain, norm3_bias])
    norms = jnp.pad(norms, ((0, 10), (0, 256 - own)))

    def flat(arrays):
        return [a.reshape(-1, a.shape[4]) for a in arrays]

    def gather(arrays):
        return Gather([a.shape for a in arrays], n), arrays

    def weight(left, right):
        g = dg(left, right, TN).astype(BF16)
        return g.reshape(n, -1, g.shape[1])

    def scatter(grads):
        arrays = [g.reshape(grid_of(n) + g.shape[1:]) for g, _ in grads]
        return Scatter([a.shape[3:] for a in arrays], [t for _, t in grads], n), arrays

    if own % 16 == 0:
        whole, kept = forward(
            clip_lengths,
            context_frames,
            tokens[0],
            context_rows,
            [cross_k, cross_v, norms, cross_q, cross_out, attn_qkv, attn_out, mlp_up, mlp_down],
            n,
            0,
        )
        _, _, _, w_q, w_o, w_qkv, w_p, w_up, w_down = whole
        q1, k1, v1, o1, h1, x1, h2, qkv, o2, x2, h3, lse1, lse2, norms = kept
        block_out, dx2, g_up, g_down, g_norm3 = mlp(
            clip_lengths, norms, x2, h3, cotangent[0], *flat([w_up, w_down])
        )
        grads = [g_down.reshape(w_down.shape), g_up.reshape(w_up.shape)]
        (s_up, s_down), (dx1, g_p, g_qkv, g_norm2) = causal_back(
            clip_lengths, dx2, x1, qkv, o2, h2, lse2, norms, w_p, w_qkv, grads, [(1, 0), (0, 0)], n, 1
        )
        (s_norms, s_q, s_k, s_v, s_o, s_qkv, s_p, s_up2), input_grad = cross_back(
            context_frames, dx1, tokens[0], context_rows, q1, k1, v1, o1, h1, lse1, norms, g_norm2, g_norm3,
            w_o, w_q, g_p, g_qkv, grads[1], n, 2
        )
    else:
        first, operands = gather([norms, cross_q, cross_k, cross_v])
        norms, *whole = alone(first, operands, 0, "gather_cross")
        w_q, w_k, w_v = flat(whole)
        norms = norms.reshape((n,) + norms.shape[3:])[:, :6, :own].transpose(1, 0, 2).reshape(6, D).astype(F32)
        gain_one, bias_one, gain_two, bias_two, gain_three, bias_three = [norms[i] for i in range(6)]

        normal_one, inverse_one = moments(stream_in)
        h1 = (normal_one * gain_one + bias_one).astype(BF16)
        q1 = dg(h1, w_q, NN).astype(BF16)
        k1 = dg(context_rows, w_k, NN).astype(BF16)
        v1 = dg(context_rows, w_v, NN).astype(BF16)
        second, operands = gather([cross_out, attn_qkv, attn_out])
        (o1, lse1), whole = attn_fwd(
            context_frames, q1, k1, v1, (0, 0, 0), False, FRAME_TOK, 512,
            second, operands, paced(second, 8.0, 4.8, 2.2), 1, "cross_fwd",
        )
        w_o, w_qkv, w_p = flat(whole)
        x1 = stream_in + dg(o1, w_o, NN)
        normal_two, inverse_two = moments(x1)
        h2 = (normal_two * gain_two + bias_two).astype(BF16)
        qkv = dg(h2, w_qkv, NN).astype(BF16)
        third, operands = gather([mlp_up, mlp_down])
        (o2, lse2), whole = attn_fwd(
            clip_lengths, qkv, qkv, qkv, (0, 6, 12), True, 1, 512,
            third, operands, paced(third, 8.0, 4.8, 1.5), 2, "causal_fwd",
        )
        w_up, w_down = flat(whole)
        x2 = x1 + dg(o2, w_p, NN)
        normal_three, inverse_three = moments(x2)
        h3 = (normal_three * gain_three + bias_three).astype(BF16)
        up = dg(h3, w_up, NN)
        hidden = gelu(up).astype(BF16)
        x3 = x2 + dg(hidden, w_down, NN)
        block_out = jnp.where(padding, x3, 0.0).astype(BF16)

        dx3 = jnp.where(padding, cotangent[0].astype(F32), 0.0)
        dz = dx3.astype(BF16)
        dup = (dg(dz, w_down, NT) * gelu_slope(up)).astype(BF16)
        back, g_gain3, g_bias3 = norm_back(normal_three, inverse_three, gain_three, dg(dup, w_up, NT))
        dx2 = dx3 + back
        dy2 = dx2.astype(BF16)
        do2 = dg(dy2, w_p, NT).astype(BF16)
        fourth, operands = scatter([(weight(hidden, dz), (1, 0)), (weight(h3, dup), (0, 0))])
        (dqkv,), (s_up, s_down) = attn_bwd(
            clip_lengths, qkv, qkv, qkv, o2, do2, lse2, (0, 6, 12), True, 1, 256, 512,
            fourth, operands, paced(fourth, 8.0, 4.8, 2.45), 3, "causal_bwd",
        )
        dh2 = sum(dg(dqkv[c], w_qkv[:, c * D : (c + 1) * D], NT) for c in range(3))
        back, g_gain2, g_bias2 = norm_back(normal_two, inverse_two, gain_two, dh2)
        dx1 = dx2 + back
        dy1 = dx1.astype(BF16)
        do1 = dg(dy1, w_o, NT).astype(BF16)
        fifth, operands = scatter(
            [(weight(o2, dy2), (0, 0))]
            + [(weight(h2, dqkv[c]), (1, c * D)) for c in range(3)]
            + [(weight(o1, dy1), (2, 0))]
        )
        (dqkv1,), (s_p, s_qkv, s_o) = attn_bwd(
            context_frames, q1, k1, v1, o1, do1, lse1, (0, 0, 0), False, FRAME_TOK, 1024, 256,
            fifth, operands, paced(fifth, 8.0, 4.8, 3.1), 4, "cross_bwd",
        )
        dh1 = dg(dqkv1[0], w_q, NT)
        back, g_gain1, g_bias1 = norm_back(normal_one, inverse_one, gain_one, dh1)
        input_grad = dx1 + back

        g_norms = jnp.stack([g_gain1, g_bias1, g_gain2, g_bias2, g_gain3, g_bias3]).astype(BF16)
        g_norms = jnp.pad(g_norms.reshape(6, n, own).transpose(1, 0, 2), ((0, 0), (0, 10), (0, 256 - own)))

        sixth, operands = scatter(
            [
                (weight(context_rows, dqkv1[2]), (3, 0)),
                (weight(context_rows, dqkv1[1]), (2, 0)),
                (weight(h1, dqkv1[0]), (1, 0)),
                (g_norms, (0, 0)),
            ]
        )
        s_norms, s_q, s_k, s_v = alone(sixth, operands, 5, "scatter_cross")
    scale = (slot_rows * tokens.shape[0] * n * lax.axis_size("rep")) ** (-0.5)
    vec = [s_norms[i, :own] * scale for i in range(6)]
    halves = (s_up, s_up2) if own % 16 == 0 else jnp.split(s_up, 2, axis=1)
    *done, s_up, input_grad = finish([s_q, s_k, s_v, s_o, s_qkv, s_p, s_down], halves, input_grad, scale)
    done = [None, *done[:6], s_up, done[6]]
    return (
        block_out[None],
        input_grad[None],
        vec[0],
        vec[1],
        done[1],
        done[2],
        done[3],
        done[4],
        vec[2],
        vec[3],
        done[5],
        done[6],
        vec[4],
        vec[5],
        done[7],
        done[8],
    )


def solution(mesh):
    in_specs = (
        P(("fsdp", "rep"), None, None),
        P(("fsdp", "rep"), None, None),
        P(("fsdp", "rep")),
        P(("fsdp", "rep")),
        P("fsdp"),
        P("fsdp"),
        P("fsdp", None),
        P("fsdp", None),
        P("fsdp", None),
        P("fsdp", None),
        P("fsdp"),
        P("fsdp"),
        P("fsdp", None),
        P("fsdp", None),
        P("fsdp"),
        P("fsdp"),
        P("fsdp", None),
        P("fsdp", None),
        P(("fsdp", "rep"), None, None),
    )
    out_specs = (
        P(("fsdp", "rep"), None, None),
        P(("fsdp", "rep"), None, None),
        P("fsdp"),
        P("fsdp"),
        P("fsdp", None),
        P("fsdp", None),
        P("fsdp", None),
        P("fsdp", None),
        P("fsdp"),
        P("fsdp"),
        P("fsdp", None),
        P("fsdp", None),
        P("fsdp"),
        P("fsdp"),
        P("fsdp", None),
        P("fsdp", None),
    )
    return jax.shard_map(shards, mesh=mesh, in_specs=in_specs, out_specs=out_specs, check_vma=False)
```
